32 devices in a mesh: dp: 8 (over y, x, core), tensor: 4 (over z).
Axes of the slice: x: 2, y: 2, z: 4, core: 2. Of those that a mesh axis runs over, the one named last changes fastest.
Arguments:
- tokens: bfloat16 [16, 1024, 768], P('dp', 'tensor'), may hold values from -6 to 6
- parents: int32 [16, 4], P('dp'), may hold values from 0 to 2, as said below
- segment_ids: int32 [16, 1024], P('dp'), may hold values from 0 to 3, as said below
- w_qkv: bfloat16 [768, 3, 768], P('dp', None, 'tensor'), may hold values from -0.21875 to 0.21875
- b_q: float32 [768], replicated, may hold values from -3 to 3
- b_v: float32 [768], replicated, may hold values from -3 to 3
- w_out: bfloat16 [768, 768], P('tensor', 'dp'), may hold values from -0.875 to 0.875
- b_out: float32 [768], replicated, may hold values from -3 to 3
- gain_one: float32 [768], replicated, may hold values from 0.5 to 1.5
- shift_one: float32 [768], replicated, may hold values from -3 to 3
- w_up: bfloat16 [768, 3072], P('dp', 'tensor'), may hold values from -0.21875 to 0.21875
- b_up: float32 [3072], replicated, may hold values from -3 to 3
- w_down: bfloat16 [3072, 768], P('tensor', 'dp'), may hold values from -0.109375 to 0.109375
- b_down: float32 [768], replicated, may hold values from -3 to 3
- gain_two: float32 [768], replicated, may hold values from 0.5 to 1.5
- shift_two: float32 [768], replicated, may hold values from -3 to 3
- cotangent: bfloat16 [16, 1024, 768], P('dp', 'tensor'), may hold values from -6 to 6
Outputs:
- output: bfloat16 [16, 1024, 768], P('dp', 'tensor')
- input_grad: float32 [16, 1024, 768], P('dp', 'tensor')
- grad_w_qkv: float32 [768, 3, 768], P('dp', None, 'tensor')
- grad_b_q: float32 [768], replicated
- grad_b_v: float32 [768], replicated
- grad_w_out: float32 [768, 768], P('tensor', 'dp')
- grad_b_out: float32 [768], replicated
- grad_gain_one: float32 [768], replicated
- grad_shift_one: float32 [768], replicated
- grad_w_up: float32 [768, 3072], P('dp', 'tensor')
- grad_b_up: float32 [3072], replicated
- grad_w_down: float32 [3072, 768], P('tensor', 'dp')
- grad_b_down: float32 [768], replicated
- grad_gain_two: float32 [768], replicated
- grad_shift_two: float32 [768], replicated
The draws below stay inside these ranges and needn't reach their ends.
Inputs may be any that keep to these rules, and one draw needn't show every extreme that they name: parents[t, 0] = 0 and 0 <= parents[t, s] < s for every later segment s. `segment_ids`: along each tree the segment number starts at 0, never falls, and every one of the 4 segments occurs.
All inputs are finite; a program needn't handle non-finite values.
Results may differ from the reference program's by a relative error of at most 0.019.
Values may be sent and summed in bfloat16 or wider, within the bound.
A program may use at most 128 MiB of HBM per device.

```python
import jax
import jax.numpy as jnp
from jax import lax

D = 768
HEADS = 12
HD = 64
FF = 3072
TREE_LEN = 1024
SEGS = 4
TREES = 16


def draw_parents(key, part):
    labels = jnp.arange(SEGS, dtype=jnp.int32)
    random_bits = jax.random.randint(key, (TREES, SEGS), 0, 1 << 20)
    chosen = random_bits % jnp.maximum(labels, 1)[None, :]
    chain = jnp.maximum(labels - 1, 0)
    first_tree = (jnp.arange(TREES) == 0)[:, None]
    return jnp.where(first_tree, chain[None, :], chosen).astype(jnp.int32)


def draw_segment_ids(key, part):
    key_one, key_two, key_three = jax.random.split(key, 3)
    first_cut = jax.random.randint(key_one, (TREES, 1), TREE_LEN // 4, TREE_LEN // 2)
    second_cut = first_cut + jax.random.randint(key_two, (TREES, 1), TREE_LEN // 8, TREE_LEN // 4)
    third_cut = second_cut + jax.random.randint(key_three, (TREES, 1), TREE_LEN // 8, TREE_LEN // 4)
    places = jnp.arange(TREE_LEN, dtype=jnp.int32)[None, :]
    result = (places >= first_cut).astype(jnp.int32) + (places >= second_cut).astype(jnp.int32) + (places >= third_cut).astype(jnp.int32)
    return result.astype(jnp.int32)


def shard_levels(key, dims, cuts, smallest, high):
    def one(dim, blocks):
        draws = jax.random.uniform(jax.random.fold_in(jax.random.fold_in(key, 6), dim), (blocks,), jnp.float32, smallest / len(cuts), high / len(cuts))
        return jnp.repeat(jnp.exp(draws), dims[dim] // blocks).reshape((-1,) + (1,) * (len(dims) - dim - 1))

    factor_of = one(*cuts[0])
    for cut in cuts[1:]:
        factor_of = factor_of * one(*cut)
    return factor_of


def noise(rng, dims, deviation, bound, cuts=(), kind=jnp.bfloat16):
    factor_of = shard_levels(rng, dims, cuts, -0.22, 0.18) if cuts else 1.0
    drawn = jax.random.normal(rng, dims, jnp.float32) * deviation * factor_of
    return jnp.minimum(jnp.maximum(drawn, -bound), bound).astype(kind)


def setup_inputs(seed: int = 0) -> dict:
    key_of = jax.random.split(jax.random.key(seed), 18)
    tokens = noise(key_of[0], (TREES, TREE_LEN, D), 1.0, 6.0, ((0, 8), (1, 4)))
    parents = draw_parents(jax.random.fold_in(key_of[17], 71), 0)
    segment_ids = draw_segment_ids(jax.random.fold_in(key_of[17], 71), 0)
    w_qkv = noise(key_of[3], (D, 3, D), D ** -0.5, 0.21875, ((0, 8), (2, 4)))
    b_q = noise(key_of[4], (D,), 0.5, 3.0, (), jnp.float32)
    b_v = noise(key_of[5], (D,), 0.5, 3.0, (), jnp.float32)
    w_out = noise(key_of[6], (D, D), (D // 16) ** -0.5, 0.875, ((0, 4), (1, 8)))
    b_out = noise(key_of[7], (D,), 0.5, 3.0, (), jnp.float32)
    gain_one = jnp.clip(1.0 + 0.1 * jax.random.normal(key_of[8], (D,), jnp.float32), 0.5, 1.5)
    shift_one = noise(key_of[9], (D,), 0.5, 3.0, (), jnp.float32)
    w_up = noise(key_of[10], (D, FF), D ** -0.5, 0.21875, ((0, 8), (1, 4)))
    b_up = noise(key_of[11], (FF,), 0.5, 3.0, (), jnp.float32)
    w_down = noise(key_of[12], (FF, D), FF ** -0.5, 0.109375, ((0, 4), (1, 8)))
    b_down = noise(key_of[13], (D,), 0.5, 3.0, (), jnp.float32)
    gain_two = jnp.clip(1.0 + 0.1 * jax.random.normal(key_of[14], (D,), jnp.float32), 0.5, 1.5)
    shift_two = noise(key_of[15], (D,), 0.5, 3.0, (), jnp.float32)
    cotangent = noise(key_of[16], (TREES, TREE_LEN, D), 1.0, 6.0, ((0, 8), (1, 4)))
    return dict(tokens=tokens, parents=parents, segment_ids=segment_ids, w_qkv=w_qkv, b_q=b_q, b_v=b_v, w_out=w_out, b_out=b_out, gain_one=gain_one, shift_one=shift_one, w_up=w_up, b_up=b_up, w_down=w_down, b_down=b_down, gain_two=gain_two, shift_two=shift_two, cotangent=cotangent)


highest = lax.Precision.HIGHEST
epsilon = 1e-12
masked_fill = -1e+30

@jax.custom_vjp
def low(v):
    return lax.optimization_barrier(v.astype(jnp.bfloat16)).astype(jnp.float32)

@jax.custom_vjp
def low_back(v):
    return v

def low_keep(v):
    return (low(v), None)

def low_pass(kept, grad):
    return (grad,)

def back_keep(v):
    return (v, None)

def back_low(kept, grad):
    return (low(grad),)
low.defvjp(low_keep, low_pass)
low_back.defvjp(back_keep, back_low)

def ancestry(parents):
    labels = jnp.arange(SEGS, dtype=jnp.int32)
    step_table = (parents[:, None] == labels[None, :]).astype(jnp.float32)
    reach = jnp.eye(SEGS, dtype=jnp.float32)
    total = reach
    for repeat_index in range(SEGS - 1):
        reach = lax.optimization_barrier(jnp.sum(reach[:, :, None] * step_table[None, :, :], axis=1))
        total = total + reach
    return (total > 0.5).astype(jnp.float32)

def layer_norm(rows, gain, shift):
    center = rows - lax.optimization_barrier(jnp.mean(rows, axis=-1, keepdims=True))
    inverse = lax.rsqrt(lax.optimization_barrier(jnp.mean(center * center, axis=-1, keepdims=True)) + epsilon)
    return center * inverse * gain + shift

def tree_forward(tree_input, parameters, tree_parents, tree_segments):
    w_qkv, b_q, b_v, w_out, b_out, gain_one, shift_one, w_up, b_up, w_down, b_down, gain_two, shift_two = parameters
    length = tree_input.shape[0]
    score_scale = HD ** (-0.5)
    reach = ancestry(tree_parents)
    pair_table = reach[tree_segments[:, None], tree_segments[None, :]]
    allowed = pair_table > 0.5
    mixed = jnp.einsum('ld,dcn->lcn', tree_input, w_qkv, precision=highest)
    queries = low(low_back(mixed[:, 0] + b_q)).reshape(length, HEADS, HD)
    key_rows = low(low_back(mixed[:, 1])).reshape(length, HEADS, HD)
    values = low(low_back(mixed[:, 2] + b_v)).reshape(length, HEADS, HD)
    scores = low_back(jnp.einsum('qhe,khe->hqk', queries, key_rows, precision=highest) * score_scale)
    scores = jnp.where(allowed[None], scores, masked_fill)
    weights = low(jax.nn.softmax(scores, axis=-1))
    context = jnp.einsum('hqk,khe->qhe', weights, values, precision=highest).reshape(length, D)
    context = low(low_back(context))
    attended = low_back(jnp.dot(context, w_out, precision=highest, preferred_element_type=jnp.float32))
    hidden = layer_norm(tree_input + attended + b_out, gain_one, shift_one)
    inner = low_back(jnp.dot(low(hidden), w_up, precision=highest, preferred_element_type=jnp.float32) + b_up)
    activated = low(jax.nn.gelu(inner, approximate=False))
    branch = low_back(jnp.dot(activated, w_down, precision=highest, preferred_element_type=jnp.float32))
    return layer_norm(hidden + branch + b_down, gain_two, shift_two)

def reference(tokens, parents, segment_ids, w_qkv, b_q, b_v, w_out, b_out, gain_one, shift_one, w_up, b_up, w_down, b_down, gain_two, shift_two, cotangent):
    parameters = (w_qkv.astype(jnp.float32), b_q.astype(jnp.float32), b_v.astype(jnp.float32), w_out.astype(jnp.float32), b_out.astype(jnp.float32), gain_one.astype(jnp.float32), shift_one.astype(jnp.float32), w_up.astype(jnp.float32), b_up.astype(jnp.float32), w_down.astype(jnp.float32), b_down.astype(jnp.float32), gain_two.astype(jnp.float32), shift_two.astype(jnp.float32))
    zero_totals = jax.tree.map(jnp.zeros_like, parameters)

    def per_tree(totals, items):
        tree_tokens, tree_parents, tree_segments, tree_cotangent = items

        def forward_only(tree_input, params_now):
            return tree_forward(tree_input, params_now, tree_parents, tree_segments)
        outputs, pullback = jax.vjp(forward_only, tree_tokens.astype(jnp.float32), parameters)
        grad_tokens, grad_params = pullback(tree_cotangent.astype(jnp.float32))
        totals = jax.tree.map(jnp.add, totals, grad_params)
        return (totals, (outputs.astype(jnp.bfloat16), grad_tokens))
    totals, stacked = lax.scan(per_tree, zero_totals, (tokens, parents, segment_ids, cotangent))
    return (stacked[0], stacked[1], totals[0], totals[1], totals[2], totals[3], totals[4], totals[5], totals[6], totals[7], totals[8], totals[9], totals[10], totals[11], totals[12])
```

```python
import functools

import jax
import jax.numpy as jnp
from jax import lax
from jax.experimental import pallas as pl
from jax.experimental.pallas import tpu as pltpu
from jax.sharding import PartitionSpec as P

HD = 64
SEGS = 4
epsilon = 1e-12
BF = jnp.bfloat16
F32 = jnp.float32
FILL = -1e30
HALF_HEADS = ((0, 1, 2, 0, 0), (0, 1, 2, 1, 1), (3, 4, 5, 0, 1))


def dot(a, b, ca=1, cb=0):
    return lax.dot_general(a, b, (((ca,), (cb,)), ((), ())), preferred_element_type=F32)


def split3(v):
    hi = v.astype(BF).astype(F32)
    mid = (v - hi).astype(BF).astype(F32)
    low = v - hi - mid
    return hi, mid, low


def lane_mask(shape, half):
    lane = lax.broadcasted_iota(jnp.int32, shape, 1)
    return (lane < HD) if half == 0 else (lane >= HD)


def pieces(v, shape):
    lane = lax.broadcasted_iota(jnp.int32, shape, 1)
    hi, mid, low = split3(v)
    return jnp.where(lane == 4, hi, jnp.where(lane == 5, mid, jnp.where(lane == 6, low, 0.0)))


def attention_forward_kernel(x_ref, a_ref, bias_ref, rf_ref, kf_ref, tiles_ref, ctx_ref, raug_ref):
    length = x_ref.shape[0]
    block = 256
    count = length // block

    def project(i, _):
        rows = pl.ds(pl.multiple_of(i * block, block), block)
        xb = x_ref[rows, :]
        for t in range(2):
            m = dot(xb, a_ref[t, :, : 5 * 128]) + bias_ref[t][:, : 5 * 128]
            base = 6 * t
            q3 = m[:, 3 * 128 : 4 * 128]
            v3 = m[:, 4 * 128 : 5 * 128]
            tiles_ref[base, rows, :] = m[:, :128].astype(BF) * jnp.asarray(0.125, BF)
            tiles_ref[base + 1, rows, :] = m[:, 128:256].astype(BF)
            tiles_ref[base + 2, rows, :] = m[:, 256:384].astype(BF)
            tiles_ref[base + 3, rows, :] = q3.astype(BF) * jnp.asarray(0.125, BF)
            tiles_ref[base + 4, rows, :] = pltpu.roll(q3, 64, 1).astype(BF)
            tiles_ref[base + 5, rows, :] = pltpu.roll(v3, 64, 1).astype(BF)
        return 0

    lax.fori_loop(0, count, project, 0)
    ones = jnp.ones((length, 128), BF)

    for t in range(2):
        base = 6 * t

        def attend(i, _, t=t, base=base):
            rows = pl.ds(pl.multiple_of(i * block, block), block)
            rf = rf_ref[rows, :]
            parts = []
            for h, (qi, ki, vi, qh, vh) in enumerate(HALF_HEADS):
                q = tiles_ref[base + qi, rows, :]
                qm = jnp.where(lane_mask(q.shape, qh), q, jnp.zeros_like(q))
                qq = jnp.concatenate([qm, rf], axis=1)
                kk = jnp.concatenate([tiles_ref[base + ki], kf_ref[...]], axis=1)
                s = dot(qq, kk, 1, 1)
                m = jnp.max(s, axis=1, keepdims=True)
                p = jnp.exp(s - m).astype(BF)
                vv = jnp.concatenate([tiles_ref[base + vi], ones], axis=1)
                o = dot(p, vv)
                total = o[:, 128:129]
                ov = jnp.where(lane_mask((block, 128), vh), o[:, :128] / total, 0.0)
                lse = m + jnp.log(total)
                raug_ref[3 * t + h, rows, :] = rf + pieces(-lse, (block, 128)).astype(BF)
                parts.append(ov)
            ctx_ref[2 * t, rows, :] = (parts[0] + parts[1]).astype(BF)
            ctx_ref[2 * t + 1, rows, :] = parts[2].astype(BF)
            return 0

        lax.fori_loop(0, count, attend, 0)


def attention_backward_kernel(tiles_ref, ctx_ref, dctx_ref, raug_ref, kf_ref, out_ref, dk_ref, dv_ref):
    length = kf_ref.shape[0]
    block = 256
    count = length // block
    groups = ((HALF_HEADS[0], HALF_HEADS[1]), (HALF_HEADS[2],))
    for t in range(2):
        base = 6 * t
        for g, heads in enumerate(groups):
            dk_ref[...] = jnp.zeros_like(dk_ref)
            dv_ref[...] = jnp.zeros_like(dv_ref)
            ki = heads[0][1]
            vi = heads[0][2]
            k_t = tiles_ref[base + ki].astype(F32).T
            row = lax.broadcasted_iota(jnp.int32, k_t.shape, 0)
            k_masks = [
                jnp.where((row < HD) if qh == 0 else (row >= HD), k_t, 0.0).astype(BF)
                for (_, _, _, qh, _) in heads
            ]

            def back(i, _, t=t, base=base, g=g, heads=heads, k_masks=k_masks, ki=ki, vi=vi):
                rows = pl.ds(pl.multiple_of(i * block, block), block)
                dq_t = jnp.zeros((128, block), F32)
                do = dctx_ref[2 * t + g, rows, :]
                prod = do.astype(F32) * ctx_ref[2 * t + g, rows, :].astype(F32)
                for h, (qi, _, _, qh, vh) in enumerate(heads):
                    q = tiles_ref[base + qi, rows, :]
                    qm = jnp.where(lane_mask(q.shape, qh), q, jnp.zeros_like(q))
                    qa = jnp.concatenate([qm, raug_ref[3 * t + 2 * g + h, rows, :]], axis=1)
                    ka = jnp.concatenate([tiles_ref[base + ki], kf_ref[...]], axis=1)
                    pt = jnp.exp(dot(ka, qa, 1, 1))
                    vmask = lane_mask(do.shape, vh)
                    dom = jnp.where(vmask, do, jnp.zeros_like(do))
                    delta = jnp.sum(jnp.where(vmask, prod, 0.0), axis=1, keepdims=True)
                    doa = jnp.concatenate([dom, pieces(-delta, do.shape).astype(BF)], axis=1)
                    va = jnp.concatenate([tiles_ref[base + vi], kf_ref[...]], axis=1)
                    dst = (pt * dot(va, doa, 1, 1)).astype(BF)
                    dv_ref[...] += dot(pt.astype(BF), dom)
                    dk_ref[...] += dot(dst, qm)
                    dq_t = dq_t + dot(k_masks[h], dst)
                dq = dq_t.T * 0.125
                if g == 0:
                    out_ref[t, rows, 0:128] = dq.astype(BF)
                else:
                    out_ref[t, rows, 384:512] = dq.astype(BF)
                return 0

            lax.fori_loop(0, count, back, 0)
            if g == 0:
                out_ref[t, :, 128:256] = dk_ref[...].astype(BF)
                out_ref[t, :, 256:384] = dv_ref[...].astype(BF)
            else:
                out_ref[t, :, 384:512] = out_ref[t, :, 384:512] + pltpu.roll(dk_ref[...], 64, 1).astype(BF)
                out_ref[t, :, 512:640] = pltpu.roll(dv_ref[...], 64, 1).astype(BF)


def attention_forward(x, a, bias, rf, kf):
    length = x.shape[0]
    vm = pl.BlockSpec(memory_space=pltpu.VMEM)
    return pl.pallas_call(
        attention_forward_kernel,
        name="attn_fwd",
        out_shape=(
            jax.ShapeDtypeStruct((12, length, 128), BF),
            jax.ShapeDtypeStruct((4, length, 128), BF),
            jax.ShapeDtypeStruct((6, length, 128), BF),
        ),
        in_specs=[vm] * 5,
        out_specs=(vm,) * 3,
        compiler_params=pltpu.CompilerParams(vmem_limit_bytes=48 << 20),
        cost_estimate=pl.CostEstimate(flops=20 * 10**9, bytes_accessed=10 * 10**6, transcendentals=6 * 10**6),
    )(x, a, bias, rf, kf)


def attention_backward(tiles, ctx, dctx, raug, kf):
    length = kf.shape[0]
    vm = pl.BlockSpec(memory_space=pltpu.VMEM)
    return pl.pallas_call(
        attention_backward_kernel,
        name="attn_bwd",
        out_shape=jax.ShapeDtypeStruct((2, length, 640), BF),
        in_specs=[vm] * 5,
        out_specs=vm,
        scratch_shapes=[pltpu.VMEM((length, 128), F32), pltpu.VMEM((length, 128), F32)],
        compiler_params=pltpu.CompilerParams(vmem_limit_bytes=48 << 20),
        cost_estimate=pl.CostEstimate(flops=40 * 10**9, bytes_accessed=10 * 10**6, transcendentals=6 * 10**6),
    )(tiles, ctx, dctx, raug, kf)


def ancestry(parents):
    labels = jnp.arange(SEGS, dtype=jnp.int32)
    step = (parents[:, None] == labels[None, :]).astype(F32)
    reach = jnp.eye(SEGS, dtype=F32)
    total = reach
    for _ in range(SEGS - 1):
        reach = jnp.sum(reach[:, :, None] * step[None, :, :], axis=1)
        total = total + reach
    return (total > 0.5).astype(F32)


def gelu_parts(u):
    cdf = 0.5 * (1.0 + lax.erf(u * (2.0**-0.5)))
    pdf = jnp.exp(-0.5 * u * u) * ((2.0 * jnp.pi) ** -0.5)
    return u * cdf, cdf + u * pdf


def norm_parts(rows):
    center = rows - jnp.mean(rows, axis=-1, keepdims=True)
    inverse = lax.rsqrt(jnp.mean(center * center, axis=-1, keepdims=True) + epsilon)
    return center * inverse, inverse


def norm_back(grad_rows, normed, inverse, gain):
    scaled = grad_rows * gain
    return inverse * (
        scaled
        - jnp.mean(scaled, axis=-1, keepdims=True)
        - normed * jnp.mean(scaled * normed, axis=-1, keepdims=True)
    )


def body(dp, ranks, tokens, parents, segment_ids, w_qkv, b_q, b_v, w_out, b_out, gain_one, shift_one,
         w_up, b_up, w_down, b_down, gain_two, shift_two, cotangent):
    d = lax.axis_index("dp")
    ti = lax.axis_index("tensor")
    k = d % 2
    local, quarter, width = tokens.shape
    half_rows = quarter // 2
    own_rows = ranks * half_rows
    length = 2 * own_rows
    part = w_qkv.shape[2]
    hidden_part = w_up.shape[1]
    shard = w_qkv.shape[0]
    chips = dp // 2
    same_core = [[i for i in range(dp) if i % 2 == c] for c in range(2)]

    def swap(v):
        return lax.ppermute(v, "dp", [(i, i ^ 1) for i in range(dp)])

    def pick(v, index, axis=0):
        return lax.dynamic_index_in_dim(v, index, axis, keepdims=False)

    def join(own, peer, axis=0):
        return jnp.where(k == 0, jnp.stack([own, peer], axis), jnp.stack([peer, own], axis))

    def to_tree(v):
        v = v.reshape(local, 2, half_rows, width)
        mine = pick(v, k, 1)
        other = swap(pick(v, 1 - k, 1))
        trees = join(mine, other).reshape(ranks, half_rows, width)
        return lax.all_to_all(trees, "tensor", 0, 0, tiled=True).reshape(own_rows, width)

    def from_tree(v):
        v = lax.all_to_all(v.reshape(ranks, half_rows, width), "tensor", 0, 0, tiled=True)
        v = v.reshape(2, local, half_rows, width)
        other = swap(pick(v, 1 - k))
        return join(pick(v, k), other, 1).reshape(local, quarter, width)

    heads = w_qkv.reshape(shard, 3, 3, HD)
    q, kk, vv = heads[:, 0], heads[:, 1], heads[:, 2]
    out_t = w_out.T.reshape(shard, 3, HD)
    packed_a = jnp.concatenate(
        [q[:, 0], q[:, 1], kk[:, 0], kk[:, 1], vv[:, 0], vv[:, 1], q[:, 2], kk[:, 2], vv[:, 2],
         out_t[:, 2], out_t[:, 0], out_t[:, 1]], axis=1)

    def gather_weight(w):
        every = lax.all_gather(w, "tensor", axis=0, tiled=False).reshape(2, 2, shard, w.shape[1])
        mine = pick(every, k)
        other = swap(pick(every, 1 - k))
        both = join(mine, other, 1)
        full = lax.all_gather(both, "dp", axis=0, tiled=False, axis_index_groups=same_core)
        return full.transpose(1, 0, 2, 3, 4).reshape(2, chips * 2 * shard, w.shape[1])

    x_own = to_tree(tokens)
    w_a = gather_weight(packed_a)
    w_b = gather_weight(w_up)
    w_c = gather_weight(w_down.T)
    x = join(x_own, swap(x_own)).reshape(length, width)
    cot_own = to_tree(cotangent)

    seg_peer = swap(segment_ids)
    par_peer = swap(parents)
    all_seg = join(segment_ids, seg_peer).reshape(ranks, -1)
    all_par = join(parents, par_peer).reshape(ranks, -1)
    seg = pick(all_seg, ti).reshape(ranks, 2, half_rows).transpose(1, 0, 2).reshape(length)
    par = pick(all_par, ti)
    labels = jnp.arange(SEGS, dtype=jnp.int32)
    hot = (seg[:, None] == labels[None, :]).astype(F32)
    reach_rows = jnp.sum(hot[:, :, None] * ancestry(par)[None], axis=1)
    rf = jnp.concatenate([FILL * (1.0 - reach_rows), jnp.zeros((length, 124), F32)], axis=1).astype(BF)
    kf = jnp.concatenate([hot, jnp.ones((length, 3), F32), jnp.zeros((length, 121), F32)], axis=1).astype(BF)

    def half_vector(b, size):
        return lax.dynamic_slice_in_dim(b, 2 * k * size, 2 * size).reshape(2, size)

    bq = half_vector(b_q, part)
    bv = half_vector(b_v, part)
    zero64 = jnp.zeros((2, HD), F32)
    bias = jnp.concatenate(
        [bq[:, :128], jnp.zeros((2, 128), F32), bv[:, :128], bq[:, 128:], zero64, bv[:, 128:], zero64,
         jnp.zeros((2, 128), F32)], axis=1)[:, None, :]

    tiles, ctx, raug = attention_forward(x, w_a, bias, rf, kf)

    def exchange(partial):
        partial = partial.reshape(2, own_rows, width)
        received = swap(pick(partial, 1 - k).astype(BF))
        return pick(partial, k) + received.astype(F32)

    def spread_rows(v):
        return join(v, swap(v)).reshape(length, width)

    partial = 0.0
    for t in range(2):
        partial = partial + dot(ctx[2 * t + 1], w_a[t, :, 512:640], 1, 1) + dot(ctx[2 * t], w_a[t, :, 640:768], 1, 1)
    attended = exchange(partial)
    n1, r1 = norm_parts(x_own.astype(F32) + attended + b_out)
    hidden = n1 * gain_one + shift_one
    rows_low = spread_rows(hidden.astype(BF))
    up_bias = half_vector(b_up, hidden_part)
    inner = [dot(rows_low, w_b[t]) + up_bias[t] for t in range(2)]
    acts = [gelu_parts(u) for u in inner]
    activated = [a.astype(BF) for a, _ in acts]
    branch = exchange(sum(dot(activated[t], w_c[t], 1, 1) for t in range(2)))
    n2, r2 = norm_parts(hidden + branch + b_down)
    output = n2 * gain_two + shift_two
    g = cot_own.astype(F32)
    gain_two_part = jnp.sum(g * n2, axis=0)
    shift_two_part = jnp.sum(g, axis=0)
    mix_two = norm_back(g, n2, r2, gain_two)
    b_down_part = jnp.sum(mix_two, axis=0)
    two_rows = spread_rows(mix_two.astype(BF))
    d_c = [dot(two_rows, activated[t], 0, 0) for t in range(2)]
    grad_inner = [(dot(two_rows, w_c[t]) * acts[t][1]).astype(BF) for t in range(2)]
    b_up_part = jnp.concatenate([jnp.sum(v.astype(F32), axis=0) for v in grad_inner])
    d_b = [dot(rows_low, grad_inner[t], 0, 0) for t in range(2)]
    grad_hidden = mix_two + exchange(sum(dot(grad_inner[t], w_b[t], 1, 1) for t in range(2)))
    gain_one_part = jnp.sum(grad_hidden * n1, axis=0)
    shift_one_part = jnp.sum(grad_hidden, axis=0)
    mix_one = norm_back(grad_hidden, n1, r1, gain_one)
    b_out_part = jnp.sum(mix_one, axis=0)
    one_rows = spread_rows(mix_one.astype(BF))
    dctx = jnp.stack(
        [dot(one_rows, w_a[t, :, lo : lo + 128]).astype(BF) for t in range(2) for lo in (640, 512)])
    d_tiles = attention_backward(tiles, ctx, dctx, raug, kf)

    def d_a_of(t):
        qkv = dot(x, d_tiles[t], 0, 0)
        o2 = dot(one_rows, ctx[2 * t + 1], 0, 0)
        o01 = dot(one_rows, ctx[2 * t], 0, 0)
        lane = lax.broadcasted_iota(jnp.int32, o2.shape, 1)
        return jnp.concatenate([qkv[:, :512], jnp.where(lane < HD, qkv[:, 512:], o2), o01], axis=1)

    d_a = [d_a_of(t) for t in range(2)]
    lane_zero = jnp.where(jnp.arange(640) < 576, 1.0, 0.0).astype(BF)
    grad_x = exchange(sum(dot(d_tiles[t] * lane_zero, w_a[t, :, :640], 1, 1) for t in range(2)))
    input_grad = from_tree((mix_one + grad_x).astype(BF)).astype(F32)
    out = from_tree(output.astype(BF))

    def scatter_weight(pair):
        v = jnp.stack([p.astype(BF) for p in pair]).reshape(2, chips, 2, shard, width).transpose(1, 2, 0, 3, 4)
        v = v.reshape(chips * 4 * shard, width)
        v = lax.psum_scatter(v, "dp", scatter_dimension=0, tiled=True, axis_index_groups=same_core)
        v = v.reshape(2, 2, shard, width)
        other = swap(pick(v, 1 - k))
        v = join(pick(v, k), other).reshape(ranks * shard, width)
        return lax.psum_scatter(v, "tensor", scatter_dimension=0, tiled=True).astype(F32)

    g_c = scatter_weight(d_c)
    g_b = scatter_weight(d_b)
    g_a = scatter_weight(d_a)
    blk = [g_a[:, i * HD : (i + 1) * HD] for i in range(12)]
    grad_qkv = jnp.stack(
        [jnp.concatenate([blk[0], blk[1], blk[6]], 1), jnp.concatenate([blk[2], blk[3], blk[7]], 1),
         jnp.concatenate([blk[4], blk[5], blk[8]], 1)], axis=1)
    grad_out = jnp.concatenate([blk[10], blk[11], blk[9]], 1).T

    sums = jnp.sum(d_tiles.astype(F32), axis=1)
    bq_part = jnp.concatenate([sums[:, :128], sums[:, 384:448]], axis=1).reshape(-1)
    bv_part = jnp.concatenate([sums[:, 256:384], sums[:, 512:576]], axis=1).reshape(-1)

    def spread(v, size):
        return lax.dynamic_update_slice_in_dim(jnp.zeros((size,), F32), v, k * v.shape[0], 0)

    summed = lax.psum(
        (spread(bq_part, width), spread(bv_part, width), b_out_part, gain_one_part, shift_one_part,
         spread(b_up_part, b_up.shape[0]), b_down_part, gain_two_part, shift_two_part), ("dp", "tensor"))
    return (out, input_grad, grad_qkv, summed[0], summed[1], grad_out, summed[2], summed[3], summed[4],
            g_b, summed[5], g_c.T, summed[6], summed[7], summed[8])


def solution(mesh):
    dp, ranks = mesh.shape["dp"], mesh.shape["tensor"]
    return jax.shard_map(
        functools.partial(body, dp, ranks),
        mesh=mesh,
        in_specs=(P("dp", "tensor", None), P("dp", None), P("dp", None), P("dp", None, "tensor"), P(), P(),
                  P("tensor", "dp"), P(), P(), P(), P("dp", "tensor"), P(), P("tensor", "dp"), P(), P(), P(),
                  P("dp", "tensor", None)),
        out_specs=(P("dp", "tensor", None), P("dp", "tensor", None), P("dp", None, "tensor"), P(), P(),
                   P("tensor", "dp"), P(), P(), P(), P("dp", "tensor"), P(), P("tensor", "dp"), P(), P(), P()),
        check_vma=False,
    )
```

```python
import functools

import jax
import jax.numpy as jnp
from jax import lax
from jax.experimental import pallas as pl
from jax.experimental.pallas import tpu as pltpu
from jax.sharding import PartitionSpec as P

HD = 64
SEGS = 4
epsilon = 1e-12
BF = jnp.bfloat16
F32 = jnp.float32
FILL = -1e30
HALF_HEADS = ((0, 1, 2, 0, 0), (0, 1, 2, 1, 1), (3, 4, 5, 0, 1))


def dot(a, b, ca=1, cb=0):
    return lax.dot_general(a, b, (((ca,), (cb,)), ((), ())), preferred_element_type=F32)


def split3(v):
    hi = v.astype(BF).astype(F32)
    mid = (v - hi).astype(BF).astype(F32)
    low = v - hi - mid
    return hi, mid, low


def lane_mask(shape, half):
    lane = lax.broadcasted_iota(jnp.int32, shape, 1)
    return (lane < HD) if half == 0 else (lane >= HD)


def pieces(v, shape):
    lane = lax.broadcasted_iota(jnp.int32, shape, 1)
    hi, mid, low = split3(v)
    return jnp.where(lane == 4, hi, jnp.where(lane == 5, mid, jnp.where(lane == 6, low, 0.0)))


def attention_forward_kernel(x_ref, a_ref, bias_ref, rf_ref, kf_ref, tiles_ref, ctx_ref, raug_ref):
    length = x_ref.shape[0]
    block = 256
    count = length // block

    def project(i, _):
        rows = pl.ds(pl.multiple_of(i * block, block), block)
        xb = x_ref[rows, :]
        for t in range(2):
            m = dot(xb, a_ref[t, :, : 5 * 128]) + bias_ref[t][:, : 5 * 128]
            base = 6 * t
            q3 = m[:, 3 * 128 : 4 * 128]
            v3 = m[:, 4 * 128 : 5 * 128]
            tiles_ref[base, rows, :] = m[:, :128].astype(BF) * jnp.asarray(0.125, BF)
            tiles_ref[base + 1, rows, :] = m[:, 128:256].astype(BF)
            tiles_ref[base + 2, rows, :] = m[:, 256:384].astype(BF)
            tiles_ref[base + 3, rows, :] = q3.astype(BF) * jnp.asarray(0.125, BF)
            tiles_ref[base + 4, rows, :] = pltpu.roll(q3, 64, 1).astype(BF)
            tiles_ref[base + 5, rows, :] = pltpu.roll(v3, 64, 1).astype(BF)
        return 0

    lax.fori_loop(0, count, project, 0)
    ones = jnp.ones((length, 128), BF)

    for t in range(2):
        base = 6 * t

        def attend(i, _, t=t, base=base):
            rows = pl.ds(pl.multiple_of(i * block, block), block)
            rf = rf_ref[rows, :]
            parts = []
            for h, (qi, ki, vi, qh, vh) in enumerate(HALF_HEADS):
                q = tiles_ref[base + qi, rows, :]
                qm = jnp.where(lane_mask(q.shape, qh), q, jnp.zeros_like(q))
                qq = jnp.concatenate([qm, rf], axis=1)
                kk = jnp.concatenate([tiles_ref[base + ki], kf_ref[...]], axis=1)
                s = dot(qq, kk, 1, 1)
                m = jnp.max(s, axis=1, keepdims=True)
                p = jnp.exp(s - m).astype(BF)
                vv = jnp.concatenate([tiles_ref[base + vi], ones], axis=1)
                o = dot(p, vv)
                total = o[:, 128:129]
                ov = jnp.where(lane_mask((block, 128), vh), o[:, :128] / total, 0.0)
                lse = m + jnp.log(total)
                raug_ref[3 * t + h, rows, :] = rf + pieces(-lse, (block, 128)).astype(BF)
                parts.append(ov)
            ctx_ref[2 * t, rows, :] = (parts[0] + parts[1]).astype(BF)
            ctx_ref[2 * t + 1, rows, :] = parts[2].astype(BF)
            return 0

        lax.fori_loop(0, count, attend, 0)


def attention_backward_kernel(tiles_ref, ctx_ref, dctx_ref, raug_ref, kf_ref, out_ref, dk_ref, dv_ref):
    length = kf_ref.shape[0]
    block = 256
    count = length // block
    groups = ((HALF_HEADS[0], HALF_HEADS[1]), (HALF_HEADS[2],))
    for t in range(2):
        base = 6 * t
        for g, heads in enumerate(groups):
            dk_ref[...] = jnp.zeros_like(dk_ref)
            dv_ref[...] = jnp.zeros_like(dv_ref)
            ki = heads[0][1]
            vi = heads[0][2]
            k_t = tiles_ref[base + ki].astype(F32).T
            row = lax.broadcasted_iota(jnp.int32, k_t.shape, 0)
            k_masks = [
                jnp.where((row < HD) if qh == 0 else (row >= HD), k_t, 0.0).astype(BF)
                for (_, _, _, qh, _) in heads
            ]

            def back(i, _, t=t, base=base, g=g, heads=heads, k_masks=k_masks, ki=ki, vi=vi):
                rows = pl.ds(pl.multiple_of(i * block, block), block)
                dq_t = jnp.zeros((128, block), F32)
                do = dctx_ref[2 * t + g, rows, :]
                prod = do.astype(F32) * ctx_ref[2 * t + g, rows, :].astype(F32)
                for h, (qi, _, _, qh, vh) in enumerate(heads):
                    q = tiles_ref[base + qi, rows, :]
                    qm = jnp.where(lane_mask(q.shape, qh), q, jnp.zeros_like(q))
                    qa = jnp.concatenate([qm, raug_ref[3 * t + 2 * g + h, rows, :]], axis=1)
                    ka = jnp.concatenate([tiles_ref[base + ki], kf_ref[...]], axis=1)
                    pt = jnp.exp(dot(ka, qa, 1, 1))
                    vmask = lane_mask(do.shape, vh)
                    dom = jnp.where(vmask, do, jnp.zeros_like(do))
                    delta = jnp.sum(jnp.where(vmask, prod, 0.0), axis=1, keepdims=True)
                    doa = jnp.concatenate([dom, pieces(-delta, do.shape).astype(BF)], axis=1)
                    va = jnp.concatenate([tiles_ref[base + vi], kf_ref[...]], axis=1)
                    dst = (pt * dot(va, doa, 1, 1)).astype(BF)
                    dv_ref[...] += dot(pt.astype(BF), dom)
                    dk_ref[...] += dot(dst, qm)
                    dq_t = dq_t + dot(k_masks[h], dst)
                dq = dq_t.T * 0.125
                if g == 0:
                    out_ref[t, rows, 0:128] = dq.astype(BF)
                else:
                    out_ref[t, rows, 384:512] = dq.astype(BF)
                return 0

            lax.fori_loop(0, count, back, 0)
            if g == 0:
                out_ref[t, :, 128:256] = dk_ref[...].astype(BF)
                out_ref[t, :, 256:384] = dv_ref[...].astype(BF)
            else:
                out_ref[t, :, 384:512] = out_ref[t, :, 384:512] + pltpu.roll(dk_ref[...], 64, 1).astype(BF)
                out_ref[t, :, 512:640] = pltpu.roll(dv_ref[...], 64, 1).astype(BF)


def attention_forward(x, a, bias, rf, kf):
    length = x.shape[0]
    vm = pl.BlockSpec(memory_space=pltpu.VMEM)
    return pl.pallas_call(
        attention_forward_kernel,
        name="attn_fwd",
        out_shape=(
            jax.ShapeDtypeStruct((12, length, 128), BF),
            jax.ShapeDtypeStruct((4, length, 128), BF),
            jax.ShapeDtypeStruct((6, length, 128), BF),
        ),
        in_specs=[vm] * 5,
        out_specs=(vm,) * 3,
        compiler_params=pltpu.CompilerParams(vmem_limit_bytes=48 << 20),
        cost_estimate=pl.CostEstimate(flops=20 * 10**9, bytes_accessed=10 * 10**6, transcendentals=6 * 10**6),
    )(x, a, bias, rf, kf)


def attention_backward(tiles, ctx, dctx, raug, kf):
    length = kf.shape[0]
    vm = pl.BlockSpec(memory_space=pltpu.VMEM)
    return pl.pallas_call(
        attention_backward_kernel,
        name="attn_bwd",
        out_shape=jax.ShapeDtypeStruct((2, length, 640), BF),
        in_specs=[vm] * 5,
        out_specs=vm,
        scratch_shapes=[pltpu.VMEM((length, 128), F32), pltpu.VMEM((length, 128), F32)],
        compiler_params=pltpu.CompilerParams(vmem_limit_bytes=48 << 20),
        cost_estimate=pl.CostEstimate(flops=40 * 10**9, bytes_accessed=10 * 10**6, transcendentals=6 * 10**6),
    )(tiles, ctx, dctx, raug, kf)


def ancestry(parents):
    labels = jnp.arange(SEGS, dtype=jnp.int32)
    step = (parents[:, None] == labels[None, :]).astype(F32)
    reach = jnp.eye(SEGS, dtype=F32)
    total = reach
    for _ in range(SEGS - 1):
        reach = jnp.sum(reach[:, :, None] * step[None, :, :], axis=1)
        total = total + reach
    return (total > 0.5).astype(F32)


def gelu_parts(u):
    cdf = 0.5 * (1.0 + lax.erf(u * (2.0**-0.5)))
    pdf = jnp.exp(-0.5 * u * u) * ((2.0 * jnp.pi) ** -0.5)
    return u * cdf, cdf + u * pdf


def norm_parts(rows):
    center = rows - jnp.mean(rows, axis=-1, keepdims=True)
    inverse = lax.rsqrt(jnp.mean(center * center, axis=-1, keepdims=True) + epsilon)
    return center * inverse, inverse


def norm_back(grad_rows, normed, inverse, gain):
    scaled = grad_rows * gain
    return inverse * (
        scaled
        - jnp.mean(scaled, axis=-1, keepdims=True)
        - normed * jnp.mean(scaled * normed, axis=-1, keepdims=True)
    )


def body(dp, ranks, tokens, parents, segment_ids, w_qkv, b_q, b_v, w_out, b_out, gain_one, shift_one,
         w_up, b_up, w_down, b_down, gain_two, shift_two, cotangent):
    d = lax.axis_index("dp")
    ti = lax.axis_index("tensor")
    k = d % 2
    local, quarter, width = tokens.shape
    half_rows = quarter // 2
    own_rows = ranks * half_rows
    length = 2 * own_rows
    part = w_qkv.shape[2]
    hidden_part = w_up.shape[1]
    shard = w_qkv.shape[0]
    chips = dp // 2
    same_core = [[i for i in range(dp) if i % 2 == c] for c in range(2)]

    def swap(v):
        return lax.ppermute(v, "dp", [(i, i ^ 1) for i in range(dp)])

    def pick(v, index, axis=0):
        return lax.dynamic_index_in_dim(v, index, axis, keepdims=False)

    def join(own, peer, axis=0):
        return jnp.where(k == 0, jnp.stack([own, peer], axis), jnp.stack([peer, own], axis))

    def to_tree(v):
        v = v.reshape(local, 2, half_rows, width)
        mine = pick(v, k, 1)
        other = swap(pick(v, 1 - k, 1))
        trees = join(mine, other).reshape(ranks, half_rows, width)
        return lax.all_to_all(trees, "tensor", 0, 0, tiled=True).reshape(own_rows, width)

    def from_tree(v):
        v = lax.all_to_all(v.reshape(ranks, half_rows, width), "tensor", 0, 0, tiled=True)
        v = v.reshape(2, local, half_rows, width)
        other = swap(pick(v, 1 - k))
        return join(pick(v, k), other, 1).reshape(local, quarter, width)

    heads = w_qkv.reshape(shard, 3, 3, HD)
    q, kk, vv = heads[:, 0], heads[:, 1], heads[:, 2]
    out_t = w_out.T.reshape(shard, 3, HD)
    packed_a = jnp.concatenate(
        [q[:, 0], q[:, 1], kk[:, 0], kk[:, 1], vv[:, 0], vv[:, 1], q[:, 2], kk[:, 2], vv[:, 2],
         out_t[:, 2], out_t[:, 0], out_t[:, 1]], axis=1)

    def gather_weight(w):
        every = lax.all_gather(w, "tensor", axis=0, tiled=False).reshape(2, 2, shard, w.shape[1])
        mine = pick(every, k)
        other = swap(pick(every, 1 - k))
        both = join(mine, other, 1)
        full = lax.all_gather(both, "dp", axis=0, tiled=False, axis_index_groups=same_core)
        return full.transpose(1, 0, 2, 3, 4).reshape(2, chips * 2 * shard, w.shape[1])

    x_own = to_tree(tokens)
    w_a = gather_weight(packed_a)
    w_b = gather_weight(w_up)
    w_c = gather_weight(w_down.T)
    x = join(x_own, swap(x_own)).reshape(length, width)
    cot_own = to_tree(cotangent)

    seg_peer = swap(segment_ids)
    par_peer = swap(parents)
    all_seg = join(segment_ids, seg_peer).reshape(ranks, -1)
    all_par = join(parents, par_peer).reshape(ranks, -1)
    seg = pick(all_seg, ti).reshape(ranks, 2, half_rows).transpose(1, 0, 2).reshape(length)
    par = pick(all_par, ti)
    labels = jnp.arange(SEGS, dtype=jnp.int32)
    hot = (seg[:, None] == labels[None, :]).astype(F32)
    reach_rows = jnp.sum(hot[:, :, None] * ancestry(par)[None], axis=1)
    rf = jnp.concatenate([FILL * (1.0 - reach_rows), jnp.zeros((length, 124), F32)], axis=1).astype(BF)
    kf = jnp.concatenate([hot, jnp.ones((length, 3), F32), jnp.zeros((length, 121), F32)], axis=1).astype(BF)

    def half_vector(b, size):
        return lax.dynamic_slice_in_dim(b, 2 * k * size, 2 * size).reshape(2, size)

    bq = half_vector(b_q, part)
    bv = half_vector(b_v, part)
    zero64 = jnp.zeros((2, HD), F32)
    bias = jnp.concatenate(
        [bq[:, :128], jnp.zeros((2, 128), F32), bv[:, :128], bq[:, 128:], zero64, bv[:, 128:], zero64,
         jnp.zeros((2, 128), F32)], axis=1)[:, None, :]

    tiles, ctx, raug = attention_forward(x, w_a, bias, rf, kf)

    def exchange(partial):
        partial = partial.reshape(2, own_rows, width)
        received = swap(pick(partial, 1 - k).astype(BF))
        return pick(partial, k) + received.astype(F32)

    def spread_rows(v):
        return join(v, swap(v)).reshape(length, width)

    partial = 0.0
    for t in range(2):
        partial = partial + dot(ctx[2 * t + 1], w_a[t, :, 512:640], 1, 1) + dot(ctx[2 * t], w_a[t, :, 640:768], 1, 1)
    attended = exchange(partial)
    n1, r1 = norm_parts(x_own.astype(F32) + attended + b_out)
    hidden = n1 * gain_one + shift_one
    rows_low = spread_rows(hidden.astype(BF))
    up_bias = half_vector(b_up, hidden_part)
    inner = [dot(rows_low, w_b[t]) + up_bias[t] for t in range(2)]
    acts = [gelu_parts(u) for u in inner]
    activated = [a.astype(BF) for a, _ in acts]
    branch = exchange(sum(dot(activated[t], w_c[t], 1, 1) for t in range(2)))
    n2, r2 = norm_parts(hidden + branch + b_down)
    output = n2 * gain_two + shift_two
    g = cot_own.astype(F32)
    gain_two_part = jnp.sum(g * n2, axis=0)
    shift_two_part = jnp.sum(g, axis=0)
    mix_two = norm_back(g, n2, r2, gain_two)
    b_down_part = jnp.sum(mix_two, axis=0)
    two_rows = spread_rows(mix_two.astype(BF))
    d_c = [dot(two_rows, activated[t], 0, 0) for t in range(2)]
    grad_inner = [(dot(two_rows, w_c[t]) * acts[t][1]).astype(BF) for t in range(2)]
    b_up_part = jnp.concatenate([jnp.sum(v.astype(F32), axis=0) for v in grad_inner])
    d_b = [dot(rows_low, grad_inner[t], 0, 0) for t in range(2)]
    grad_hidden = mix_two + exchange(sum(dot(grad_inner[t], w_b[t], 1, 1) for t in range(2)))
    gain_one_part = jnp.sum(grad_hidden * n1, axis=0)
    shift_one_part = jnp.sum(grad_hidden, axis=0)
    mix_one = norm_back(grad_hidden, n1, r1, gain_one)
    b_out_part = jnp.sum(mix_one, axis=0)
    one_rows = spread_rows(mix_one.astype(BF))
    dctx = jnp.stack(
        [dot(one_rows, w_a[t, :, lo : lo + 128]).astype(BF) for t in range(2) for lo in (640, 512)])
    d_tiles = attention_backward(tiles, ctx, dctx, raug, kf)

    def d_a_of(t):
        qkv = dot(x, d_tiles[t], 0, 0)
        o2 = dot(one_rows, ctx[2 * t + 1], 0, 0)
        o01 = dot(one_rows, ctx[2 * t], 0, 0)
        lane = lax.broadcasted_iota(jnp.int32, o2.shape, 1)
        return jnp.concatenate([qkv[:, :512], jnp.where(lane < HD, qkv[:, 512:], o2), o01], axis=1)

    d_a = [d_a_of(t) for t in range(2)]
    lane_zero = jnp.where(jnp.arange(640) < 576, 1.0, 0.0).astype(BF)
    grad_x = exchange(sum(dot(d_tiles[t] * lane_zero, w_a[t, :, :640], 1, 1) for t in range(2)))
    input_grad = from_tree((mix_one + grad_x).astype(BF)).astype(F32)
    out = from_tree(output.astype(BF))

    def scatter_weight(pair):
        v = jnp.stack([p.astype(BF) for p in pair]).reshape(2, chips, 2, shard, width).transpose(1, 2, 0, 3, 4)
        v = v.reshape(chips * 4 * shard, width)
        v = lax.psum_scatter(v, "dp", scatter_dimension=0, tiled=True, axis_index_groups=same_core)
        v = v.reshape(2, 2, shard, width)
        other = swap(pick(v, 1 - k))
        v = join(pick(v, k), other).reshape(ranks * shard, width)
        return lax.psum_scatter(v, "tensor", scatter_dimension=0, tiled=True).astype(F32)

    g_c = scatter_weight(d_c)
    g_b = scatter_weight(d_b)
    g_a = scatter_weight(d_a)
    blk = [g_a[:, i * HD : (i + 1) * HD] for i in range(12)]
    grad_qkv = jnp.stack(
        [jnp.concatenate([blk[0], blk[1], blk[6]], 1), jnp.concatenate([blk[2], blk[3], blk[7]], 1),
         jnp.concatenate([blk[4], blk[5], blk[8]], 1)], axis=1)
    grad_out = jnp.concatenate([blk[10], blk[11], blk[9]], 1).T

    sums = jnp.sum(d_tiles.astype(F32), axis=1)
    bq_part = jnp.concatenate([sums[:, :128], sums[:, 384:448]], axis=1).reshape(-1)
    bv_part = jnp.concatenate([sums[:, 256:384], sums[:, 512:576]], axis=1).reshape(-1)

    def spread(v, size):
        return lax.dynamic_update_slice_in_dim(jnp.zeros((size,), F32), v, k * v.shape[0], 0)

    summed = lax.psum(
        (spread(bq_part, width), spread(bv_part, width), b_out_part, gain_one_part, shift_one_part,
         spread(b_up_part, b_up.shape[0]), b_down_part, gain_two_part, shift_two_part), ("dp", "tensor"))
    return (out, input_grad, grad_qkv, summed[0], summed[1], grad_out, summed[2], summed[3], summed[4],
            g_b, summed[5], g_c.T, summed[6], summed[7], summed[8])


A_BLK, B_BLK, C_BLK = 0, 1, 2
ROW_BLOCK = 256


def erf_exact(x):
    x = jnp.clip(x, -3.832506856900711, 3.832506856900711)
    z = x * x
    p = jnp.full_like(z, 0.00022905065861350646)
    for c in (0.0034082910107109506, 0.050955695062380861, 0.18520832239976145, 1.128379143519084):
        p = p * z + c
    q = jnp.full_like(z, -1.1791602954361697e-7)
    for c in (0.000023547966471313185, 0.0010179625278914885, 0.014070470171167667, 0.11098505178285362,
              0.49746925110067538, 1.0):
        q = q * z + c
    return x * p / q


def gelu_pair(u):
    cdf = 0.5 * (1.0 + erf_exact(u * (2.0**-0.5)))
    pdf = jnp.exp(-0.5 * u * u) * ((2.0 * jnp.pi) ** -0.5)
    return u * cdf, cdf + u * pdf


def row_mean(v):
    return jnp.mean(v, axis=-1, keepdims=True)


def layer_kernel(tok, cot_in, par, seg, wqkv, wout, wup, wdown, bq, bv, bout, g1, s1, bup, bdown, g2, s2,
                 out, dxr, ga_out, gb_out, gc_out, vec_out,
                 W, X, tiles, ctx, raug, rf, kf, n1, r1, H, act, gp, cot, mix, G2, G1, dctx, own,
                 sbuf, rbuf, obuf, dW, rs1, rs2, zbuf, tbuf, dkv, ash, csh, seg_all, par_all, vec, vrecv,
                 ssem, rsem):
    d = lax.axis_index("dp")
    t = lax.axis_index("tensor")
    k = lax.rem(d, 2)
    c = d // 2
    ranks = 4
    cx = c + 1 - 2 * lax.rem(c, 2)
    cy = lax.rem(c + 2, 4)
    cd = 3 - c
    length = X.shape[0]
    half = length // 2
    piece = half // ranks
    width = X.shape[1]
    shard = ash.shape[0]
    pair = 2 * shard
    home = t // 2
    here = k * half
    there = (1 - k) * half
    counters = {"s": 0, "r": 0}
    pending = []

    def new(kind, n=1):
        base = counters[kind]
        counters[kind] = base + n
        return base

    def remote(src, dst, s, r, dd, tt):
        return pltpu.make_async_remote_copy(
            src_ref=src, dst_ref=dst, send_sem=ssem.at[s], recv_sem=rsem.at[r], device_id=(dd, tt),
            device_id_type=pl.DeviceIdType.MESH)

    def send(src, dst, r, dd, tt):
        cp = remote(src, dst, new("s"), r, dd, tt)
        cp.start()
        pending.append((None, cp))

    def send_or_copy(src, dst, r, dd, tt):
        cp = remote(src, dst, new("s"), r, dd, tt)
        mine = jnp.logical_and(dd == d, tt == t)

        @pl.when(mine)
        def _():
            pltpu.make_async_copy(src, dst, rsem.at[r]).start()

        @pl.when(jnp.logical_not(mine))
        def _():
            cp.start()

        pending.append((mine, cp))

    def settle(entry):
        mine, cp = entry
        if mine is None:
            cp.wait_send()
        else:
            @pl.when(jnp.logical_not(mine))
            def _():
                cp.wait_send()

    def arrive(dst, r):
        pltpu.make_async_copy(dst, dst, rsem.at[r]).wait()

    def rows_at(start, n, align=None):
        return pl.ds(pl.multiple_of(start, align or n), n)

    barrier = pltpu.get_barrier_semaphore()
    partners = [(2 * c + 1 - k, t), (2 * cx + k, t), (2 * cy + k, t)]
    for j in range(1, ranks):
        for core in range(2):
            partners.append((2 * c + core, lax.rem(t + j, ranks)))
    for dev in partners:
        pl.semaphore_signal(barrier, inc=1, device_id=dev, device_id_type=pl.DeviceIdType.MESH)
    pl.semaphore_wait(barrier, len(partners))

    slot = lax.rem(t, 2) * 2 + k

    def z_send(b, src):
        base = new("r", 4)
        dst = W.at[b, lax.rem(t, 2), rows_at(c * pair + k * shard, shard), :]
        for j in (1, 2, 3, 0):
            send_or_copy(src, dst, base + slot, 2 * c + home, lax.rem(t + j, ranks))
        return base

    def z_wait(b, base):
        for tt in range(2):
            for kk in range(2):
                arrive(W.at[b, tt, rows_at(c * pair + kk * shard, shard), :], base + 2 * tt + kk)

    def plane_rows(b, h, chip):
        return W.at[b, h, rows_at(chip * pair, pair), :]

    def plane_send(b):
        base = new("r", 6)
        for h in range(2):
            src = plane_rows(b, h, c)
            send(src, src, base + 3 * h, 2 * cx + k, t)
            send(src, src, base + 3 * h + 1, 2 * cy + k, t)
        return base

    def plane_forward(b, base):
        arrive(plane_rows(b, 0, cx), base)
        send(plane_rows(b, 0, cx), plane_rows(b, 0, cx), base + 2, 2 * cy + k, t)
        arrive(plane_rows(b, 1, cy), base + 4)
        send(plane_rows(b, 1, cy), plane_rows(b, 1, cy), base + 5, 2 * cx + k, t)

    def plane_wait(b, base):
        arrive(plane_rows(b, 0, cy), base + 1)
        arrive(plane_rows(b, 1, cx), base + 3)
        arrive(plane_rows(b, 0, cd), base + 2)
        arrive(plane_rows(b, 1, cd), base + 5)

    q_all = wqkv[:, 0, :].astype(F32)
    k_all = wqkv[:, 1, :].astype(F32)
    v_all = wqkv[:, 2, :].astype(F32)
    o_all = wout[...].astype(F32).T
    ash[:, 0:128] = q_all[:, :128].astype(BF)
    ash[:, 128:256] = k_all[:, :128].astype(BF)
    ash[:, 256:384] = v_all[:, :128].astype(BF)
    ash[:, 384:512] = jnp.concatenate([q_all[:, 128:], k_all[:, 128:]], axis=1).astype(BF)
    ash[:, 512:640] = jnp.concatenate([v_all[:, 128:], o_all[:, 128:]], axis=1).astype(BF)
    ash[:, 640:768] = o_all[:, :128].astype(BF)
    za = z_send(A_BLK, ash)

    seg_base = new("r", 2)
    for i, (src, dst) in enumerate(((seg, seg_all), (par, par_all))):
        send(src, dst.at[k], seg_base + i, 2 * c + 1 - k, t)
        dst[pl.ds(k, 1)] = src[...][None]
    csh[...] = wdown[...].astype(F32).T.astype(BF)

    z_wait(A_BLK, za)
    pa = plane_send(A_BLK)

    def tree_send(src, dst):
        base = new("r", 4)
        for s in range(2):
            for h in range(2):
                send_or_copy(src.at[s, pl.ds(h * piece, piece), :], dst(h), base + t, 2 * c + h, 2 * k + s)
        return base

    tok_base = tree_send(tok, lambda h: X.at[rows_at(h * half + t * piece, piece), :])
    zb = z_send(B_BLK, wup)

    arrive(seg_all.at[1 - k], seg_base)
    arrive(par_all.at[1 - k], seg_base + 1)
    lane1 = lax.broadcasted_iota(jnp.int32, (1, 128), 1)
    both = par_all[pl.ds(home, 1)][0]
    second = lax.rem(t, 2) == 1
    parents = jnp.where(second, both[1:2, :], both[0:1, :])
    par_of = [jnp.broadcast_to(parents[:, j : j + 1], (1, 128)) for j in range(SEGS)]
    reach_rows = []
    for s in range(SEGS):
        now = jnp.full((1, 128), s, jnp.int32)
        seen = lane1 == s
        for _ in range(SEGS - 1):
            now = functools.reduce(lambda acc, j: jnp.where(now == j, par_of[j], acc), range(SEGS), now)
            seen = jnp.logical_or(seen, lane1 == now)
        reach_rows.append(jnp.where(lane1 < SEGS, jnp.where(seen, 0.0, FILL), 0.0))
    lane_f = lax.broadcasted_iota(jnp.int32, (piece, 128), 1).astype(F32)
    for h in range(2):
        for q in range(ranks):
            both = seg_all[pl.ds(home, 1), :, pl.ds((2 * q + h) * piece, piece)][0].astype(F32)
            part = jnp.where(second, both[1:2, :], both[0:1, :])
            segs = jnp.broadcast_to(part, (piece, piece)).T
            rows = pl.ds(h * half + q * piece, piece)
            table = jnp.zeros((piece, 128), F32)
            for s in range(SEGS):
                table = jnp.where(segs == s, jnp.broadcast_to(reach_rows[s], (piece, 128)), table)
            rf[rows, :] = table.astype(BF)
            hot = jnp.where(lane_f < SEGS, jnp.where(segs == lane_f, 1.0, 0.0), jnp.where(lane_f < SEGS + 3, 1.0, 0.0))
            kf[rows, :] = hot.astype(BF)

    plane_forward(A_BLK, pa)
    fwd_base = new("r", 4)
    for j in range(ranks):
        q = lax.rem(t + j, ranks)
        mine = X.at[rows_at(here + q * piece, piece), :]
        arrive(mine, tok_base + q)
        send(mine, mine, fwd_base + q, 2 * c + 1 - k, t)
    zc = z_send(C_BLK, csh)
    plane_wait(A_BLK, pa)

    def half_lanes(ref):
        return ref[:, pl.ds(pl.multiple_of(k * 384, 384), 384)]

    bq2, bv2 = half_lanes(bq), half_lanes(bv)
    zero64 = jnp.zeros((1, HD), F32)
    biases = []
    for tt in range(2):
        lo = 192 * tt
        biases.append((bq2[:, lo : lo + 128], bv2[:, lo : lo + 128],
                       jnp.concatenate([bq2[:, lo + 128 : lo + 192], zero64], axis=1),
                       jnp.concatenate([bv2[:, lo + 128 : lo + 192], zero64], axis=1)))
    eighth = jnp.asarray(0.125, BF)

    def project(start):
        def run(i, _):
            rows = rows_at(start + i * ROW_BLOCK, ROW_BLOCK)
            xb = X[rows, :]
            for tt in range(2):
                m = dot(xb, W[A_BLK, tt, :, 0:640])
                b_q01, b_v01, b_q2, b_v2 = biases[tt]
                base = 6 * tt
                q3 = m[:, 384:512] + b_q2
                v3 = m[:, 512:640] + b_v2
                tiles[base, rows, :] = (m[:, 0:128] + b_q01).astype(BF) * eighth
                tiles[base + 1, rows, :] = m[:, 128:256].astype(BF)
                tiles[base + 2, rows, :] = (m[:, 256:384] + b_v01).astype(BF)
                tiles[base + 3, rows, :] = q3.astype(BF) * eighth
                tiles[base + 4, rows, :] = pltpu.roll(q3, 64, 1).astype(BF)
                tiles[base + 5, rows, :] = pltpu.roll(v3, 64, 1).astype(BF)
            return 0

        lax.fori_loop(0, half // ROW_BLOCK, run, 0)

    project(here)
    for q in range(ranks):
        arrive(X.at[rows_at(there + q * piece, piece), :], fwd_base + q)
    project(there)

    ones = jnp.ones((length, 128), BF)

    def attend_all(tt):
        base = 6 * tt

        def attend(i, _):
            rows = rows_at(i * ROW_BLOCK, ROW_BLOCK)
            rfb = rf[rows, :]
            parts = []
            for h, (qi, ki, vi, qh, vh) in enumerate(HALF_HEADS):
                qt = tiles[base + qi, rows, :]
                qm = jnp.where(lane_mask(qt.shape, qh), qt, jnp.zeros_like(qt))
                s = dot(jnp.concatenate([qm, rfb], axis=1), jnp.concatenate([tiles[base + ki], kf[...]], axis=1), 1, 1)
                top = jnp.max(s, axis=1, keepdims=True)
                p = jnp.exp(s - top).astype(BF)
                o = dot(p, jnp.concatenate([tiles[base + vi], ones], axis=1))
                total = o[:, 128:129]
                parts.append(jnp.where(lane_mask((ROW_BLOCK, 128), vh), o[:, :128] / total, 0.0))
                lse = top + jnp.log(total)
                raug[3 * tt + h, rows, :] = rfb + pieces(-lse, (ROW_BLOCK, 128)).astype(BF)
            ctx[tt, rows, 0:128] = parts[2].astype(BF)
            ctx[tt, rows, 128:256] = (parts[0] + parts[1]).astype(BF)
            return 0

        lax.fori_loop(0, length // ROW_BLOCK, attend, 0)

    z_wait(B_BLK, zb)
    pb = plane_send(B_BLK)
    attend_all(0)
    plane_forward(B_BLK, pb)
    z_wait(C_BLK, zc)
    pc = plane_send(C_BLK)
    cot_base = tree_send(cot_in, lambda h: cot.at[rows_at(t * piece, piece), :])
    attend_all(1)

    exchanged = []

    def exchange(compute, index):
        r = new("r")
        if len(exchanged) >= 2:
            done = exchanged[-2]
            pending[:] = [e for e in pending if e is not done]
            done[1].wait_send()

        def give(i, _):
            rows = rows_at(i * ROW_BLOCK, ROW_BLOCK)
            sbuf[index, rows, :] = compute(rows_at(there + i * ROW_BLOCK, ROW_BLOCK)).astype(BF)
            return 0

        lax.fori_loop(0, half // ROW_BLOCK, give, 0)
        send(sbuf.at[index], rbuf.at[index], r, 2 * c + 1 - k, t)
        exchanged.append(pending[-1])

        def keep(i, _):
            rows = rows_at(i * ROW_BLOCK, ROW_BLOCK)
            own[rows, :] = compute(rows_at(here + i * ROW_BLOCK, ROW_BLOCK))
            return 0

        lax.fori_loop(0, half // ROW_BLOCK, keep, 0)
        return r

    def over_pieces(step, buffer):
        base = new("r", ranks)
        s_base = new("s", ranks)
        def one(i, _):
            rows = rows_at(i * piece, piece)
            full = rows_at(here + i * piece, piece)
            buffer[full, :] = step(rows)
            remote(buffer.at[full, :], buffer.at[full, :], s_base + i, base + i, 2 * c + 1 - k, t).start()
            return 0
        lax.fori_loop(0, ranks, one, 0)
        for i in range(ranks):
            full = rows_at(here + i * piece, piece)
            pending.append((None, remote(buffer.at[full, :], buffer.at[full, :], s_base + i, base + i, 2 * c + 1 - k, t)))
        return base

    def wait_pieces(buffer, base):
        for i in range(ranks):
            arrive(buffer.at[rows_at(there + i * piece, piece), :], base + i)

    ra = exchange(lambda rows: dot(ctx[0, rows, :], W[A_BLK, 0, :, 512:768], 1, 1)
                  + dot(ctx[1, rows, :], W[A_BLK, 1, :, 512:768], 1, 1), 0)
    arrive(rbuf.at[0], ra)

    def norm_one(rows):
        x_rows = X[rows_at(here + rows.start, piece), :].astype(F32)
        z = x_rows + own[rows, :] + rbuf[0, rows, :].astype(F32) + bout[...]
        center = z - row_mean(z)
        inverse = lax.rsqrt(row_mean(center * center) + epsilon)
        normed = center * inverse
        n1[rows, :] = normed
        r1[rows, :] = jnp.broadcast_to(inverse, (piece, 128))
        return (normed * g1[...] + s1[...]).astype(BF)

    hb = over_pieces(norm_one, H)
    plane_forward(C_BLK, pc)
    plane_wait(B_BLK, pb)

    def up(start):
        def run(i, _):
            rows = rows_at(start + i * ROW_BLOCK, ROW_BLOCK)
            for tt in range(2):
                bias = bup[:, pl.ds(pl.multiple_of((2 * k + tt) * width, width), width)]
                value, slope = gelu_pair(dot(H[rows, :], W[B_BLK, tt]) + bias)
                act[tt, rows, :] = value.astype(BF)
                gp[tt, rows, :] = slope.astype(BF)
            return 0

        lax.fori_loop(0, half // ROW_BLOCK, run, 0)

    up(here)
    wait_pieces(H, hb)
    up(there)
    plane_wait(C_BLK, pc)
    rb = exchange(lambda rows: dot(act[0, rows, :], W[C_BLK, 0], 1, 1) + dot(act[1, rows, :], W[C_BLK, 1], 1, 1), 1)
    for q in range(ranks):
        arrive(cot.at[pl.ds(q * piece, piece), :], cot_base + q)
    vec[...] = jnp.zeros_like(vec)
    arrive(rbuf.at[1], rb)

    def col_add(row, v):
        vec[row : row + 1, :] = vec[row : row + 1, :] + jnp.sum(v, axis=0, keepdims=True)

    def norm_two(rows):
        z = n1[rows, :] * g1[...] + s1[...] + own[rows, :] + rbuf[1, rows, :].astype(F32) + bdown[...]
        center = z - row_mean(z)
        inverse = lax.rsqrt(row_mean(center * center) + epsilon)
        normed = center * inverse
        obuf[rows, :] = (normed * g2[...] + s2[...]).astype(BF)
        g = cot[rows, :].astype(F32)
        col_add(0, g * normed)
        col_add(1, g)
        gg = g * g2[...]
        back = inverse * (gg - row_mean(gg) - normed * row_mean(gg * normed))
        col_add(2, back)
        mix[rows, :] = back
        return back.astype(BF)

    g2b = over_pieces(norm_two, G2)

    def tree_return(target, base):
        for q in range(ranks):
            send_or_copy(obuf.at[pl.ds(q * piece, piece), :],
                         target.at[lax.rem(t, 2), rows_at(k * piece, piece), :],
                         base + lax.rem(t, 2) * 2 + k, 2 * c + home, q)

    out_base = new("r", 4)
    tree_return(out, out_base)
    out_sends = pending[-4:]

    def transpose_into(src):
        def run(i, _):
            rows = rows_at(i * piece, piece)
            tbuf[:, rows] = src[rows, :].astype(F32).T.astype(BF)
            return 0

        lax.fori_loop(0, length // piece, run, 0)

    def grad_rows(b, tt, chip, kk):
        return dW.at[b, tt, rows_at(chip * pair + kk * shard, shard), :]

    def reduce_one(b, tt):
        base = new("r", 4)
        for i, chip in enumerate((cy, cd)):
            send(grad_rows(b, tt, chip, 0), rs1.at[b, tt, 0, i], base + i, 2 * cy + k, t)
        for i, chip in enumerate((cx, cd)):
            send(grad_rows(b, tt, chip, 1), rs1.at[b, tt, 1, i], base + 2 + i, 2 * cx + k, t)
        return base

    def add_rows(b, tt, chip, kk, received):
        rows = rows_at(chip * pair + kk * shard, shard)
        dW[b, tt, rows, :] = (dW[b, tt, rows, :].astype(F32) + received.astype(F32)).astype(BF)

    def reduce_two(b, tt, base):
        nxt = new("r", 2)
        for kk, other in ((0, cx), (1, cy)):
            arrive(rs1.at[b, tt, kk, 1], base + 2 * kk + 1)
            add_rows(b, tt, other, kk, rs1[b, tt, kk, 1])
            send(grad_rows(b, tt, other, kk), rs2.at[b, tt, kk], nxt + kk, 2 * other + k, t)
        for kk in range(2):
            arrive(rs1.at[b, tt, kk, 0], base + 2 * kk)
            add_rows(b, tt, c, kk, rs1[b, tt, kk, 0])
        return nxt

    z_bases = [new("r", 4) for _ in range(3)]

    def reduce_z(b, tt, nxt):
        for kk in range(2):
            arrive(rs2.at[b, tt, kk], nxt + kk)
            add_rows(b, tt, c, kk, rs2[b, tt, kk])
            send_or_copy(grad_rows(b, tt, c, kk), zbuf.at[b, t], z_bases[b] + t, 2 * c + kk, 2 * k + tt)

    def reduce_end(b):
        for q in range(ranks):
            arrive(zbuf.at[b, q], z_bases[b] + q)
        total = zbuf[b, 0].astype(F32)
        for q in range(1, ranks):
            total = total + zbuf[b, q].astype(F32)
        return total

    def grad_matmul(b, tt, right):
        def run(i, _):
            rows = rows_at(i * ROW_BLOCK, ROW_BLOCK)
            dW[b, tt, rows, :] = dot(tbuf[rows, :], right[tt]).astype(BF)
            return 0

        lax.fori_loop(0, width // ROW_BLOCK, run, 0)

    wait_pieces(G2, g2b)
    transpose_into(G2)
    grad_matmul(C_BLK, 0, act)
    rc0 = reduce_one(C_BLK, 0)
    grad_matmul(C_BLK, 1, act)
    rc1 = reduce_one(C_BLK, 1)

    def back_up(i, _):
        rows = rows_at(i * ROW_BLOCK, ROW_BLOCK)
        for tt in range(2):
            gi = (dot(G2[rows, :], W[C_BLK, tt]) * gp[tt, rows, :].astype(F32)).astype(BF)
            gp[tt, rows, :] = gi
            row = 6 + 2 * k + tt
            vec[pl.ds(row, 1), :] = vec[pl.ds(row, 1), :] + jnp.sum(gi.astype(F32), axis=0, keepdims=True)
        return 0

    lax.fori_loop(0, length // ROW_BLOCK, back_up, 0)
    rh = exchange(lambda rows: dot(gp[0, rows, :], W[B_BLK, 0], 1, 1) + dot(gp[1, rows, :], W[B_BLK, 1], 1, 1), 0)
    transpose_into(H)
    grad_matmul(B_BLK, 0, gp)
    rb0 = reduce_one(B_BLK, 0)
    arrive(rbuf.at[0], rh)

    def norm_one_back(rows):
        grad = mix[rows, :] + own[rows, :] + rbuf[0, rows, :].astype(F32)
        normed = n1[rows, :]
        col_add(3, grad * normed)
        col_add(4, grad)
        hh = grad * g1[...]
        back = r1[rows, 0:1] * (hh - row_mean(hh) - normed * row_mean(hh * normed))
        col_add(5, back)
        mix[rows, :] = back
        return back.astype(BF)

    g1b = over_pieces(norm_one_back, G1)
    grad_matmul(B_BLK, 1, gp)
    rb1 = reduce_one(B_BLK, 1)
    wait_pieces(G1, g1b)

    def back_context(i, _):
        rows = rows_at(i * ROW_BLOCK, ROW_BLOCK)
        for tt in range(2):
            dctx[tt, rows, :] = dot(G1[rows, :], W[A_BLK, tt, :, 512:768]).astype(BF)
        return 0

    lax.fori_loop(0, length // ROW_BLOCK, back_context, 0)
    transpose_into(G1)

    def out_matmul(i, _):
        rows = rows_at(i * ROW_BLOCK, ROW_BLOCK)
        for tt in range(2):
            dW[A_BLK, tt, rows, 512:768] = dot(tbuf[rows, :], ctx[tt]).astype(BF)
        return 0

    lax.fori_loop(0, width // ROW_BLOCK, out_matmul, 0)
    transpose_into(X)

    grads = act

    def attend_back(tt, g):
        base = 6 * tt
        heads = HALF_HEADS[0:2] if g == 0 else HALF_HEADS[2:3]
        lanes = slice(128, 256) if g == 0 else slice(0, 128)
        dkv[...] = jnp.zeros_like(dkv)
        ki, vi = heads[0][1], heads[0][2]
        k_t = tiles[base + ki].astype(F32).T
        row = lax.broadcasted_iota(jnp.int32, k_t.shape, 0)
        k_masks = [jnp.where((row < HD) if hd[3] == 0 else (row >= HD), k_t, 0.0).astype(BF) for hd in heads]

        def back(i, _):
            rows = rows_at(i * ROW_BLOCK, ROW_BLOCK)
            dq_t = jnp.zeros((128, ROW_BLOCK), F32)
            do = dctx[tt, rows, lanes]
            prod = do.astype(F32) * ctx[tt, rows, lanes].astype(F32)
            for h, (qi, _, _, qh, vh) in enumerate(heads):
                qt = tiles[base + qi, rows, :]
                qm = jnp.where(lane_mask(qt.shape, qh), qt, jnp.zeros_like(qt))
                qa = jnp.concatenate([qm, raug[3 * tt + 2 * g + h, rows, :]], axis=1)
                pt = jnp.exp(dot(jnp.concatenate([tiles[base + ki], kf[...]], axis=1), qa, 1, 1))
                vmask = lane_mask(do.shape, vh)
                dom = jnp.where(vmask, do, jnp.zeros_like(do))
                delta = jnp.sum(jnp.where(vmask, prod, 0.0), axis=1, keepdims=True)
                doa = jnp.concatenate([dom, pieces(-delta, do.shape).astype(BF)], axis=1)
                dst = (pt * dot(jnp.concatenate([tiles[base + vi], kf[...]], axis=1), doa, 1, 1)).astype(BF)
                dkv[1] += dot(pt.astype(BF), dom)
                dkv[0] += dot(dst, qm)
                dq_t = dq_t + dot(k_masks[h], dst)
            dq = (dq_t.T * 0.125).astype(BF)
            if g == 0:
                grads[tt, rows, 0:128] = dq
            else:
                grads[tt, rows, 384:512] = dq
            return 0

        lax.fori_loop(0, length // ROW_BLOCK, back, 0)
        if g == 0:
            grads[tt, :, 128:256] = dkv[0].astype(BF)
            grads[tt, :, 256:384] = dkv[1].astype(BF)
        else:
            grads[tt, :, 384:512] = grads[tt, :, 384:512] + pltpu.roll(dkv[0], 64, 1).astype(BF)
            grads[tt, :, 512:640] = pltpu.roll(dkv[1], 64, 1).astype(BF)

    def qkv_matmul(tt):
        low = lax.broadcasted_iota(jnp.int32, (ROW_BLOCK, 128), 1) < HD

        def run(i, _):
            rows = rows_at(i * ROW_BLOCK, ROW_BLOCK)
            g = dot(tbuf[rows, :], grads[tt, :, 0:640])
            dW[A_BLK, tt, rows, 0:512] = g[:, 0:512].astype(BF)
            kept = dW[A_BLK, tt, rows, 512:640]
            dW[A_BLK, tt, rows, 512:640] = jnp.where(low, g[:, 512:640].astype(BF), kept)
            return 0

        lax.fori_loop(0, width // ROW_BLOCK, run, 0)
        row = 10 + 2 * k + tt
        vec[pl.ds(row, 1), 0:640] = jnp.sum(grads[tt, :, 0:640].astype(F32), axis=0, keepdims=True)

    attend_back(0, 0)
    sc0 = reduce_two(C_BLK, 0, rc0)
    sc1 = reduce_two(C_BLK, 1, rc1)
    attend_back(0, 1)
    reduce_z(C_BLK, 0, sc0)
    reduce_z(C_BLK, 1, sc1)
    qkv_matmul(0)
    ra0 = reduce_one(A_BLK, 0)
    attend_back(1, 0)
    sb0 = reduce_two(B_BLK, 0, rb0)
    sb1 = reduce_two(B_BLK, 1, rb1)
    gc_out[...] = reduce_end(C_BLK)
    attend_back(1, 1)
    qkv_matmul(1)
    ra1 = reduce_one(A_BLK, 1)

    v_base = new("r", 8)
    me = 4 * k + t
    vrecv[pl.ds(me, 1)] = vec[...][None]
    for dev in [(2 * c + 1 - k, t)] + partners[3:]:
        send(vec, vrecv.at[me], v_base + me, dev[0], dev[1])

    rx = exchange(lambda rows: dot(grads[0, rows, 0:640], W[A_BLK, 0, :, 0:640], 1, 1)
                  + dot(grads[1, rows, 0:640], W[A_BLK, 1, :, 0:640], 1, 1), 1)
    arrive(rbuf.at[1], rx)

    for s in range(2):
        for h in range(2):
            arrive(out.at[s, pl.ds(h * piece, piece), :], out_base + 2 * s + h)
    for entry in out_sends:
        pending[:] = [e for e in pending if e is not entry]
        settle(entry)

    def finish(i, _):
        rows = rows_at(i * piece, piece)
        obuf[rows, :] = (mix[rows, :] + own[rows, :] + rbuf[1, rows, :].astype(F32)).astype(BF)
        return 0

    lax.fori_loop(0, ranks, finish, 0)
    dx_base = new("r", 4)
    tree_return(dxr, dx_base)
    reduce_z(B_BLK, 0, sb0)
    reduce_z(B_BLK, 1, sb1)
    sa0 = reduce_two(A_BLK, 0, ra0)

    for j in range(1, 8):
        src = lax.rem(me + j, 8)
        arrive(vrecv.at[src], v_base + src)
    total = vrecv[0]
    for j in range(1, 8):
        total = total + vrecv[j]
    x_base = new("r", 2)
    vrecv2 = vrecv.at[8]
    vrecv3 = vrecv.at[9]
    vrecv[10] = total
    send(vrecv.at[10], vrecv2, x_base, 2 * cx + k, t)
    sa1 = reduce_two(A_BLK, 1, ra1)
    arrive(vrecv2, x_base)
    total = total + vrecv[8]
    vrecv[11] = total
    send(vrecv.at[11], vrecv3, x_base + 1, 2 * cy + k, t)
    reduce_z(A_BLK, 0, sa0)
    reduce_z(A_BLK, 1, sa1)
    gb_out[...] = reduce_end(B_BLK)
    arrive(vrecv3, x_base + 1)
    vec_out[...] = total + vrecv[9]
    for s in range(2):
        for h in range(2):
            arrive(dxr.at[s, pl.ds(h * piece, piece), :], dx_base + 2 * s + h)
    ga_out[...] = reduce_end(A_BLK)
    for entry in pending:
        settle(entry)


def fused_layer(tokens, cotangent, parents, segment_ids, w_qkv, w_out, w_up, w_down, vectors):
    local, quarter, width = tokens.shape
    length = segment_ids.shape[1]
    half = length // 2
    shard = w_qkv.shape[0]
    vm = pl.BlockSpec(memory_space=pltpu.VMEM)
    anywhere = pl.BlockSpec(memory_space=pl.ANY)
    rows = [v.reshape(1, -1) for v in vectors]
    sems = 192
    return pl.pallas_call(
        layer_kernel,
        name="layer",
        out_shape=(
            jax.ShapeDtypeStruct(tokens.shape, BF),
            jax.ShapeDtypeStruct(tokens.shape, BF),
            jax.ShapeDtypeStruct((shard, width), F32),
            jax.ShapeDtypeStruct((shard, width), F32),
            jax.ShapeDtypeStruct((shard, width), F32),
            jax.ShapeDtypeStruct((16, width), F32),
        ),
        in_specs=[anywhere, anywhere, vm, vm, vm, vm, anywhere, vm] + [vm] * len(rows),
        out_specs=(anywhere, anywhere, vm, vm, vm, vm),
        scratch_shapes=[
            pltpu.VMEM((3, 2, width, width), BF),
            pltpu.VMEM((length, width), BF),
            pltpu.VMEM((12, length, 128), BF),
            pltpu.VMEM((2, length, 256), BF),
            pltpu.VMEM((6, length, 128), BF),
            pltpu.VMEM((length, 128), BF),
            pltpu.VMEM((length, 128), BF),
            pltpu.VMEM((half, width), F32),
            pltpu.VMEM((half, 128), F32),
            pltpu.VMEM((length, width), BF),
            pltpu.VMEM((2, length, width), BF),
            pltpu.VMEM((2, length, width), BF),
            pltpu.VMEM((half, width), BF),
            pltpu.VMEM((half, width), F32),
            pltpu.VMEM((length, width), BF),
            pltpu.VMEM((length, width), BF),
            pltpu.VMEM((2, length, 256), BF),
            pltpu.VMEM((half, width), F32),
            pltpu.VMEM((2, half, width), BF),
            pltpu.VMEM((2, half, width), BF),
            pltpu.VMEM((half, width), BF),
            pltpu.VMEM((3, 2, width, width), BF),
            pltpu.VMEM((3, 2, 2, 2, shard, width), BF),
            pltpu.VMEM((3, 2, 2, shard, width), BF),
            pltpu.VMEM((3, 4, shard, width), BF),
            pltpu.VMEM((width, length), BF),
            pltpu.VMEM((2, length, 128), F32),
            pltpu.VMEM((shard, width), BF),
            pltpu.VMEM((shard, width), BF),
            pltpu.VMEM((2,) + segment_ids.shape, jnp.int32),
            pltpu.VMEM((2,) + parents.shape, jnp.int32),
            pltpu.VMEM((16, width), F32),
            pltpu.VMEM((12, 16, width), F32),
            pltpu.SemaphoreType.DMA((sems,)),
            pltpu.SemaphoreType.DMA((sems,)),
        ],
        compiler_params=pltpu.CompilerParams(collective_id=0, has_side_effects=True, vmem_limit_bytes=63 << 20),
        cost_estimate=pl.CostEstimate(flops=60 * 10**9, bytes_accessed=30 * 10**6, transcendentals=16 * 10**6),
    )(tokens, cotangent, parents, segment_ids, w_qkv, w_out, w_up, w_down, *rows)


def plane_body(tokens, parents, segment_ids, w_qkv, b_q, b_v, w_out, b_out, gain_one, shift_one,
               w_up, b_up, w_down, b_down, gain_two, shift_two, cotangent):
    out, dx, ga, gb, gc, vec = fused_layer(
        tokens, cotangent, parents, segment_ids, w_qkv, w_out, w_up, w_down,
        (b_q, b_v, b_out, gain_one, shift_one, b_up, b_down, gain_two, shift_two))
    blk = [ga[:, i * HD : (i + 1) * HD] for i in range(12)]
    grad_qkv = jnp.stack(
        [jnp.concatenate([blk[0], blk[1], blk[6]], 1), jnp.concatenate([blk[2], blk[3], blk[7]], 1),
         jnp.concatenate([blk[4], blk[5], blk[8]], 1)], axis=1)
    grad_out = jnp.concatenate([blk[10], blk[11], blk[9]], 1).T
    proj = vec[10:14]
    grad_bq = jnp.concatenate([proj[:, 0:128], proj[:, 384:448]], 1).reshape(-1)
    grad_bv = jnp.concatenate([proj[:, 256:384], proj[:, 512:576]], 1).reshape(-1)
    return (out, dx.astype(F32), grad_qkv, grad_bq, grad_bv, grad_out, vec[5], vec[3], vec[4],
            gb, vec[6:10].reshape(-1), gc.T, vec[2], vec[0], vec[1])


def solution(mesh):
    dp, ranks = mesh.shape["dp"], mesh.shape["tensor"]
    return jax.shard_map(
        plane_body if (dp, ranks) == (8, 4) else functools.partial(body, dp, ranks),
        mesh=mesh,
        in_specs=(P("dp", "tensor", None), P("dp", None), P("dp", None), P("dp", None, "tensor"), P(), P(),
                  P("tensor", "dp"), P(), P(), P(), P("dp", "tensor"), P(), P("tensor", "dp"), P(), P(), P(),
                  P("dp", "tensor", None)),
        out_specs=(P("dp", "tensor", None), P("dp", "tensor", None), P("dp", None, "tensor"), P(), P(),
                   P("tensor", "dp"), P(), P(), P(), P("dp", "tensor"), P(), P("tensor", "dp"), P(), P(), P()),
        check_vma=False,
    )
```

```python
import functools

import jax
import jax.numpy as jnp
from jax import lax
from jax.experimental import pallas as pl
from jax.experimental.pallas import tpu as pltpu
from jax.sharding import PartitionSpec as P

HD = 64
SEGS = 4
epsilon = 1e-12
BF = jnp.bfloat16
F32 = jnp.float32
FILL = -1e30
HALF_HEADS = ((0, 1, 2, 0, 0), (0, 1, 2, 1, 1), (3, 4, 5, 0, 1))


def dot(a, b, ca=1, cb=0):
    return lax.dot_general(a, b, (((ca,), (cb,)), ((), ())), preferred_element_type=F32)


def split3(v):
    hi = v.astype(BF).astype(F32)
    mid = (v - hi).astype(BF).astype(F32)
    low = v - hi - mid
    return hi, mid, low


def lane_mask(shape, half):
    lane = lax.broadcasted_iota(jnp.int32, shape, 1)
    return (lane < HD) if half == 0 else (lane >= HD)


def pieces(v, shape):
    lane = lax.broadcasted_iota(jnp.int32, shape, 1)
    hi, mid, low = split3(v)
    return jnp.where(lane == 4, hi, jnp.where(lane == 5, mid, jnp.where(lane == 6, low, 0.0)))


def attention_forward_kernel(x_ref, a_ref, bias_ref, rf_ref, kf_ref, tiles_ref, ctx_ref, raug_ref):
    length = x_ref.shape[0]
    block = 256
    count = length // block

    def project(i, _):
        rows = pl.ds(pl.multiple_of(i * block, block), block)
        xb = x_ref[rows, :]
        for t in range(2):
            m = dot(xb, a_ref[t, :, : 5 * 128]) + bias_ref[t][:, : 5 * 128]
            base = 6 * t
            q3 = m[:, 3 * 128 : 4 * 128]
            v3 = m[:, 4 * 128 : 5 * 128]
            tiles_ref[base, rows, :] = m[:, :128].astype(BF) * jnp.asarray(0.125, BF)
            tiles_ref[base + 1, rows, :] = m[:, 128:256].astype(BF)
            tiles_ref[base + 2, rows, :] = m[:, 256:384].astype(BF)
            tiles_ref[base + 3, rows, :] = q3.astype(BF) * jnp.asarray(0.125, BF)
            tiles_ref[base + 4, rows, :] = pltpu.roll(q3, 64, 1).astype(BF)
            tiles_ref[base + 5, rows, :] = pltpu.roll(v3, 64, 1).astype(BF)
        return 0

    lax.fori_loop(0, count, project, 0)
    ones = jnp.ones((length, 128), BF)

    for t in range(2):
        base = 6 * t

        def attend(i, _, t=t, base=base):
            rows = pl.ds(pl.multiple_of(i * block, block), block)
            rf = rf_ref[rows, :]
            parts = []
            for h, (qi, ki, vi, qh, vh) in enumerate(HALF_HEADS):
                q = tiles_ref[base + qi, rows, :]
                qm = jnp.where(lane_mask(q.shape, qh), q, jnp.zeros_like(q))
                qq = jnp.concatenate([qm, rf], axis=1)
                kk = jnp.concatenate([tiles_ref[base + ki], kf_ref[...]], axis=1)
                s = dot(qq, kk, 1, 1)
                m = jnp.max(s, axis=1, keepdims=True)
                p = jnp.exp(s - m).astype(BF)
                vv = jnp.concatenate([tiles_ref[base + vi], ones], axis=1)
                o = dot(p, vv)
                total = o[:, 128:129]
                ov = jnp.where(lane_mask((block, 128), vh), o[:, :128] / total, 0.0)
                lse = m + jnp.log(total)
                raug_ref[3 * t + h, rows, :] = rf + pieces(-lse, (block, 128)).astype(BF)
                parts.append(ov)
            ctx_ref[2 * t, rows, :] = (parts[0] + parts[1]).astype(BF)
            ctx_ref[2 * t + 1, rows, :] = parts[2].astype(BF)
            return 0

        lax.fori_loop(0, count, attend, 0)


def attention_backward_kernel(tiles_ref, ctx_ref, dctx_ref, raug_ref, kf_ref, out_ref, dk_ref, dv_ref):
    length = kf_ref.shape[0]
    block = 256
    count = length // block
    groups = ((HALF_HEADS[0], HALF_HEADS[1]), (HALF_HEADS[2],))
    for t in range(2):
        base = 6 * t
        for g, heads in enumerate(groups):
            dk_ref[...] = jnp.zeros_like(dk_ref)
            dv_ref[...] = jnp.zeros_like(dv_ref)
            ki = heads[0][1]
            vi = heads[0][2]
            k_t = tiles_ref[base + ki].astype(F32).T
            row = lax.broadcasted_iota(jnp.int32, k_t.shape, 0)
            k_masks = [
                jnp.where((row < HD) if qh == 0 else (row >= HD), k_t, 0.0).astype(BF)
                for (_, _, _, qh, _) in heads
            ]

            def back(i, _, t=t, base=base, g=g, heads=heads, k_masks=k_masks, ki=ki, vi=vi):
                rows = pl.ds(pl.multiple_of(i * block, block), block)
                dq_t = jnp.zeros((128, block), F32)
                do = dctx_ref[2 * t + g, rows, :]
                prod = do.astype(F32) * ctx_ref[2 * t + g, rows, :].astype(F32)
                for h, (qi, _, _, qh, vh) in enumerate(heads):
                    q = tiles_ref[base + qi, rows, :]
                    qm = jnp.where(lane_mask(q.shape, qh), q, jnp.zeros_like(q))
                    qa = jnp.concatenate([qm, raug_ref[3 * t + 2 * g + h, rows, :]], axis=1)
                    ka = jnp.concatenate([tiles_ref[base + ki], kf_ref[...]], axis=1)
                    pt = jnp.exp(dot(ka, qa, 1, 1))
                    vmask = lane_mask(do.shape, vh)
                    dom = jnp.where(vmask, do, jnp.zeros_like(do))
                    delta = jnp.sum(jnp.where(vmask, prod, 0.0), axis=1, keepdims=True)
                    doa = jnp.concatenate([dom, pieces(-delta, do.shape).astype(BF)], axis=1)
                    va = jnp.concatenate([tiles_ref[base + vi], kf_ref[...]], axis=1)
                    dst = (pt * dot(va, doa, 1, 1)).astype(BF)
                    dv_ref[...] += dot(pt.astype(BF), dom)
                    dk_ref[...] += dot(dst, qm)
                    dq_t = dq_t + dot(k_masks[h], dst)
                dq = dq_t.T * 0.125
                if g == 0:
                    out_ref[t, rows, 0:128] = dq.astype(BF)
                else:
                    out_ref[t, rows, 384:512] = dq.astype(BF)
                return 0

            lax.fori_loop(0, count, back, 0)
            if g == 0:
                out_ref[t, :, 128:256] = dk_ref[...].astype(BF)
                out_ref[t, :, 256:384] = dv_ref[...].astype(BF)
            else:
                out_ref[t, :, 384:512] = out_ref[t, :, 384:512] + pltpu.roll(dk_ref[...], 64, 1).astype(BF)
                out_ref[t, :, 512:640] = pltpu.roll(dv_ref[...], 64, 1).astype(BF)


def attention_forward(x, a, bias, rf, kf):
    length = x.shape[0]
    vm = pl.BlockSpec(memory_space=pltpu.VMEM)
    return pl.pallas_call(
        attention_forward_kernel,
        name="attn_fwd",
        out_shape=(
            jax.ShapeDtypeStruct((12, length, 128), BF),
            jax.ShapeDtypeStruct((4, length, 128), BF),
            jax.ShapeDtypeStruct((6, length, 128), BF),
        ),
        in_specs=[vm] * 5,
        out_specs=(vm,) * 3,
        compiler_params=pltpu.CompilerParams(vmem_limit_bytes=48 << 20),
        cost_estimate=pl.CostEstimate(flops=20 * 10**9, bytes_accessed=10 * 10**6, transcendentals=6 * 10**6),
    )(x, a, bias, rf, kf)


def attention_backward(tiles, ctx, dctx, raug, kf):
    length = kf.shape[0]
    vm = pl.BlockSpec(memory_space=pltpu.VMEM)
    return pl.pallas_call(
        attention_backward_kernel,
        name="attn_bwd",
        out_shape=jax.ShapeDtypeStruct((2, length, 640), BF),
        in_specs=[vm] * 5,
        out_specs=vm,
        scratch_shapes=[pltpu.VMEM((length, 128), F32), pltpu.VMEM((length, 128), F32)],
        compiler_params=pltpu.CompilerParams(vmem_limit_bytes=48 << 20),
        cost_estimate=pl.CostEstimate(flops=40 * 10**9, bytes_accessed=10 * 10**6, transcendentals=6 * 10**6),
    )(tiles, ctx, dctx, raug, kf)


def ancestry(parents):
    labels = jnp.arange(SEGS, dtype=jnp.int32)
    step = (parents[:, None] == labels[None, :]).astype(F32)
    reach = jnp.eye(SEGS, dtype=F32)
    total = reach
    for _ in range(SEGS - 1):
        reach = jnp.sum(reach[:, :, None] * step[None, :, :], axis=1)
        total = total + reach
    return (total > 0.5).astype(F32)


def gelu_parts(u):
    cdf = 0.5 * (1.0 + lax.erf(u * (2.0**-0.5)))
    pdf = jnp.exp(-0.5 * u * u) * ((2.0 * jnp.pi) ** -0.5)
    return u * cdf, cdf + u * pdf


def norm_parts(rows):
    center = rows - jnp.mean(rows, axis=-1, keepdims=True)
    inverse = lax.rsqrt(jnp.mean(center * center, axis=-1, keepdims=True) + epsilon)
    return center * inverse, inverse


def norm_back(grad_rows, normed, inverse, gain):
    scaled = grad_rows * gain
    return inverse * (
        scaled
        - jnp.mean(scaled, axis=-1, keepdims=True)
        - normed * jnp.mean(scaled * normed, axis=-1, keepdims=True)
    )


def body(dp, ranks, tokens, parents, segment_ids, w_qkv, b_q, b_v, w_out, b_out, gain_one, shift_one,
         w_up, b_up, w_down, b_down, gain_two, shift_two, cotangent):
    d = lax.axis_index("dp")
    ti = lax.axis_index("tensor")
    k = d % 2
    local, quarter, width = tokens.shape
    half_rows = quarter // 2
    own_rows = ranks * half_rows
    length = 2 * own_rows
    part = w_qkv.shape[2]
    hidden_part = w_up.shape[1]
    shard = w_qkv.shape[0]
    chips = dp // 2
    same_core = [[i for i in range(dp) if i % 2 == c] for c in range(2)]

    def swap(v):
        return lax.ppermute(v, "dp", [(i, i ^ 1) for i in range(dp)])

    def pick(v, index, axis=0):
        return lax.dynamic_index_in_dim(v, index, axis, keepdims=False)

    def join(own, peer, axis=0):
        return jnp.where(k == 0, jnp.stack([own, peer], axis), jnp.stack([peer, own], axis))

    def to_tree(v):
        v = v.reshape(local, 2, half_rows, width)
        mine = pick(v, k, 1)
        other = swap(pick(v, 1 - k, 1))
        trees = join(mine, other).reshape(ranks, half_rows, width)
        return lax.all_to_all(trees, "tensor", 0, 0, tiled=True).reshape(own_rows, width)

    def from_tree(v):
        v = lax.all_to_all(v.reshape(ranks, half_rows, width), "tensor", 0, 0, tiled=True)
        v = v.reshape(2, local, half_rows, width)
        other = swap(pick(v, 1 - k))
        return join(pick(v, k), other, 1).reshape(local, quarter, width)

    heads = w_qkv.reshape(shard, 3, 3, HD)
    q, kk, vv = heads[:, 0], heads[:, 1], heads[:, 2]
    out_t = w_out.T.reshape(shard, 3, HD)
    packed_a = jnp.concatenate(
        [q[:, 0], q[:, 1], kk[:, 0], kk[:, 1], vv[:, 0], vv[:, 1], q[:, 2], kk[:, 2], vv[:, 2],
         out_t[:, 2], out_t[:, 0], out_t[:, 1]], axis=1)

    def gather_weight(w):
        every = lax.all_gather(w, "tensor", axis=0, tiled=False).reshape(2, 2, shard, w.shape[1])
        mine = pick(every, k)
        other = swap(pick(every, 1 - k))
        both = join(mine, other, 1)
        full = lax.all_gather(both, "dp", axis=0, tiled=False, axis_index_groups=same_core)
        return full.transpose(1, 0, 2, 3, 4).reshape(2, chips * 2 * shard, w.shape[1])

    x_own = to_tree(tokens)
    w_a = gather_weight(packed_a)
    w_b = gather_weight(w_up)
    w_c = gather_weight(w_down.T)
    x = join(x_own, swap(x_own)).reshape(length, width)
    cot_own = to_tree(cotangent)

    seg_peer = swap(segment_ids)
    par_peer = swap(parents)
    all_seg = join(segment_ids, seg_peer).reshape(ranks, -1)
    all_par = join(parents, par_peer).reshape(ranks, -1)
    seg = pick(all_seg, ti).reshape(ranks, 2, half_rows).transpose(1, 0, 2).reshape(length)
    par = pick(all_par, ti)
    labels = jnp.arange(SEGS, dtype=jnp.int32)
    hot = (seg[:, None] == labels[None, :]).astype(F32)
    reach_rows = jnp.sum(hot[:, :, None] * ancestry(par)[None], axis=1)
    rf = jnp.concatenate([FILL * (1.0 - reach_rows), jnp.zeros((length, 124), F32)], axis=1).astype(BF)
    kf = jnp.concatenate([hot, jnp.ones((length, 3), F32), jnp.zeros((length, 121), F32)], axis=1).astype(BF)

    def half_vector(b, size):
        return lax.dynamic_slice_in_dim(b, 2 * k * size, 2 * size).reshape(2, size)

    bq = half_vector(b_q, part)
    bv = half_vector(b_v, part)
    zero64 = jnp.zeros((2, HD), F32)
    bias = jnp.concatenate(
        [bq[:, :128], jnp.zeros((2, 128), F32), bv[:, :128], bq[:, 128:], zero64, bv[:, 128:], zero64,
         jnp.zeros((2, 128), F32)], axis=1)[:, None, :]

    tiles, ctx, raug = attention_forward(x, w_a, bias, rf, kf)

    def exchange(partial):
        partial = partial.reshape(2, own_rows, width)
        received = swap(pick(partial, 1 - k).astype(BF))
        return pick(partial, k) + received.astype(F32)

    def spread_rows(v):
        return join(v, swap(v)).reshape(length, width)

    partial = 0.0
    for t in range(2):
        partial = partial + dot(ctx[2 * t + 1], w_a[t, :, 512:640], 1, 1) + dot(ctx[2 * t], w_a[t, :, 640:768], 1, 1)
    attended = exchange(partial)
    n1, r1 = norm_parts(x_own.astype(F32) + attended + b_out)
    hidden = n1 * gain_one + shift_one
    rows_low = spread_rows(hidden.astype(BF))
    up_bias = half_vector(b_up, hidden_part)
    inner = [dot(rows_low, w_b[t]) + up_bias[t] for t in range(2)]
    acts = [gelu_parts(u) for u in inner]
    activated = [a.astype(BF) for a, _ in acts]
    branch = exchange(sum(dot(activated[t], w_c[t], 1, 1) for t in range(2)))
    n2, r2 = norm_parts(hidden + branch + b_down)
    output = n2 * gain_two + shift_two
    g = cot_own.astype(F32)
    gain_two_part = jnp.sum(g * n2, axis=0)
    shift_two_part = jnp.sum(g, axis=0)
    mix_two = norm_back(g, n2, r2, gain_two)
    b_down_part = jnp.sum(mix_two, axis=0)
    two_rows = spread_rows(mix_two.astype(BF))
    d_c = [dot(two_rows, activated[t], 0, 0) for t in range(2)]
    grad_inner = [(dot(two_rows, w_c[t]) * acts[t][1]).astype(BF) for t in range(2)]
    b_up_part = jnp.concatenate([jnp.sum(v.astype(F32), axis=0) for v in grad_inner])
    d_b = [dot(rows_low, grad_inner[t], 0, 0) for t in range(2)]
    grad_hidden = mix_two + exchange(sum(dot(grad_inner[t], w_b[t], 1, 1) for t in range(2)))
    gain_one_part = jnp.sum(grad_hidden * n1, axis=0)
    shift_one_part = jnp.sum(grad_hidden, axis=0)
    mix_one = norm_back(grad_hidden, n1, r1, gain_one)
    b_out_part = jnp.sum(mix_one, axis=0)
    one_rows = spread_rows(mix_one.astype(BF))
    dctx = jnp.stack(
        [dot(one_rows, w_a[t, :, lo : lo + 128]).astype(BF) for t in range(2) for lo in (640, 512)])
    d_tiles = attention_backward(tiles, ctx, dctx, raug, kf)

    def d_a_of(t):
        qkv = dot(x, d_tiles[t], 0, 0)
        o2 = dot(one_rows, ctx[2 * t + 1], 0, 0)
        o01 = dot(one_rows, ctx[2 * t], 0, 0)
        lane = lax.broadcasted_iota(jnp.int32, o2.shape, 1)
        return jnp.concatenate([qkv[:, :512], jnp.where(lane < HD, qkv[:, 512:], o2), o01], axis=1)

    d_a = [d_a_of(t) for t in range(2)]
    lane_zero = jnp.where(jnp.arange(640) < 576, 1.0, 0.0).astype(BF)
    grad_x = exchange(sum(dot(d_tiles[t] * lane_zero, w_a[t, :, :640], 1, 1) for t in range(2)))
    input_grad = from_tree((mix_one + grad_x).astype(BF)).astype(F32)
    out = from_tree(output.astype(BF))

    def scatter_weight(pair):
        v = jnp.stack([p.astype(BF) for p in pair]).reshape(2, chips, 2, shard, width).transpose(1, 2, 0, 3, 4)
        v = v.reshape(chips * 4 * shard, width)
        v = lax.psum_scatter(v, "dp", scatter_dimension=0, tiled=True, axis_index_groups=same_core)
        v = v.reshape(2, 2, shard, width)
        other = swap(pick(v, 1 - k))
        v = join(pick(v, k), other).reshape(ranks * shard, width)
        return lax.psum_scatter(v, "tensor", scatter_dimension=0, tiled=True).astype(F32)

    g_c = scatter_weight(d_c)
    g_b = scatter_weight(d_b)
    g_a = scatter_weight(d_a)
    blk = [g_a[:, i * HD : (i + 1) * HD] for i in range(12)]
    grad_qkv = jnp.stack(
        [jnp.concatenate([blk[0], blk[1], blk[6]], 1), jnp.concatenate([blk[2], blk[3], blk[7]], 1),
         jnp.concatenate([blk[4], blk[5], blk[8]], 1)], axis=1)
    grad_out = jnp.concatenate([blk[10], blk[11], blk[9]], 1).T

    sums = jnp.sum(d_tiles.astype(F32), axis=1)
    bq_part = jnp.concatenate([sums[:, :128], sums[:, 384:448]], axis=1).reshape(-1)
    bv_part = jnp.concatenate([sums[:, 256:384], sums[:, 512:576]], axis=1).reshape(-1)

    def spread(v, size):
        return lax.dynamic_update_slice_in_dim(jnp.zeros((size,), F32), v, k * v.shape[0], 0)

    summed = lax.psum(
        (spread(bq_part, width), spread(bv_part, width), b_out_part, gain_one_part, shift_one_part,
         spread(b_up_part, b_up.shape[0]), b_down_part, gain_two_part, shift_two_part), ("dp", "tensor"))
    return (out, input_grad, grad_qkv, summed[0], summed[1], grad_out, summed[2], summed[3], summed[4],
            g_b, summed[5], g_c.T, summed[6], summed[7], summed[8])


A_BLK, B_BLK, C_BLK = 0, 1, 2
ROW_BLOCK = 256


def erf_exact(x):
    x = jnp.clip(x, -3.832506856900711, 3.832506856900711)
    z = x * x
    p = jnp.full_like(z, 0.00022905065861350646)
    for c in (0.0034082910107109506, 0.050955695062380861, 0.18520832239976145, 1.128379143519084):
        p = p * z + c
    q = jnp.full_like(z, -1.1791602954361697e-7)
    for c in (0.000023547966471313185, 0.0010179625278914885, 0.014070470171167667, 0.11098505178285362,
              0.49746925110067538, 1.0):
        q = q * z + c
    return x * p / q


def gelu_pair(u):
    cdf = 0.5 * (1.0 + erf_exact(u * (2.0**-0.5)))
    pdf = jnp.exp(-0.5 * u * u) * ((2.0 * jnp.pi) ** -0.5)
    return u * cdf, cdf + u * pdf


def row_mean(v):
    return jnp.mean(v, axis=-1, keepdims=True)


def layer_kernel(tok, cot_in, par, seg, wqkv, wout, wup, wdown, bq, bv, bout, g1, s1, bup, bdown, g2, s2,
                 out, dxr, ga_out, gb_out, gc_out, vec_out,
                 W, X, tiles, ctx, raug, rf, kf, n1, r1, H, act, gp, cot, mix, G2, G1, dctx, own,
                 sbuf, rbuf, obuf, dW, rs1, rs2, zbuf, tbuf, dkv, ash, seg_all, par_all, vec, vrecv,
                 ssem, rsem):
    row_of = {n: ref[...][None, :] for n, ref in (("bout", bout), ("g1", g1), ("s1", s1), ("bdown", bdown),
                                                  ("g2", g2), ("s2", s2))}
    d = lax.axis_index("dp")
    t = lax.axis_index("tensor")
    k = lax.rem(d, 2)
    c = d // 2
    ranks = 4
    cx = c + 1 - 2 * lax.rem(c, 2)
    cy = lax.rem(c + 2, 4)
    cd = 3 - c
    length = X.shape[0]
    half = length // 2
    piece = half // ranks
    width = X.shape[1]
    shard = ash.shape[0]
    pair = 2 * shard
    home = t // 2
    here = k * half
    there = (1 - k) * half
    counters = {"s": 0, "r": 0}
    pending = []

    def new(kind, n=1):
        base = counters[kind]
        counters[kind] = base + n
        return base

    def remote(src, dst, s, r, dd, tt):
        return pltpu.make_async_remote_copy(
            src_ref=src, dst_ref=dst, send_sem=ssem.at[s], recv_sem=rsem.at[r], device_id=(dd, tt),
            device_id_type=pl.DeviceIdType.MESH)

    def send(src, dst, r, dd, tt):
        cp = remote(src, dst, new("s"), r, dd, tt)
        cp.start()
        pending.append((None, cp))

    def send_or_copy(src, dst, r, dd, tt):
        cp = remote(src, dst, new("s"), r, dd, tt)
        mine = jnp.logical_and(dd == d, tt == t)

        @pl.when(mine)
        def _():
            pltpu.make_async_copy(src, dst, rsem.at[r]).start()

        @pl.when(jnp.logical_not(mine))
        def _():
            cp.start()

        pending.append((mine, cp))

    def settle(entry):
        mine, cp = entry
        if mine is None:
            cp.wait_send()
        else:
            @pl.when(jnp.logical_not(mine))
            def _():
                cp.wait_send()

    def arrive(dst, r):
        pltpu.make_async_copy(dst, dst, rsem.at[r]).wait()

    def rows_at(start, n, align=None):
        return pl.ds(pl.multiple_of(start, align or n), n)

    barrier = pltpu.get_barrier_semaphore()
    partners = [(2 * c + 1 - k, t), (2 * cx + k, t), (2 * cy + k, t)]
    for j in range(1, ranks):
        for core in range(2):
            partners.append((2 * c + core, lax.rem(t + j, ranks)))
    for dev in partners:
        pl.semaphore_signal(barrier, inc=1, device_id=dev, device_id_type=pl.DeviceIdType.MESH)
    pl.semaphore_wait(barrier, len(partners))

    slot = lax.rem(t, 2) * 2 + k
    step = 1 - 2 * k

    def shard_rows(b, tt, kk):
        return W.at[b, tt, rows_at(c * pair + kk * shard, shard), :]

    def send_if(wanted, src, dst, r, dd, tt):
        cp = remote(src, dst, new("s"), r, dd, tt)

        @pl.when(wanted)
        def _():
            cp.start()

        pending.append((jnp.logical_not(wanted), cp))

    def z_own(b, src):
        base = new("r", 4)
        dst = shard_rows(b, lax.rem(t, 2), k)
        send_if(t < ranks - 1, src, dst, base + slot, 2 * c + home, lax.rem(t + 1, ranks))
        send_if(t > 0, src, dst, base + slot, 2 * c + home, lax.rem(t + ranks - 1, ranks))
        send_or_copy(src, dst, base + slot, 2 * c + home, t)
        return base

    def z_pass(b, base, tt, wanted):
        for kk in range(2):
            rows = shard_rows(b, tt, kk)
            arrive(rows, base + 2 * tt + kk)
            send_if(wanted, rows, rows, base + 2 * tt + kk, d, lax.rem(t + step + ranks, ranks))

    def z_near(b, base):
        z_pass(b, base, 1 - k, t == 2 - k)

    def z_far(b, base):
        z_pass(b, base, k, jnp.logical_or(t == 1, t == 2))

    def plane_rows(b, far, chip):
        return W.at[b, k if far else 1 - k, rows_at(chip * pair, pair), :]

    def plane_send(b, far):
        base = new("r", 3)
        src = plane_rows(b, far, c)
        send(src, src, base, 2 * cx + k, t)
        send(src, src, base + 1, 2 * cy + k, t)
        return base

    def plane_forward(b, near, far):
        rows = plane_rows(b, False, cx)
        arrive(rows, near)
        send(rows, rows, near + 2, 2 * cy + k, t)
        rows = plane_rows(b, True, cy)
        arrive(rows, far + 1)
        send(rows, rows, far + 2, 2 * cx + k, t)

    def plane_wait(b, near, far):
        arrive(plane_rows(b, False, cy), near + 1)
        arrive(plane_rows(b, True, cx), far)
        arrive(plane_rows(b, False, cd), near + 2)
        arrive(plane_rows(b, True, cd), far + 2)

    q_all = wqkv[0].astype(F32)
    k_all = wqkv[1].astype(F32)
    v_all = wqkv[2].astype(F32)
    o_all = wout[...].astype(F32).T
    ash[:, 0:128] = q_all[:, :128].astype(BF)
    ash[:, 128:256] = k_all[:, :128].astype(BF)
    ash[:, 256:384] = v_all[:, :128].astype(BF)
    ash[:, 384:512] = jnp.concatenate([q_all[:, 128:], k_all[:, 128:]], axis=1).astype(BF)
    ash[:, 512:640] = jnp.concatenate([v_all[:, 128:], o_all[:, 128:]], axis=1).astype(BF)
    ash[:, 640:768] = o_all[:, :128].astype(BF)
    za = z_own(A_BLK, ash)

    seg_base = new("r", 2)
    for i, (src, dst) in enumerate(((seg, seg_all), (par, par_all))):
        send(src, dst.at[k], seg_base + i, 2 * c + 1 - k, t)
        dst[pl.ds(k, 1)] = src[...][None]
    z_near(A_BLK, za)
    pa_near = plane_send(A_BLK, False)
    zb = z_own(B_BLK, wup)
    z_far(A_BLK, za)
    pa_far = plane_send(A_BLK, True)

    def tree_send(src, dst):
        base = new("r", 4)
        for s in range(2):
            for h in range(2):
                send_or_copy(src.at[s, pl.ds(h * piece, piece), :], dst(h), base + t, 2 * c + h, 2 * k + s)
        return base

    tok_base = tree_send(tok, lambda h: X.at[rows_at(h * half + t * piece, piece), :])

    arrive(seg_all.at[1 - k], seg_base)
    arrive(par_all.at[1 - k], seg_base + 1)
    lane1 = lax.broadcasted_iota(jnp.int32, (1, 128), 1)
    both = par_all[pl.ds(home, 1)][0]
    second = lax.rem(t, 2) == 1
    parents = jnp.where(second, both[1:2, :], both[0:1, :])
    par_of = [jnp.broadcast_to(parents[:, j : j + 1], (1, 128)) for j in range(SEGS)]
    reach_rows = []
    for s in range(SEGS):
        now = jnp.full((1, 128), s, jnp.int32)
        seen = lane1 == s
        for _ in range(SEGS - 1):
            now = functools.reduce(lambda acc, j: jnp.where(now == j, par_of[j], acc), range(SEGS), now)
            seen = jnp.logical_or(seen, lane1 == now)
        reach_rows.append(jnp.where(lane1 < SEGS, jnp.where(seen, 0.0, FILL), 0.0))
    lane_f = lax.broadcasted_iota(jnp.int32, (piece, 128), 1).astype(F32)
    for h in range(2):
        for q in range(ranks):
            both = seg_all[pl.ds(home, 1), :, pl.ds((2 * q + h) * piece, piece)][0].astype(F32)
            part = jnp.where(second, both[1:2, :], both[0:1, :])
            segs = jnp.broadcast_to(part, (piece, piece)).T
            rows = pl.ds(h * half + q * piece, piece)
            table = jnp.zeros((piece, 128), F32)
            for s in range(SEGS):
                table = jnp.where(segs == s, jnp.broadcast_to(reach_rows[s], (piece, 128)), table)
            rf[rows, :] = table.astype(BF)
            hot = jnp.where(lane_f < SEGS, jnp.where(segs == lane_f, 1.0, 0.0), jnp.where(lane_f < SEGS + 3, 1.0, 0.0))
            kf[rows, :] = hot.astype(BF)

    z_near(B_BLK, zb)
    z_far(B_BLK, zb)
    plane_forward(A_BLK, pa_near, pa_far)
    pb_near = plane_send(B_BLK, False)
    pb_far = plane_send(B_BLK, True)
    fwd_base = new("r", 4)
    for j in range(ranks):
        q = lax.rem(t + j, ranks)
        mine = X.at[rows_at(here + q * piece, piece), :]
        arrive(mine, tok_base + q)
        send(mine, mine, fwd_base + q, 2 * c + 1 - k, t)
    zc = z_own(C_BLK, wdown)
    plane_wait(A_BLK, pa_near, pa_far)

    def half_lanes(ref):
        row = ref[...][None, :]
        return jnp.where(k == 0, row[:, : width // 2], row[:, width // 2 :])

    bq2, bv2 = half_lanes(bq), half_lanes(bv)
    zero64 = jnp.zeros((1, HD), F32)
    biases = []
    for tt in range(2):
        lo = 192 * tt
        biases.append((bq2[:, lo : lo + 128], bv2[:, lo : lo + 128],
                       jnp.concatenate([bq2[:, lo + 128 : lo + 192], zero64], axis=1),
                       jnp.concatenate([bv2[:, lo + 128 : lo + 192], zero64], axis=1)))
    eighth = jnp.asarray(0.125, BF)

    def project(start):
        def run(i, _):
            rows = rows_at(start + i * ROW_BLOCK, ROW_BLOCK)
            xb = X[rows, :]
            for tt in range(2):
                m = dot(xb, W[A_BLK, tt, :, 0:640])
                b_q01, b_v01, b_q2, b_v2 = biases[tt]
                base = 6 * tt
                q3 = m[:, 384:512] + b_q2
                v3 = m[:, 512:640] + b_v2
                tiles[base, rows, :] = (m[:, 0:128] + b_q01).astype(BF) * eighth
                tiles[base + 1, rows, :] = m[:, 128:256].astype(BF)
                tiles[base + 2, rows, :] = (m[:, 256:384] + b_v01).astype(BF)
                tiles[base + 3, rows, :] = q3.astype(BF) * eighth
                tiles[base + 4, rows, :] = pltpu.roll(q3, 64, 1).astype(BF)
                tiles[base + 5, rows, :] = pltpu.roll(v3, 64, 1).astype(BF)
            return 0

        lax.fori_loop(0, half // ROW_BLOCK, run, 0)

    project(here)
    for q in range(ranks):
        arrive(X.at[rows_at(there + q * piece, piece), :], fwd_base + q)
    project(there)

    ones = jnp.ones((length, 128), BF)

    def attend_all(tt):
        base = 6 * tt

        def attend(i, _):
            rows = rows_at(i * ROW_BLOCK, ROW_BLOCK)
            rfb = rf[rows, :]
            parts = []
            for h, (qi, ki, vi, qh, vh) in enumerate(HALF_HEADS):
                qt = tiles[base + qi, rows, :]
                qm = jnp.where(lane_mask(qt.shape, qh), qt, jnp.zeros_like(qt))
                s = dot(jnp.concatenate([qm, rfb], axis=1), jnp.concatenate([tiles[base + ki], kf[...]], axis=1), 1, 1)
                top = jnp.max(s, axis=1, keepdims=True)
                p = jnp.exp(s - top).astype(BF)
                o = dot(p, jnp.concatenate([tiles[base + vi], ones], axis=1))
                total = o[:, 128:129]
                parts.append(jnp.where(lane_mask((ROW_BLOCK, 128), vh), o[:, :128] / total, 0.0))
                lse = top + jnp.log(total)
                raug[3 * tt + h, rows, :] = rfb + pieces(-lse, (ROW_BLOCK, 128)).astype(BF)
            ctx[tt, rows, 0:128] = parts[2].astype(BF)
            ctx[tt, rows, 128:256] = (parts[0] + parts[1]).astype(BF)
            return 0

        lax.fori_loop(0, length // ROW_BLOCK, attend, 0)

    z_near(C_BLK, zc)
    attend_all(0)
    z_far(C_BLK, zc)
    plane_forward(B_BLK, pb_near, pb_far)
    pc_near = plane_send(C_BLK, False)
    pc_far = plane_send(C_BLK, True)
    cot_base = tree_send(cot_in, lambda h: cot.at[rows_at(t * piece, piece), :])
    attend_all(1)

    exchanged = []

    def exchange(compute, index):
        r = new("r")
        if len(exchanged) >= 2:
            done = exchanged[-2]
            pending[:] = [e for e in pending if e is not done]
            done[1].wait_send()

        def give(i, _):
            rows = rows_at(i * ROW_BLOCK, ROW_BLOCK)
            sbuf[index, rows, :] = compute(rows_at(there + i * ROW_BLOCK, ROW_BLOCK)).astype(BF)
            return 0

        lax.fori_loop(0, half // ROW_BLOCK, give, 0)
        send(sbuf.at[index], rbuf.at[index], r, 2 * c + 1 - k, t)
        exchanged.append(pending[-1])

        def keep(i, _):
            rows = rows_at(i * ROW_BLOCK, ROW_BLOCK)
            own[rows, :] = compute(rows_at(here + i * ROW_BLOCK, ROW_BLOCK))
            return 0

        lax.fori_loop(0, half // ROW_BLOCK, keep, 0)
        return r

    def over_pieces(step, buffer):
        base = new("r", ranks)
        s_base = new("s", ranks)
        def one(i, _):
            rows = rows_at(i * piece, piece)
            full = rows_at(here + i * piece, piece)
            buffer[full, :] = step(rows)
            remote(buffer.at[full, :], buffer.at[full, :], s_base + i, base + i, 2 * c + 1 - k, t).start()
            return 0
        lax.fori_loop(0, ranks, one, 0)
        for i in range(ranks):
            full = rows_at(here + i * piece, piece)
            pending.append((None, remote(buffer.at[full, :], buffer.at[full, :], s_base + i, base + i, 2 * c + 1 - k, t)))
        return base

    def wait_pieces(buffer, base):
        for i in range(ranks):
            arrive(buffer.at[rows_at(there + i * piece, piece), :], base + i)

    ra = exchange(lambda rows: dot(ctx[0, rows, :], W[A_BLK, 0, :, 512:768], 1, 1)
                  + dot(ctx[1, rows, :], W[A_BLK, 1, :, 512:768], 1, 1), 0)
    arrive(rbuf.at[0], ra)

    def norm_one(rows):
        x_rows = X[rows_at(here + rows.start, piece), :].astype(F32)
        z = x_rows + own[rows, :] + rbuf[0, rows, :].astype(F32) + row_of['bout']
        center = z - row_mean(z)
        inverse = lax.rsqrt(row_mean(center * center) + epsilon)
        normed = center * inverse
        n1[rows, :] = normed
        r1[rows, :] = jnp.broadcast_to(inverse, (piece, 128))
        return (normed * row_of['g1'] + row_of['s1']).astype(BF)

    hb = over_pieces(norm_one, H)
    plane_wait(B_BLK, pb_near, pb_far)

    up_row = bup[...][None, :]
    up_bias = [jnp.where(k == 0, up_row[:, tt * width : (tt + 1) * width],
                         up_row[:, (2 + tt) * width : (3 + tt) * width]) for tt in range(2)]

    def up(start):
        def run(i, _):
            rows = rows_at(start + i * ROW_BLOCK, ROW_BLOCK)
            for tt in range(2):
                bias = up_bias[tt]
                value, slope = gelu_pair(dot(H[rows, :], W[B_BLK, tt]) + bias)
                act[tt, rows, :] = value.astype(BF)
                gp[tt, rows, :] = slope.astype(BF)
            return 0

        lax.fori_loop(0, half // ROW_BLOCK, run, 0)

    up(here)
    plane_forward(C_BLK, pc_near, pc_far)
    wait_pieces(H, hb)
    up(there)
    plane_wait(C_BLK, pc_near, pc_far)
    rb = exchange(lambda rows: dot(act[0, rows, :], W[C_BLK, 0], 1, 1) + dot(act[1, rows, :], W[C_BLK, 1], 1, 1), 1)
    for q in range(ranks):
        arrive(cot.at[pl.ds(q * piece, piece), :], cot_base + q)
    vec[...] = jnp.zeros_like(vec)
    arrive(rbuf.at[1], rb)

    def col_add(row, v):
        vec[row : row + 1, :] = vec[row : row + 1, :] + jnp.sum(v, axis=0, keepdims=True)

    def norm_two(rows):
        z = n1[rows, :] * row_of['g1'] + row_of['s1'] + own[rows, :] + rbuf[1, rows, :].astype(F32) + row_of['bdown']
        center = z - row_mean(z)
        inverse = lax.rsqrt(row_mean(center * center) + epsilon)
        normed = center * inverse
        obuf[rows, :] = (normed * row_of['g2'] + row_of['s2']).astype(BF)
        g = cot[rows, :].astype(F32)
        col_add(0, g * normed)
        col_add(1, g)
        gg = g * row_of['g2']
        back = inverse * (gg - row_mean(gg) - normed * row_mean(gg * normed))
        col_add(2, back)
        mix[rows, :] = back
        return back.astype(BF)

    g2b = over_pieces(norm_two, G2)

    def tree_return(target, base):
        for q in range(ranks):
            send_or_copy(obuf.at[pl.ds(q * piece, piece), :],
                         target.at[lax.rem(t, 2), rows_at(k * piece, piece), :],
                         base + lax.rem(t, 2) * 2 + k, 2 * c + home, q)

    out_base = new("r", 4)
    tree_return(out, out_base)
    out_sends = pending[-4:]

    def transpose_into(src):
        def run(i, _):
            rows = rows_at(i * piece, piece)
            tbuf[:, rows] = src[rows, :].astype(F32).T.astype(BF)
            return 0

        lax.fori_loop(0, length // piece, run, 0)

    def grad_rows(b, tt, chip, kk):
        return dW.at[b, tt, rows_at(chip * pair + kk * shard, shard), :]

    def reduce_one(b, tt):
        base = new("r", 4)
        for i, chip in enumerate((cy, cd)):
            send(grad_rows(b, tt, chip, 0), rs1.at[b, tt, 0, i], base + i, 2 * cy + k, t)
        for i, chip in enumerate((cx, cd)):
            send(grad_rows(b, tt, chip, 1), rs1.at[b, tt, 1, i], base + 2 + i, 2 * cx + k, t)
        return base

    def add_rows(b, tt, chip, kk, received):
        rows = rows_at(chip * pair + kk * shard, shard)
        dW[b, tt, rows, :] = (dW[b, tt, rows, :].astype(F32) + received.astype(F32)).astype(BF)

    def reduce_two(b, tt, base):
        nxt = new("r", 2)
        for kk, other in ((0, cx), (1, cy)):
            arrive(rs1.at[b, tt, kk, 1], base + 2 * kk + 1)
            add_rows(b, tt, other, kk, rs1[b, tt, kk, 1])
            send(grad_rows(b, tt, other, kk), rs2.at[b, tt, kk], nxt + kk, 2 * other + k, t)
        for kk in range(2):
            arrive(rs1.at[b, tt, kk, 0], base + 2 * kk)
            add_rows(b, tt, c, kk, rs1[b, tt, kk, 0])
        return nxt

    z_bases = [new("r", 4) for _ in range(3)]

    def reduce_z(b, tt, nxt):
        for kk in range(2):
            arrive(rs2.at[b, tt, kk], nxt + kk)
            add_rows(b, tt, c, kk, rs2[b, tt, kk])
            send_or_copy(grad_rows(b, tt, c, kk), zbuf.at[b, t], z_bases[b] + t, 2 * c + kk, 2 * k + tt)

    def reduce_end(b):
        for q in range(ranks):
            arrive(zbuf.at[b, q], z_bases[b] + q)
        total = zbuf[b, 0].astype(F32)
        for q in range(1, ranks):
            total = total + zbuf[b, q].astype(F32)
        return total

    def grad_matmul(b, tt, right):
        def run(i, _):
            rows = rows_at(i * ROW_BLOCK, ROW_BLOCK)
            dW[b, tt, rows, :] = dot(tbuf[rows, :], right[tt]).astype(BF)
            return 0

        lax.fori_loop(0, width // ROW_BLOCK, run, 0)

    wait_pieces(G2, g2b)
    transpose_into(G2)
    grad_matmul(C_BLK, 0, act)
    rc0 = reduce_one(C_BLK, 0)
    grad_matmul(C_BLK, 1, act)
    rc1 = reduce_one(C_BLK, 1)

    def back_up(i, _):
        rows = rows_at(i * ROW_BLOCK, ROW_BLOCK)
        for tt in range(2):
            gi = (dot(G2[rows, :], W[C_BLK, tt]) * gp[tt, rows, :].astype(F32)).astype(BF)
            gp[tt, rows, :] = gi
            row = 6 + 2 * k + tt
            vec[pl.ds(row, 1), :] = vec[pl.ds(row, 1), :] + jnp.sum(gi.astype(F32), axis=0, keepdims=True)
        return 0

    lax.fori_loop(0, length // ROW_BLOCK, back_up, 0)
    rh = exchange(lambda rows: dot(gp[0, rows, :], W[B_BLK, 0], 1, 1) + dot(gp[1, rows, :], W[B_BLK, 1], 1, 1), 0)
    transpose_into(H)
    grad_matmul(B_BLK, 0, gp)
    rb0 = reduce_one(B_BLK, 0)
    sc0 = reduce_two(C_BLK, 0, rc0)
    arrive(rbuf.at[0], rh)

    def norm_one_back(rows):
        grad = mix[rows, :] + own[rows, :] + rbuf[0, rows, :].astype(F32)
        normed = n1[rows, :]
        col_add(3, grad * normed)
        col_add(4, grad)
        hh = grad * row_of['g1']
        back = r1[rows, 0:1] * (hh - row_mean(hh) - normed * row_mean(hh * normed))
        col_add(5, back)
        mix[rows, :] = back
        return back.astype(BF)

    g1b = over_pieces(norm_one_back, G1)
    grad_matmul(B_BLK, 1, gp)
    rb1 = reduce_one(B_BLK, 1)
    wait_pieces(G1, g1b)

    def back_context(i, _):
        rows = rows_at(i * ROW_BLOCK, ROW_BLOCK)
        for tt in range(2):
            dctx[tt, rows, :] = dot(G1[rows, :], W[A_BLK, tt, :, 512:768]).astype(BF)
        return 0

    lax.fori_loop(0, length // ROW_BLOCK, back_context, 0)
    sc1 = reduce_two(C_BLK, 1, rc1)
    transpose_into(G1)

    def out_matmul(i, _):
        rows = rows_at(i * ROW_BLOCK, ROW_BLOCK)
        for tt in range(2):
            dW[A_BLK, tt, rows, 512:768] = dot(tbuf[rows, :], ctx[tt]).astype(BF)
        return 0

    lax.fori_loop(0, width // ROW_BLOCK, out_matmul, 0)
    transpose_into(X)

    grads = act

    def attend_back(tt, g):
        base = 6 * tt
        heads = HALF_HEADS[0:2] if g == 0 else HALF_HEADS[2:3]
        lanes = slice(128, 256) if g == 0 else slice(0, 128)
        dkv[...] = jnp.zeros_like(dkv)
        ki, vi = heads[0][1], heads[0][2]
        k_t = tiles[base + ki].astype(F32).T
        row = lax.broadcasted_iota(jnp.int32, k_t.shape, 0)
        k_masks = [jnp.where((row < HD) if hd[3] == 0 else (row >= HD), k_t, 0.0).astype(BF) for hd in heads]

        def back(i, _):
            rows = rows_at(i * ROW_BLOCK, ROW_BLOCK)
            dq_t = jnp.zeros((128, ROW_BLOCK), F32)
            do = dctx[tt, rows, lanes]
            prod = do.astype(F32) * ctx[tt, rows, lanes].astype(F32)
            for h, (qi, _, _, qh, vh) in enumerate(heads):
                qt = tiles[base + qi, rows, :]
                qm = jnp.where(lane_mask(qt.shape, qh), qt, jnp.zeros_like(qt))
                qa = jnp.concatenate([qm, raug[3 * tt + 2 * g + h, rows, :]], axis=1)
                pt = jnp.exp(dot(jnp.concatenate([tiles[base + ki], kf[...]], axis=1), qa, 1, 1))
                vmask = lane_mask(do.shape, vh)
                dom = jnp.where(vmask, do, jnp.zeros_like(do))
                delta = jnp.sum(jnp.where(vmask, prod, 0.0), axis=1, keepdims=True)
                doa = jnp.concatenate([dom, pieces(-delta, do.shape).astype(BF)], axis=1)
                dst = (pt * dot(jnp.concatenate([tiles[base + vi], kf[...]], axis=1), doa, 1, 1)).astype(BF)
                dkv[1] += dot(pt.astype(BF), dom)
                dkv[0] += dot(dst, qm)
                dq_t = dq_t + dot(k_masks[h], dst)
            dq = (dq_t.T * 0.125).astype(BF)
            if g == 0:
                grads[tt, rows, 0:128] = dq
            else:
                grads[tt, rows, 384:512] = dq
            return 0

        lax.fori_loop(0, length // ROW_BLOCK, back, 0)
        if g == 0:
            grads[tt, :, 128:256] = dkv[0].astype(BF)
            grads[tt, :, 256:384] = dkv[1].astype(BF)
        else:
            grads[tt, :, 384:512] = grads[tt, :, 384:512] + pltpu.roll(dkv[0], 64, 1).astype(BF)
            grads[tt, :, 512:640] = pltpu.roll(dkv[1], 64, 1).astype(BF)

    def qkv_matmul(tt):
        low = lax.broadcasted_iota(jnp.int32, (ROW_BLOCK, 128), 1) < HD

        def run(i, _):
            rows = rows_at(i * ROW_BLOCK, ROW_BLOCK)
            g = dot(tbuf[rows, :], grads[tt, :, 0:640])
            dW[A_BLK, tt, rows, 0:512] = g[:, 0:512].astype(BF)
            kept = dW[A_BLK, tt, rows, 512:640]
            dW[A_BLK, tt, rows, 512:640] = jnp.where(low, g[:, 512:640].astype(BF), kept)
            return 0

        lax.fori_loop(0, width // ROW_BLOCK, run, 0)
        row = 10 + 2 * k + tt
        vec[pl.ds(row, 1), 0:640] = jnp.sum(grads[tt, :, 0:640].astype(F32), axis=0, keepdims=True)

    reduce_z(C_BLK, 0, sc0)
    attend_back(0, 0)
    reduce_z(C_BLK, 1, sc1)
    sb0 = reduce_two(B_BLK, 0, rb0)
    attend_back(0, 1)
    qkv_matmul(0)
    ra0 = reduce_one(A_BLK, 0)
    sb1 = reduce_two(B_BLK, 1, rb1)
    reduce_z(B_BLK, 0, sb0)
    attend_back(1, 0)
    sa0 = reduce_two(A_BLK, 0, ra0)
    reduce_z(B_BLK, 1, sb1)
    attend_back(1, 1)
    qkv_matmul(1)
    ra1 = reduce_one(A_BLK, 1)

    v_base = new("r", 8)
    me = 4 * k + t
    vrecv[pl.ds(me, 1)] = vec[...][None]
    for dev in [(2 * c + 1 - k, t)] + partners[3:]:
        send(vec, vrecv.at[me], v_base + me, dev[0], dev[1])

    rx = exchange(lambda rows: dot(grads[0, rows, 0:640], W[A_BLK, 0, :, 0:640], 1, 1)
                  + dot(grads[1, rows, 0:640], W[A_BLK, 1, :, 0:640], 1, 1), 1)
    arrive(rbuf.at[1], rx)

    for s in range(2):
        for h in range(2):
            arrive(out.at[s, pl.ds(h * piece, piece), :], out_base + 2 * s + h)
    for entry in out_sends:
        pending[:] = [e for e in pending if e is not entry]
        settle(entry)

    def finish(i, _):
        rows = rows_at(i * piece, piece)
        obuf[rows, :] = (mix[rows, :] + own[rows, :] + rbuf[1, rows, :].astype(F32)).astype(BF)
        return 0

    lax.fori_loop(0, ranks, finish, 0)
    dx_base = new("r", 4)
    tree_return(dxr, dx_base)
    reduce_z(A_BLK, 0, sa0)
    gc_out[...] = reduce_end(C_BLK)

    for j in range(1, 8):
        src = lax.rem(me + j, 8)
        arrive(vrecv.at[src], v_base + src)
    total = vrecv[0]
    for j in range(1, 8):
        total = total + vrecv[j]
    x_base = new("r", 2)
    vrecv2 = vrecv.at[8]
    vrecv3 = vrecv.at[9]
    vrecv[10] = total
    send(vrecv.at[10], vrecv2, x_base, 2 * cx + k, t)
    sa1 = reduce_two(A_BLK, 1, ra1)
    arrive(vrecv2, x_base)
    total = total + vrecv[8]
    vrecv[11] = total
    send(vrecv.at[11], vrecv3, x_base + 1, 2 * cy + k, t)
    reduce_z(A_BLK, 1, sa1)
    gb_out[...] = reduce_end(B_BLK)
    arrive(vrecv3, x_base + 1)
    vec_out[...] = total + vrecv[9]
    for s in range(2):
        for h in range(2):
            arrive(dxr.at[s, pl.ds(h * piece, piece), :], dx_base + 2 * s + h)
    ga_out[...] = reduce_end(A_BLK)
    for entry in pending:
        settle(entry)


def fused_layer(tokens, cotangent, parents, segment_ids, w_qkv, w_out, w_up, w_down, vectors):
    local, quarter, width = tokens.shape
    length = segment_ids.shape[1]
    half = length // 2
    shard = w_qkv.shape[1]
    vm = pl.BlockSpec(memory_space=pltpu.VMEM)
    anywhere = pl.BlockSpec(memory_space=pl.ANY)
    rows = list(vectors)
    sems = 192
    return pl.pallas_call(
        layer_kernel,
        name="layer",
        out_shape=(
            jax.ShapeDtypeStruct(tokens.shape, BF),
            jax.ShapeDtypeStruct(tokens.shape, BF),
            jax.ShapeDtypeStruct((shard, width), F32),
            jax.ShapeDtypeStruct((shard, width), F32),
            jax.ShapeDtypeStruct((shard, width), F32),
            jax.ShapeDtypeStruct((16, width), F32),
        ),
        in_specs=[anywhere, anywhere, vm, vm, vm, vm, anywhere, anywhere] + [vm] * len(rows),
        out_specs=(anywhere, anywhere, vm, vm, vm, vm),
        scratch_shapes=[
            pltpu.VMEM((3, 2, width, width), BF),
            pltpu.VMEM((length, width), BF),
            pltpu.VMEM((12, length, 128), BF),
            pltpu.VMEM((2, length, 256), BF),
            pltpu.VMEM((6, length, 128), BF),
            pltpu.VMEM((length, 128), BF),
            pltpu.VMEM((length, 128), BF),
            pltpu.VMEM((half, width), F32),
            pltpu.VMEM((half, 128), F32),
            pltpu.VMEM((length, width), BF),
            pltpu.VMEM((2, length, width), BF),
            pltpu.VMEM((2, length, width), BF),
            pltpu.VMEM((half, width), BF),
            pltpu.VMEM((half, width), F32),
            pltpu.VMEM((length, width), BF),
            pltpu.VMEM((length, width), BF),
            pltpu.VMEM((2, length, 256), BF),
            pltpu.VMEM((half, width), F32),
            pltpu.VMEM((2, half, width), BF),
            pltpu.VMEM((2, half, width), BF),
            pltpu.VMEM((half, width), BF),
            pltpu.VMEM((3, 2, width, width), BF),
            pltpu.VMEM((3, 2, 2, 2, shard, width), BF),
            pltpu.VMEM((3, 2, 2, shard, width), BF),
            pltpu.VMEM((3, 4, shard, width), BF),
            pltpu.VMEM((width, length), BF),
            pltpu.VMEM((2, length, 128), F32),
            pltpu.VMEM((shard, width), BF),
            pltpu.VMEM((2,) + segment_ids.shape, jnp.int32),
            pltpu.VMEM((2,) + parents.shape, jnp.int32),
            pltpu.VMEM((16, width), F32),
            pltpu.VMEM((12, 16, width), F32),
            pltpu.SemaphoreType.DMA((sems,)),
            pltpu.SemaphoreType.DMA((sems,)),
        ],
        compiler_params=pltpu.CompilerParams(collective_id=0, has_side_effects=True, vmem_limit_bytes=63 << 20),
        cost_estimate=pl.CostEstimate(flops=60 * 10**9, bytes_accessed=30 * 10**6, transcendentals=16 * 10**6),
    )(tokens, cotangent, parents, segment_ids, w_qkv, w_out, w_up, w_down, *rows)


def plane_body(tokens, parents, segment_ids, w_qkv, b_q, b_v, w_out, b_out, gain_one, shift_one,
               w_up, b_up, w_down, b_down, gain_two, shift_two, cotangent):
    out, dx, ga, gb, gc, vec = fused_layer(
        tokens, cotangent, parents, segment_ids, w_qkv.transpose(1, 0, 2), w_out, w_up, w_down.T,
        (b_q, b_v, b_out, gain_one, shift_one, b_up, b_down, gain_two, shift_two))
    blk = [ga[:, i * HD : (i + 1) * HD] for i in range(12)]
    grad_qkv = jnp.stack(
        [jnp.concatenate([blk[0], blk[1], blk[6]], 1), jnp.concatenate([blk[2], blk[3], blk[7]], 1),
         jnp.concatenate([blk[4], blk[5], blk[8]], 1)], axis=1)
    grad_out = jnp.concatenate([blk[10], blk[11], blk[9]], 1).T
    proj = vec[10:14]
    grad_bq = jnp.concatenate([proj[:, 0:128], proj[:, 384:448]], 1).reshape(-1)
    grad_bv = jnp.concatenate([proj[:, 256:384], proj[:, 512:576]], 1).reshape(-1)
    return (out, dx.astype(F32), grad_qkv, grad_bq, grad_bv, grad_out, vec[5], vec[3], vec[4],
            gb, vec[6:10].reshape(-1), gc.T, vec[2], vec[0], vec[1])


def solution(mesh):
    dp, ranks = mesh.shape["dp"], mesh.shape["tensor"]
    return jax.shard_map(
        plane_body if (dp, ranks) == (8, 4) else functools.partial(body, dp, ranks),
        mesh=mesh,
        in_specs=(P("dp", "tensor", None), P("dp", None), P("dp", None), P("dp", None, "tensor"), P(), P(),
                  P("tensor", "dp"), P(), P(), P(), P("dp", "tensor"), P(), P("tensor", "dp"), P(), P(), P(),
                  P("dp", "tensor", None)),
        out_specs=(P("dp", "tensor", None), P("dp", "tensor", None), P("dp", None, "tensor"), P(), P(),
                   P("tensor", "dp"), P(), P(), P(), P("dp", "tensor"), P(), P("tensor", "dp"), P(), P(), P()),
        check_vma=False,
    )
```

```python
import functools

import jax
import jax.numpy as jnp
from jax import lax
from jax.experimental import pallas as pl
from jax.experimental.pallas import tpu as pltpu
from jax.sharding import PartitionSpec as P

HD = 64
SEGS = 4
epsilon = 1e-12
BF = jnp.bfloat16
F32 = jnp.float32
FILL = -1e30
HALF_HEADS = ((0, 1, 2, 0, 0), (0, 1, 2, 1, 1), (3, 4, 5, 0, 1))


def dot(a, b, ca=1, cb=0):
    return lax.dot_general(a, b, (((ca,), (cb,)), ((), ())), preferred_element_type=F32)


def split3(v):
    hi = v.astype(BF).astype(F32)
    mid = (v - hi).astype(BF).astype(F32)
    low = v - hi - mid
    return hi, mid, low


def lane_mask(shape, half):
    lane = lax.broadcasted_iota(jnp.int32, shape, 1)
    return (lane < HD) if half == 0 else (lane >= HD)


def pieces(v, shape):
    lane = lax.broadcasted_iota(jnp.int32, shape, 1)
    hi, mid, low = split3(v)
    return jnp.where(lane == 4, hi, jnp.where(lane == 5, mid, jnp.where(lane == 6, low, 0.0)))


def attention_forward_kernel(x_ref, a_ref, bias_ref, rf_ref, kf_ref, tiles_ref, ctx_ref, raug_ref):
    length = x_ref.shape[0]
    block = 256
    count = length // block

    def project(i, _):
        rows = pl.ds(pl.multiple_of(i * block, block), block)
        xb = x_ref[rows, :]
        for t in range(2):
            m = dot(xb, a_ref[t, :, : 5 * 128]) + bias_ref[t][:, : 5 * 128]
            base = 6 * t
            q3 = m[:, 3 * 128 : 4 * 128]
            v3 = m[:, 4 * 128 : 5 * 128]
            tiles_ref[base, rows, :] = m[:, :128].astype(BF) * jnp.asarray(0.125, BF)
            tiles_ref[base + 1, rows, :] = m[:, 128:256].astype(BF)
            tiles_ref[base + 2, rows, :] = m[:, 256:384].astype(BF)
            tiles_ref[base + 3, rows, :] = q3.astype(BF) * jnp.asarray(0.125, BF)
            tiles_ref[base + 4, rows, :] = pltpu.roll(q3, 64, 1).astype(BF)
            tiles_ref[base + 5, rows, :] = pltpu.roll(v3, 64, 1).astype(BF)
        return 0

    lax.fori_loop(0, count, project, 0)
    ones = jnp.ones((length, 128), BF)

    for t in range(2):
        base = 6 * t

        def attend(i, _, t=t, base=base):
            rows = pl.ds(pl.multiple_of(i * block, block), block)
            rf = rf_ref[rows, :]
            parts = []
            for h, (qi, ki, vi, qh, vh) in enumerate(HALF_HEADS):
                q = tiles_ref[base + qi, rows, :]
                qm = jnp.where(lane_mask(q.shape, qh), q, jnp.zeros_like(q))
                qq = jnp.concatenate([qm, rf], axis=1)
                kk = jnp.concatenate([tiles_ref[base + ki], kf_ref[...]], axis=1)
                s = dot(qq, kk, 1, 1)
                m = jnp.max(s, axis=1, keepdims=True)
                p = jnp.exp(s - m).astype(BF)
                vv = jnp.concatenate([tiles_ref[base + vi], ones], axis=1)
                o = dot(p, vv)
                total = o[:, 128:129]
                ov = jnp.where(lane_mask((block, 128), vh), o[:, :128] / total, 0.0)
                lse = m + jnp.log(total)
                raug_ref[3 * t + h, rows, :] = rf + pieces(-lse, (block, 128)).astype(BF)
                parts.append(ov)
            ctx_ref[2 * t, rows, :] = (parts[0] + parts[1]).astype(BF)
            ctx_ref[2 * t + 1, rows, :] = parts[2].astype(BF)
            return 0

        lax.fori_loop(0, count, attend, 0)


def attention_backward_kernel(tiles_ref, ctx_ref, dctx_ref, raug_ref, kf_ref, out_ref, dk_ref, dv_ref):
    length = kf_ref.shape[0]
    block = 256
    count = length // block
    groups = ((HALF_HEADS[0], HALF_HEADS[1]), (HALF_HEADS[2],))
    for t in range(2):
        base = 6 * t
        for g, heads in enumerate(groups):
            dk_ref[...] = jnp.zeros_like(dk_ref)
            dv_ref[...] = jnp.zeros_like(dv_ref)
            ki = heads[0][1]
            vi = heads[0][2]
            k_t = tiles_ref[base + ki].astype(F32).T
            row = lax.broadcasted_iota(jnp.int32, k_t.shape, 0)
            k_masks = [
                jnp.where((row < HD) if qh == 0 else (row >= HD), k_t, 0.0).astype(BF)
                for (_, _, _, qh, _) in heads
            ]

            def back(i, _, t=t, base=base, g=g, heads=heads, k_masks=k_masks, ki=ki, vi=vi):
                rows = pl.ds(pl.multiple_of(i * block, block), block)
                dq_t = jnp.zeros((128, block), F32)
                do = dctx_ref[2 * t + g, rows, :]
                prod = do.astype(F32) * ctx_ref[2 * t + g, rows, :].astype(F32)
                for h, (qi, _, _, qh, vh) in enumerate(heads):
                    q = tiles_ref[base + qi, rows, :]
                    qm = jnp.where(lane_mask(q.shape, qh), q, jnp.zeros_like(q))
                    qa = jnp.concatenate([qm, raug_ref[3 * t + 2 * g + h, rows, :]], axis=1)
                    ka = jnp.concatenate([tiles_ref[base + ki], kf_ref[...]], axis=1)
                    pt = jnp.exp(dot(ka, qa, 1, 1))
                    vmask = lane_mask(do.shape, vh)
                    dom = jnp.where(vmask, do, jnp.zeros_like(do))
                    delta = jnp.sum(jnp.where(vmask, prod, 0.0), axis=1, keepdims=True)
                    doa = jnp.concatenate([dom, pieces(-delta, do.shape).astype(BF)], axis=1)
                    va = jnp.concatenate([tiles_ref[base + vi], kf_ref[...]], axis=1)
                    dst = (pt * dot(va, doa, 1, 1)).astype(BF)
                    dv_ref[...] += dot(pt.astype(BF), dom)
                    dk_ref[...] += dot(dst, qm)
                    dq_t = dq_t + dot(k_masks[h], dst)
                dq = dq_t.T * 0.125
                if g == 0:
                    out_ref[t, rows, 0:128] = dq.astype(BF)
                else:
                    out_ref[t, rows, 384:512] = dq.astype(BF)
                return 0

            lax.fori_loop(0, count, back, 0)
            if g == 0:
                out_ref[t, :, 128:256] = dk_ref[...].astype(BF)
                out_ref[t, :, 256:384] = dv_ref[...].astype(BF)
            else:
                out_ref[t, :, 384:512] = out_ref[t, :, 384:512] + pltpu.roll(dk_ref[...], 64, 1).astype(BF)
                out_ref[t, :, 512:640] = pltpu.roll(dv_ref[...], 64, 1).astype(BF)


def attention_forward(x, a, bias, rf, kf):
    length = x.shape[0]
    vm = pl.BlockSpec(memory_space=pltpu.VMEM)
    return pl.pallas_call(
        attention_forward_kernel,
        name="attn_fwd",
        out_shape=(
            jax.ShapeDtypeStruct((12, length, 128), BF),
            jax.ShapeDtypeStruct((4, length, 128), BF),
            jax.ShapeDtypeStruct((6, length, 128), BF),
        ),
        in_specs=[vm] * 5,
        out_specs=(vm,) * 3,
        compiler_params=pltpu.CompilerParams(vmem_limit_bytes=48 << 20),
        cost_estimate=pl.CostEstimate(flops=20 * 10**9, bytes_accessed=10 * 10**6, transcendentals=6 * 10**6),
    )(x, a, bias, rf, kf)


def attention_backward(tiles, ctx, dctx, raug, kf):
    length = kf.shape[0]
    vm = pl.BlockSpec(memory_space=pltpu.VMEM)
    return pl.pallas_call(
        attention_backward_kernel,
        name="attn_bwd",
        out_shape=jax.ShapeDtypeStruct((2, length, 640), BF),
        in_specs=[vm] * 5,
        out_specs=vm,
        scratch_shapes=[pltpu.VMEM((length, 128), F32), pltpu.VMEM((length, 128), F32)],
        compiler_params=pltpu.CompilerParams(vmem_limit_bytes=48 << 20),
        cost_estimate=pl.CostEstimate(flops=40 * 10**9, bytes_accessed=10 * 10**6, transcendentals=6 * 10**6),
    )(tiles, ctx, dctx, raug, kf)


def ancestry(parents):
    labels = jnp.arange(SEGS, dtype=jnp.int32)
    step = (parents[:, None] == labels[None, :]).astype(F32)
    reach = jnp.eye(SEGS, dtype=F32)
    total = reach
    for _ in range(SEGS - 1):
        reach = jnp.sum(reach[:, :, None] * step[None, :, :], axis=1)
        total = total + reach
    return (total > 0.5).astype(F32)


def gelu_parts(u):
    cdf = 0.5 * (1.0 + lax.erf(u * (2.0**-0.5)))
    pdf = jnp.exp(-0.5 * u * u) * ((2.0 * jnp.pi) ** -0.5)
    return u * cdf, cdf + u * pdf


def norm_parts(rows):
    center = rows - jnp.mean(rows, axis=-1, keepdims=True)
    inverse = lax.rsqrt(jnp.mean(center * center, axis=-1, keepdims=True) + epsilon)
    return center * inverse, inverse


def norm_back(grad_rows, normed, inverse, gain):
    scaled = grad_rows * gain
    return inverse * (
        scaled
        - jnp.mean(scaled, axis=-1, keepdims=True)
        - normed * jnp.mean(scaled * normed, axis=-1, keepdims=True)
    )


def body(dp, ranks, tokens, parents, segment_ids, w_qkv, b_q, b_v, w_out, b_out, gain_one, shift_one,
         w_up, b_up, w_down, b_down, gain_two, shift_two, cotangent):
    d = lax.axis_index("dp")
    ti = lax.axis_index("tensor")
    k = d % 2
    local, quarter, width = tokens.shape
    half_rows = quarter // 2
    own_rows = ranks * half_rows
    length = 2 * own_rows
    part = w_qkv.shape[2]
    hidden_part = w_up.shape[1]
    shard = w_qkv.shape[0]
    chips = dp // 2
    same_core = [[i for i in range(dp) if i % 2 == c] for c in range(2)]

    def swap(v):
        return lax.ppermute(v, "dp", [(i, i ^ 1) for i in range(dp)])

    def pick(v, index, axis=0):
        return lax.dynamic_index_in_dim(v, index, axis, keepdims=False)

    def join(own, peer, axis=0):
        return jnp.where(k == 0, jnp.stack([own, peer], axis), jnp.stack([peer, own], axis))

    def to_tree(v):
        v = v.reshape(local, 2, half_rows, width)
        mine = pick(v, k, 1)
        other = swap(pick(v, 1 - k, 1))
        trees = join(mine, other).reshape(ranks, half_rows, width)
        return lax.all_to_all(trees, "tensor", 0, 0, tiled=True).reshape(own_rows, width)

    def from_tree(v):
        v = lax.all_to_all(v.reshape(ranks, half_rows, width), "tensor", 0, 0, tiled=True)
        v = v.reshape(2, local, half_rows, width)
        other = swap(pick(v, 1 - k))
        return join(pick(v, k), other, 1).reshape(local, quarter, width)

    heads = w_qkv.reshape(shard, 3, 3, HD)
    q, kk, vv = heads[:, 0], heads[:, 1], heads[:, 2]
    out_t = w_out.T.reshape(shard, 3, HD)
    packed_a = jnp.concatenate(
        [q[:, 0], q[:, 1], kk[:, 0], kk[:, 1], vv[:, 0], vv[:, 1], q[:, 2], kk[:, 2], vv[:, 2],
         out_t[:, 2], out_t[:, 0], out_t[:, 1]], axis=1)

    def gather_weight(w):
        every = lax.all_gather(w, "tensor", axis=0, tiled=False).reshape(2, 2, shard, w.shape[1])
        mine = pick(every, k)
        other = swap(pick(every, 1 - k))
        both = join(mine, other, 1)
        full = lax.all_gather(both, "dp", axis=0, tiled=False, axis_index_groups=same_core)
        return full.transpose(1, 0, 2, 3, 4).reshape(2, chips * 2 * shard, w.shape[1])

    x_own = to_tree(tokens)
    w_a = gather_weight(packed_a)
    w_b = gather_weight(w_up)
    w_c = gather_weight(w_down.T)
    x = join(x_own, swap(x_own)).reshape(length, width)
    cot_own = to_tree(cotangent)

    seg_peer = swap(segment_ids)
    par_peer = swap(parents)
    all_seg = join(segment_ids, seg_peer).reshape(ranks, -1)
    all_par = join(parents, par_peer).reshape(ranks, -1)
    seg = pick(all_seg, ti).reshape(ranks, 2, half_rows).transpose(1, 0, 2).reshape(length)
    par = pick(all_par, ti)
    labels = jnp.arange(SEGS, dtype=jnp.int32)
    hot = (seg[:, None] == labels[None, :]).astype(F32)
    reach_rows = jnp.sum(hot[:, :, None] * ancestry(par)[None], axis=1)
    rf = jnp.concatenate([FILL * (1.0 - reach_rows), jnp.zeros((length, 124), F32)], axis=1).astype(BF)
    kf = jnp.concatenate([hot, jnp.ones((length, 3), F32), jnp.zeros((length, 121), F32)], axis=1).astype(BF)

    def half_vector(b, size):
        return lax.dynamic_slice_in_dim(b, 2 * k * size, 2 * size).reshape(2, size)

    bq = half_vector(b_q, part)
    bv = half_vector(b_v, part)
    zero64 = jnp.zeros((2, HD), F32)
    bias = jnp.concatenate(
        [bq[:, :128], jnp.zeros((2, 128), F32), bv[:, :128], bq[:, 128:], zero64, bv[:, 128:], zero64,
         jnp.zeros((2, 128), F32)], axis=1)[:, None, :]

    tiles, ctx, raug = attention_forward(x, w_a, bias, rf, kf)

    def exchange(partial):
        partial = partial.reshape(2, own_rows, width)
        received = swap(pick(partial, 1 - k).astype(BF))
        return pick(partial, k) + received.astype(F32)

    def spread_rows(v):
        return join(v, swap(v)).reshape(length, width)

    partial = 0.0
    for t in range(2):
        partial = partial + dot(ctx[2 * t + 1], w_a[t, :, 512:640], 1, 1) + dot(ctx[2 * t], w_a[t, :, 640:768], 1, 1)
    attended = exchange(partial)
    n1, r1 = norm_parts(x_own.astype(F32) + attended + b_out)
    hidden = n1 * gain_one + shift_one
    rows_low = spread_rows(hidden.astype(BF))
    up_bias = half_vector(b_up, hidden_part)
    inner = [dot(rows_low, w_b[t]) + up_bias[t] for t in range(2)]
    acts = [gelu_parts(u) for u in inner]
    activated = [a.astype(BF) for a, _ in acts]
    branch = exchange(sum(dot(activated[t], w_c[t], 1, 1) for t in range(2)))
    n2, r2 = norm_parts(hidden + branch + b_down)
    output = n2 * gain_two + shift_two
    g = cot_own.astype(F32)
    gain_two_part = jnp.sum(g * n2, axis=0)
    shift_two_part = jnp.sum(g, axis=0)
    mix_two = norm_back(g, n2, r2, gain_two)
    b_down_part = jnp.sum(mix_two, axis=0)
    two_rows = spread_rows(mix_two.astype(BF))
    d_c = [dot(two_rows, activated[t], 0, 0) for t in range(2)]
    grad_inner = [(dot(two_rows, w_c[t]) * acts[t][1]).astype(BF) for t in range(2)]
    b_up_part = jnp.concatenate([jnp.sum(v.astype(F32), axis=0) for v in grad_inner])
    d_b = [dot(rows_low, grad_inner[t], 0, 0) for t in range(2)]
    grad_hidden = mix_two + exchange(sum(dot(grad_inner[t], w_b[t], 1, 1) for t in range(2)))
    gain_one_part = jnp.sum(grad_hidden * n1, axis=0)
    shift_one_part = jnp.sum(grad_hidden, axis=0)
    mix_one = norm_back(grad_hidden, n1, r1, gain_one)
    b_out_part = jnp.sum(mix_one, axis=0)
    one_rows = spread_rows(mix_one.astype(BF))
    dctx = jnp.stack(
        [dot(one_rows, w_a[t, :, lo : lo + 128]).astype(BF) for t in range(2) for lo in (640, 512)])
    d_tiles = attention_backward(tiles, ctx, dctx, raug, kf)

    def d_a_of(t):
        qkv = dot(x, d_tiles[t], 0, 0)
        o2 = dot(one_rows, ctx[2 * t + 1], 0, 0)
        o01 = dot(one_rows, ctx[2 * t], 0, 0)
        lane = lax.broadcasted_iota(jnp.int32, o2.shape, 1)
        return jnp.concatenate([qkv[:, :512], jnp.where(lane < HD, qkv[:, 512:], o2), o01], axis=1)

    d_a = [d_a_of(t) for t in range(2)]
    lane_zero = jnp.where(jnp.arange(640) < 576, 1.0, 0.0).astype(BF)
    grad_x = exchange(sum(dot(d_tiles[t] * lane_zero, w_a[t, :, :640], 1, 1) for t in range(2)))
    input_grad = from_tree((mix_one + grad_x).astype(BF)).astype(F32)
    out = from_tree(output.astype(BF))

    def scatter_weight(pair):
        v = jnp.stack([p.astype(BF) for p in pair]).reshape(2, chips, 2, shard, width).transpose(1, 2, 0, 3, 4)
        v = v.reshape(chips * 4 * shard, width)
        v = lax.psum_scatter(v, "dp", scatter_dimension=0, tiled=True, axis_index_groups=same_core)
        v = v.reshape(2, 2, shard, width)
        other = swap(pick(v, 1 - k))
        v = join(pick(v, k), other).reshape(ranks * shard, width)
        return lax.psum_scatter(v, "tensor", scatter_dimension=0, tiled=True).astype(F32)

    g_c = scatter_weight(d_c)
    g_b = scatter_weight(d_b)
    g_a = scatter_weight(d_a)
    blk = [g_a[:, i * HD : (i + 1) * HD] for i in range(12)]
    grad_qkv = jnp.stack(
        [jnp.concatenate([blk[0], blk[1], blk[6]], 1), jnp.concatenate([blk[2], blk[3], blk[7]], 1),
         jnp.concatenate([blk[4], blk[5], blk[8]], 1)], axis=1)
    grad_out = jnp.concatenate([blk[10], blk[11], blk[9]], 1).T

    sums = jnp.sum(d_tiles.astype(F32), axis=1)
    bq_part = jnp.concatenate([sums[:, :128], sums[:, 384:448]], axis=1).reshape(-1)
    bv_part = jnp.concatenate([sums[:, 256:384], sums[:, 512:576]], axis=1).reshape(-1)

    def spread(v, size):
        return lax.dynamic_update_slice_in_dim(jnp.zeros((size,), F32), v, k * v.shape[0], 0)

    summed = lax.psum(
        (spread(bq_part, width), spread(bv_part, width), b_out_part, gain_one_part, shift_one_part,
         spread(b_up_part, b_up.shape[0]), b_down_part, gain_two_part, shift_two_part), ("dp", "tensor"))
    return (out, input_grad, grad_qkv, summed[0], summed[1], grad_out, summed[2], summed[3], summed[4],
            g_b, summed[5], g_c.T, summed[6], summed[7], summed[8])


A_BLK, B_BLK, C_BLK = 0, 1, 2
ROW_BLOCK = 256
FORWARD_BLOCK = 512
BACKWARD_BLOCK = 256


def gelu_pair(u):
    t = 1.0 / (1.0 + (0.3275911 * 2.0**-0.5) * jnp.abs(u))
    bell = jnp.exp(-0.5 * u * u)
    poly = jnp.full_like(t, 0.5 * 1.061405429)
    for coef in (-1.453152027, 1.421413741, -0.284496736, 0.254829592):
        poly = poly * t + 0.5 * coef
    tail = poly * t * bell
    cdf = jnp.where(u > 0.0, 1.0 - tail, tail)
    return u * cdf, cdf + u * (bell * ((2.0 * jnp.pi) ** -0.5))


def row_mean(v):
    return jnp.mean(v, axis=-1, keepdims=True)


def layer_kernel(tok, cot_in, par, seg, wqkv, wout, wup, wdown, bq, bv, bout, g1, s1, bup, bdown, g2, s2,
                 out, dxr, ga_out, gb_out, gc_out, vec_out,
                 W, X, tiles, ctx, raug, rf, kf, n1, r1, H, act, gp, mix, G2, G1, dctx, own,
                 sbuf, rbuf, obuf, dW, rs1, rs2, rs3, zbuf, tbuf, dkv, ash, seg_all, par_all, vec, vrecv,
                 ssem, rsem):
    row_of = {n: ref[...][None, :] for n, ref in (("bout", bout), ("g1", g1), ("s1", s1), ("bdown", bdown),
                                                  ("g2", g2), ("s2", s2))}
    d = lax.axis_index("dp")
    t = lax.axis_index("tensor")
    k = lax.rem(d, 2)
    c = d // 2
    ranks = 4
    cx = c + 1 - 2 * lax.rem(c, 2)
    cy = lax.rem(c + 2, 4)
    cd = 3 - c
    length = X.shape[0]
    half = length // 2
    piece = half // ranks
    width = X.shape[1]
    shard = ash.shape[0]
    pair = 2 * shard
    home = t // 2
    here = k * half
    there = (1 - k) * half
    counters = {"s": 0, "r": 0}
    pending = []

    def new(kind, n=1):
        base = counters[kind]
        counters[kind] = base + n
        return base

    def remote(src, dst, s, r, dd, tt):
        return pltpu.make_async_remote_copy(
            src_ref=src, dst_ref=dst, send_sem=ssem.at[s], recv_sem=rsem.at[r], device_id=(dd, tt),
            device_id_type=pl.DeviceIdType.MESH)

    def send(src, dst, r, dd, tt):
        cp = remote(src, dst, new("s"), r, dd, tt)
        cp.start()
        pending.append((None, cp))

    def send_or_copy(src, dst, r, dd, tt):
        cp = remote(src, dst, new("s"), r, dd, tt)
        mine = jnp.logical_and(dd == d, tt == t)

        @pl.when(mine)
        def _():
            pltpu.make_async_copy(src, dst, rsem.at[r]).start()

        @pl.when(jnp.logical_not(mine))
        def _():
            cp.start()

        pending.append((mine, cp))

    def settle(entry):
        mine, cp = entry
        if mine is None:
            cp.wait_send()
        else:
            @pl.when(jnp.logical_not(mine))
            def _():
                cp.wait_send()

    def arrive(dst, r):
        pltpu.make_async_copy(dst, dst, rsem.at[r]).wait()

    def rows_at(start, n, align=None):
        return pl.ds(pl.multiple_of(start, align or n), n)

    barrier = pltpu.get_barrier_semaphore()
    partners = [(2 * c + 1 - k, t), (2 * cx + k, t), (2 * cy + k, t)]
    for j in range(1, ranks):
        for core in range(2):
            partners.append((2 * c + core, lax.rem(t + j, ranks)))
    for dev in partners:
        pl.semaphore_signal(barrier, inc=1, device_id=dev, device_id_type=pl.DeviceIdType.MESH)

    q_all = wqkv[0].astype(F32)
    k_all = wqkv[1].astype(F32)
    v_all = wqkv[2].astype(F32)
    o_all = wout[...].astype(F32).T
    ash[:, 0:128] = q_all[:, :128].astype(BF)
    ash[:, 128:256] = k_all[:, :128].astype(BF)
    ash[:, 256:384] = v_all[:, :128].astype(BF)
    ash[:, 384:512] = jnp.concatenate([q_all[:, 128:], k_all[:, 128:]], axis=1).astype(BF)
    ash[:, 512:640] = jnp.concatenate([v_all[:, 128:], o_all[:, 128:]], axis=1).astype(BF)
    ash[:, 640:768] = o_all[:, :128].astype(BF)
    pl.semaphore_wait(barrier, len(partners))

    slot = lax.rem(t, 2) * 2 + k
    step = 1 - 2 * k

    def shard_rows(b, tt, kk):
        return W.at[b, tt, rows_at(c * pair + kk * shard, shard), :]

    def send_if(wanted, src, dst, r, dd, tt):
        cp = remote(src, dst, new("s"), r, dd, tt)

        @pl.when(wanted)
        def _():
            cp.start()

        pending.append((jnp.logical_not(wanted), cp))

    def z_own(b, src):
        base = new("r", 4)
        dst = shard_rows(b, lax.rem(t, 2), k)
        for j in (1, -1, 2, -2):
            inside = jnp.logical_and(t + j >= 0, t + j < ranks)
            send_if(inside, src, dst, base + slot, 2 * c + home, lax.rem(t + j + ranks, ranks))
        send_or_copy(src, dst, base + slot, 2 * c + home, t)
        return base

    def z_near(b, base):
        for kk in range(2):
            arrive(shard_rows(b, 1 - k, kk), base + 2 * (1 - k) + kk)

    def z_far(b, base):
        for kk in range(2):
            rows = shard_rows(b, k, kk)
            arrive(rows, base + 2 * k + kk)
            send_if(t == 2 - k, rows, rows, base + 2 * k + kk, d, lax.rem(t + step + ranks, ranks))

    def plane_rows(b, far, chip):
        return W.at[b, k if far else 1 - k, rows_at(chip * pair, pair), :]

    def plane_send(b):
        near, far = new("r", 3), new("r", 3)
        n_rows, f_rows = plane_rows(b, False, c), plane_rows(b, True, c)
        send(n_rows, n_rows, near, 2 * cx + k, t)
        send(f_rows, f_rows, far + 1, 2 * cy + k, t)
        send(n_rows, n_rows, near + 1, 2 * cy + k, t)
        send(f_rows, f_rows, far, 2 * cx + k, t)
        return near, far

    def plane_forward(b, near, far):
        rows = plane_rows(b, False, cx)
        arrive(rows, near)
        send(rows, rows, near + 2, 2 * cy + k, t)
        rows = plane_rows(b, True, cy)
        arrive(rows, far + 1)
        send(rows, rows, far + 2, 2 * cx + k, t)

    def plane_wait(b, near, far):
        arrive(plane_rows(b, False, cy), near + 1)
        arrive(plane_rows(b, True, cx), far)
        arrive(plane_rows(b, False, cd), near + 2)
        arrive(plane_rows(b, True, cd), far + 2)

    seg_base = new("r", 2)
    for i, (src, dst) in enumerate(((seg, seg_all), (par, par_all))):
        send(src, dst.at[k], seg_base + i, 2 * c + 1 - k, t)
        dst[pl.ds(k, 1)] = src[...][None]
    def tree_send(src, dst):
        base = new("r", 4)
        for s in range(2):
            for h in range(2):
                send_or_copy(src.at[s, pl.ds(h * piece, piece), :], dst(h), base + t, 2 * c + h, 2 * k + s)
        return base

    za = z_own(A_BLK, ash)
    zb = z_own(B_BLK, wup)
    tok_base = tree_send(tok, lambda h: X.at[rows_at(h * half + t * piece, piece), :])

    arrive(seg_all.at[1 - k], seg_base)
    arrive(par_all.at[1 - k], seg_base + 1)
    lane1 = lax.broadcasted_iota(jnp.int32, (1, 128), 1)
    both = par_all[pl.ds(home, 1)][0]
    second = lax.rem(t, 2) == 1
    parents = jnp.where(second, both[1:2, :], both[0:1, :])
    par_of = [jnp.broadcast_to(parents[:, j : j + 1], (1, 128)) for j in range(SEGS)]
    reach_rows = []
    for s in range(SEGS):
        now = jnp.full((1, 128), s, jnp.int32)
        seen = lane1 == s
        for _ in range(SEGS - 1):
            now = functools.reduce(lambda acc, j: jnp.where(now == j, par_of[j], acc), range(SEGS), now)
            seen = jnp.logical_or(seen, lane1 == now)
        reach_rows.append(jnp.where(lane1 < SEGS, jnp.where(seen, 0.0, FILL), 0.0))
    lane_f = lax.broadcasted_iota(jnp.int32, (piece, 128), 1).astype(F32)
    for h in range(2):
        for q in range(ranks):
            both = seg_all[pl.ds(home, 1), :, pl.ds((2 * q + h) * piece, piece)][0].astype(F32)
            part = jnp.where(second, both[1:2, :], both[0:1, :])
            segs = jnp.broadcast_to(part, (piece, piece)).T
            rows = pl.ds(h * half + q * piece, piece)
            table = jnp.zeros((piece, 128), F32)
            for s in range(SEGS):
                table = jnp.where(segs == s, jnp.broadcast_to(reach_rows[s], (piece, 128)), table)
            rf[rows, :] = table.astype(BF)
            hot = jnp.where(lane_f < SEGS, jnp.where(segs == lane_f, 1.0, 0.0), jnp.where(lane_f < SEGS + 3, 1.0, 0.0))
            kf[rows, :] = hot.astype(BF)

    z_near(A_BLK, za)
    z_far(A_BLK, za)
    pa = plane_send(A_BLK)
    z_near(B_BLK, zb)
    z_far(B_BLK, zb)
    plane_forward(A_BLK, *pa)
    pb = plane_send(B_BLK)
    zc = z_own(C_BLK, wdown)
    fwd_base = new("r", 4)
    for j in range(ranks):
        q = lax.rem(t + j, ranks)
        mine = X.at[rows_at(here + q * piece, piece), :]
        arrive(mine, tok_base + q)
        send(mine, mine, fwd_base + q, 2 * c + 1 - k, t)
    plane_wait(A_BLK, *pa)

    def half_lanes(ref):
        row = ref[...][None, :]
        return jnp.where(k == 0, row[:, : width // 2], row[:, width // 2 :])

    bq2, bv2 = half_lanes(bq), half_lanes(bv)
    zero64 = jnp.zeros((1, HD), F32)
    biases = []
    for tt in range(2):
        lo = 192 * tt
        biases.append((bq2[:, lo : lo + 128], bv2[:, lo : lo + 128],
                       jnp.concatenate([bq2[:, lo + 128 : lo + 192], zero64], axis=1),
                       jnp.concatenate([bv2[:, lo + 128 : lo + 192], zero64], axis=1)))
    eighth = jnp.asarray(0.125, BF)

    def project(start):
        def run(i, _):
            rows = rows_at(start + i * ROW_BLOCK, ROW_BLOCK)
            xb = X[rows, :]
            for tt in range(2):
                m = dot(xb, W[A_BLK, tt, :, 0:640])
                b_q01, b_v01, b_q2, b_v2 = biases[tt]
                base = 6 * tt
                q3 = m[:, 384:512] + b_q2
                v3 = m[:, 512:640] + b_v2
                tiles[base, rows, :] = (m[:, 0:128] + b_q01).astype(BF) * eighth
                tiles[base + 1, rows, :] = m[:, 128:256].astype(BF)
                tiles[base + 2, rows, :] = (m[:, 256:384] + b_v01).astype(BF)
                tiles[base + 3, rows, :] = q3.astype(BF) * eighth
                tiles[base + 4, rows, :] = pltpu.roll(q3, 64, 1).astype(BF)
                tiles[base + 5, rows, :] = pltpu.roll(v3, 64, 1).astype(BF)
            return 0

        lax.fori_loop(0, half // ROW_BLOCK, run, 0)

    project(here)
    plane_forward(B_BLK, *pb)
    for q in range(ranks):
        arrive(X.at[rows_at(there + q * piece, piece), :], fwd_base + q)
    project(there)

    ones = jnp.ones((length, 128), BF)

    def attend_all(tt, lo, hi):
        base = 6 * tt

        def attend(i, _):
            rows = rows_at(i * FORWARD_BLOCK, FORWARD_BLOCK)
            rfb = rf[rows, :]
            parts = []

            def score(h):
                qi, ki, _, qh, _ = HALF_HEADS[h]
                qt = tiles[base + qi, rows, :]
                qm = jnp.where(lane_mask(qt.shape, qh), qt, jnp.zeros_like(qt))
                return dot(jnp.concatenate([qm, rfb], axis=1), jnp.concatenate([tiles[base + ki], kf[...]], axis=1), 1, 1)

            def soften(s):
                top = jnp.max(s, axis=1, keepdims=True)
                return top, jnp.exp(s - top).astype(BF)

            def mix_values(h, top, p):
                vi, vh = HALF_HEADS[h][2], HALF_HEADS[h][4]
                o = dot(p, jnp.concatenate([tiles[base + vi], ones], axis=1))
                total = o[:, 128:129]
                parts.append(jnp.where(lane_mask((FORWARD_BLOCK, 128), vh), o[:, :128] / total, 0.0))
                lse = top + jnp.log(total)
                raug[3 * tt + h, rows, :] = rfb + pieces(-lse, (FORWARD_BLOCK, 128)).astype(BF)

            s0 = score(0)
            s1 = score(1)
            e0 = soften(s0)
            s2 = score(2)
            mix_values(0, *e0)
            e1 = soften(s1)
            mix_values(1, *e1)
            e2 = soften(s2)
            mix_values(2, *e2)
            ctx[tt, rows, 0:128] = parts[2].astype(BF)
            ctx[tt, rows, 128:256] = (parts[0] + parts[1]).astype(BF)
            return 0

        lax.fori_loop(lo, hi, attend, 0)

    blocks = length // FORWARD_BLOCK
    attend_all(0, 0, blocks // 2)
    z_near(C_BLK, zc)
    z_far(C_BLK, zc)
    pc = plane_send(C_BLK)
    cot_base = tree_send(cot_in, lambda h: dW.at[A_BLK, 0, rows_at(t * piece, piece), :])
    attend_all(0, blocks // 2, blocks)
    attend_all(1, 0, blocks)
    plane_forward(C_BLK, *pc)

    exchanged = []

    def exchange(compute, index):
        blocks = half // ROW_BLOCK
        r_base, s_base = new("r", blocks), new("s", blocks)
        if len(exchanged) >= 2:
            for entry in exchanged[-2]:
                pending[:] = [e for e in pending if e is not entry]
                settle(entry)

        def copy_of(i):
            rows = rows_at(i * ROW_BLOCK, ROW_BLOCK)
            return remote(sbuf.at[index, rows, :], rbuf.at[index, rows, :], s_base + i, r_base + i, 2 * c + 1 - k, t)

        def give(i, _):
            sbuf[index, rows_at(i * ROW_BLOCK, ROW_BLOCK), :] = compute(
                rows_at(there + i * ROW_BLOCK, ROW_BLOCK)).astype(BF)
            copy_of(i).start()
            return 0

        lax.fori_loop(0, blocks, give, 0)
        entries = [(None, copy_of(i)) for i in range(blocks)]
        exchanged.append(entries)
        pending.extend(entries)

        def keep(i, _):
            own[rows_at(i * ROW_BLOCK, ROW_BLOCK), :] = compute(rows_at(here + i * ROW_BLOCK, ROW_BLOCK))
            return 0

        lax.fori_loop(0, blocks, keep, 0)

        def ready(i):
            per = ROW_BLOCK // piece

            @pl.when(lax.rem(i, per) == 0)
            def _():
                arrive(rbuf.at[index, rows_at(i * piece, ROW_BLOCK, piece), :], r_base + i // per)

        return ready

    def over_pieces(step, buffer):
        base = new("r", ranks)
        s_base = new("s", ranks)
        def one(i, _):
            rows = rows_at(i * piece, piece)
            full = rows_at(here + i * piece, piece)
            buffer[full, :] = step(rows, i)
            remote(buffer.at[full, :], buffer.at[full, :], s_base + i, base + i, 2 * c + 1 - k, t).start()
            return 0
        lax.fori_loop(0, ranks, one, 0)
        for i in range(ranks):
            full = rows_at(here + i * piece, piece)
            pending.append((None, remote(buffer.at[full, :], buffer.at[full, :], s_base + i, base + i, 2 * c + 1 - k, t)))
        return base

    def wait_pieces(buffer, base):
        for i in range(ranks):
            arrive(buffer.at[rows_at(there + i * piece, piece), :], base + i)

    ra = exchange(lambda rows: dot(ctx[0, rows, :], W[A_BLK, 0, :, 512:768], 1, 1)
                  + dot(ctx[1, rows, :], W[A_BLK, 1, :, 512:768], 1, 1), 0)

    def norm_one(rows, i):
        ra(i)
        x_rows = X[rows_at(here + rows.start, piece), :].astype(F32)
        z = x_rows + own[rows, :] + rbuf[0, rows, :].astype(F32) + row_of['bout']
        center = z - row_mean(z)
        inverse = lax.rsqrt(row_mean(center * center) + epsilon)
        normed = center * inverse
        n1[rows, :] = normed
        r1[rows, :] = jnp.broadcast_to(inverse, (piece, 128))
        return (normed * row_of['g1'] + row_of['s1']).astype(BF)

    hb = over_pieces(norm_one, H)
    plane_wait(B_BLK, *pb)

    up_row = bup[...][None, :]
    up_bias = [jnp.where(k == 0, up_row[:, tt * width : (tt + 1) * width],
                         up_row[:, (2 + tt) * width : (3 + tt) * width]) for tt in range(2)]

    def up(start):
        def run(i, _):
            rows = rows_at(start + i * ROW_BLOCK, ROW_BLOCK)
            for tt in range(2):
                bias = up_bias[tt]
                value, slope = gelu_pair(dot(H[rows, :], W[B_BLK, tt]) + bias)
                act[tt, rows, :] = value.astype(BF)
                gp[tt, rows, :] = slope.astype(BF)
            return 0

        lax.fori_loop(0, half // ROW_BLOCK, run, 0)

    up(here)
    wait_pieces(H, hb)
    up(there)
    plane_wait(C_BLK, *pc)
    rb = exchange(lambda rows: dot(act[0, rows, :], W[C_BLK, 0], 1, 1) + dot(act[1, rows, :], W[C_BLK, 1], 1, 1), 1)
    for q in range(ranks):
        arrive(dW.at[A_BLK, 0, pl.ds(q * piece, piece), :], cot_base + q)
    def piece_back(i, target, r_base, s_base):
        return remote(obuf.at[rows_at(i * piece, piece), :],
                      target.at[lax.rem(t, 2), rows_at(k * piece, piece), :],
                      s_base + i, r_base + lax.rem(t, 2) * 2 + k, 2 * c + home, i)

    def give_back(i, target, r_base, s_base):
        cp = piece_back(i, target, r_base, s_base)
        mine = jnp.logical_and(home == k, t == i)

        @pl.when(mine)
        def _():
            pltpu.make_async_copy(obuf.at[rows_at(i * piece, piece), :],
                                  target.at[lax.rem(t, 2), rows_at(k * piece, piece), :],
                                  rsem.at[r_base + lax.rem(t, 2) * 2 + k]).start()

        @pl.when(jnp.logical_not(mine))
        def _():
            cp.start()

    def given(target, r_base, s_base):
        return [(jnp.logical_and(home == k, t == i), piece_back(i, target, r_base, s_base)) for i in range(ranks)]

    out_base, out_sends = new("r", 4), new("s", ranks)
    vec[...] = jnp.zeros_like(vec)

    def col_add(row, v):
        vec[row : row + 1, :] = vec[row : row + 1, :] + jnp.sum(v, axis=0, keepdims=True)

    def norm_two(rows, i):
        rb(i)
        z = n1[rows, :] * row_of['g1'] + row_of['s1'] + own[rows, :] + rbuf[1, rows, :].astype(F32) + row_of['bdown']
        center = z - row_mean(z)
        inverse = lax.rsqrt(row_mean(center * center) + epsilon)
        normed = center * inverse
        obuf[rows, :] = (normed * row_of['g2'] + row_of['s2']).astype(BF)
        give_back(i, out, out_base, out_sends)
        g = dW[A_BLK, 0, rows, :].astype(F32)
        col_add(0, g * normed)
        col_add(1, g)
        gg = g * row_of['g2']
        back = inverse * (gg - row_mean(gg) - normed * row_mean(gg * normed))
        col_add(2, back)
        mix[rows, :] = back
        return back.astype(BF)

    g2b = over_pieces(norm_two, G2)
    out_entries = given(out, out_base, out_sends)
    pending.extend(out_entries)

    def transpose_into(src):
        def run(i, _):
            rows = rows_at(i * piece, piece)
            tbuf[:, rows] = src[rows, :].astype(F32).T.astype(BF)
            return 0

        lax.fori_loop(0, length // piece, run, 0)

    def grad_rows(part, chip, kk):
        b, tt, lo, hi = part
        return dW.at[b, tt, rows_at(chip * pair + kk * shard, shard), lo:hi]

    def reduce_one(part):
        b, tt, lo, hi = part
        base = new("r", 4)
        for i, chip in enumerate((cd, cy)):
            send(grad_rows(part, chip, 0), rs1.at[b, tt, 0, i, :, lo:hi], base + i, 2 * cy + k, t)
        for i, chip in enumerate((cd, cx)):
            send(grad_rows(part, chip, 1), rs1.at[b, tt, 1, i, :, lo:hi], base + 2 + i, 2 * cx + k, t)
        return part, base

    def add_rows(part, chip, kk, received):
        b, tt, lo, hi = part
        rows = rows_at(chip * pair + kk * shard, shard)
        dW[b, tt, rows, lo:hi] = (dW[b, tt, rows, lo:hi].astype(F32) + received.astype(F32)).astype(BF)

    def reduce_two(state):
        part, base = state
        b, tt, lo, hi = part
        nxt = new("r", 2)
        for kk, other in ((0, cx), (1, cy)):
            arrive(rs1.at[b, tt, kk, 0, :, lo:hi], base + 2 * kk)
            add_rows(part, other, kk, rs1[b, tt, kk, 0, :, lo:hi])
            send(grad_rows(part, other, kk), rs2.at[b, tt, kk, :, lo:hi], nxt + kk, 2 * other + k, t)
        for kk in range(2):
            arrive(rs1.at[b, tt, kk, 1, :, lo:hi], base + 2 * kk + 1)
            add_rows(part, c, kk, rs1[b, tt, kk, 1, :, lo:hi])
        return part, nxt

    outer = t == (ranks - 1) * (1 - k)
    joiner = t == 1 + (1 - k)
    inward = t + 2 * k - 1
    z_bases = {}

    def reduce_join(state):
        part, nxt = state
        b, tt, lo, hi = part
        base = new("r", 2)
        for kk in range(2):
            arrive(rs2.at[b, tt, kk, :, lo:hi], nxt + kk)
            add_rows(part, c, kk, rs2[b, tt, kk, :, lo:hi])
            send_if(outer, grad_rows(part, c, kk), rs3.at[b, tt, kk, :, lo:hi], base + kk, d,
                    lax.rem(inward + ranks, ranks))
        return part, base

    def reduce_z(state):
        part, base = state
        b, tt, lo, hi = part
        if (b, lo) not in z_bases:
            z_bases[(b, lo)] = new("r", 3)
        z_base = z_bases[(b, lo)]
        for kk in range(2):
            @pl.when(joiner)
            def _(kk=kk):
                arrive(rs3.at[b, tt, kk, :, lo:hi], base + kk)
                add_rows(part, c, kk, rs3[b, tt, kk, :, lo:hi])

            from_slot = lax.rem(t - k + ranks, ranks)
            target = zbuf.at[b, jnp.minimum(from_slot, 2), :, lo:hi]
            cp = remote(grad_rows(part, c, kk), target, new("s"), z_base + jnp.minimum(from_slot, 2),
                        2 * c + kk, 2 * k + tt)
            mine = jnp.logical_and(kk == k, t == 2 * k + tt)

            @pl.when(mine)
            def _(kk=kk):
                pltpu.make_async_copy(grad_rows(part, c, kk), target,
                                      rsem.at[z_base + jnp.minimum(from_slot, 2)]).start()

            away = jnp.logical_and(jnp.logical_not(mine), jnp.logical_not(outer))

            @pl.when(away)
            def _(cp=cp):
                cp.start()

            pending.append((jnp.logical_not(away), cp))

    def reduce_end(b):
        for (blk, lo), base in z_bases.items():
            if blk == b:
                hi = lo + (width if (b, width // 2) not in z_bases else width // 2)
                for q in range(3):
                    arrive(zbuf.at[b, q, :, lo:hi], base + q)
        total = zbuf[b, 0].astype(F32)
        for q in range(1, 3):
            total = total + zbuf[b, q].astype(F32)
        return total

    def grad_matmul(b, tt, right):
        def run(i, _):
            rows = rows_at(i * ROW_BLOCK, ROW_BLOCK)
            dW[b, tt, rows, :] = dot(tbuf[rows, :], right[tt]).astype(BF)
            return 0

        lax.fori_loop(0, width // ROW_BLOCK, run, 0)

    wait_pieces(G2, g2b)
    transpose_into(G2)
    grad_matmul(C_BLK, 0, act)
    rc0 = reduce_one((C_BLK, 0, 0, width))
    grad_matmul(C_BLK, 1, act)
    rc1 = reduce_one((C_BLK, 1, 0, width))

    def back_up(i, _):
        rows = rows_at(i * ROW_BLOCK, ROW_BLOCK)
        for tt in range(2):
            gi = (dot(G2[rows, :], W[C_BLK, tt]) * gp[tt, rows, :].astype(F32)).astype(BF)
            gp[tt, rows, :] = gi
            row = 6 + 2 * k + tt
            vec[pl.ds(row, 1), :] = vec[pl.ds(row, 1), :] + jnp.sum(gi.astype(F32), axis=0, keepdims=True)
        return 0

    lax.fori_loop(0, length // ROW_BLOCK, back_up, 0)
    rh = exchange(lambda rows: dot(gp[0, rows, :], W[B_BLK, 0], 1, 1) + dot(gp[1, rows, :], W[B_BLK, 1], 1, 1), 0)
    transpose_into(H)

    def norm_one_back(rows, i):
        rh(i)
        grad = mix[rows, :] + own[rows, :] + rbuf[0, rows, :].astype(F32)
        normed = n1[rows, :]
        col_add(3, grad * normed)
        col_add(4, grad)
        hh = grad * row_of['g1']
        back = r1[rows, 0:1] * (hh - row_mean(hh) - normed * row_mean(hh * normed))
        col_add(5, back)
        mix[rows, :] = back
        return back.astype(BF)

    g1b = over_pieces(norm_one_back, G1)
    grad_matmul(B_BLK, 0, gp)
    sc0 = reduce_two(rc0)
    rb0 = reduce_one((B_BLK, 0, 0, width))
    grad_matmul(B_BLK, 1, gp)
    sc1 = reduce_two(rc1)
    rb1 = reduce_one((B_BLK, 1, 0, width))
    wait_pieces(G1, g1b)

    def back_context(i, _):
        rows = rows_at(i * ROW_BLOCK, ROW_BLOCK)
        for tt in range(2):
            dctx[tt, rows, :] = dot(G1[rows, :], W[A_BLK, tt, :, 512:768]).astype(BF)
        return 0

    lax.fori_loop(0, length // ROW_BLOCK, back_context, 0)
    transpose_into(G1)

    def out_matmul(i, _):
        rows = rows_at(i * ROW_BLOCK, ROW_BLOCK)
        for tt in range(2):
            dW[A_BLK, tt, rows, 512:768] = dot(tbuf[rows, :], ctx[tt]).astype(BF)
        return 0

    lax.fori_loop(0, width // ROW_BLOCK, out_matmul, 0)
    transpose_into(X)

    grads = act

    def attend_back(tt, g, lo=0, hi=length // BACKWARD_BLOCK):
        base = 6 * tt
        heads = HALF_HEADS[0:2] if g == 0 else HALF_HEADS[2:3]
        lanes = slice(128, 256) if g == 0 else slice(0, 128)
        if lo == 0:
            dkv[...] = jnp.zeros_like(dkv)
        ki, vi = heads[0][1], heads[0][2]
        k_t = tiles[base + ki].astype(F32).T
        row = lax.broadcasted_iota(jnp.int32, k_t.shape, 0)
        k_masks = [jnp.where((row < HD) if hd[3] == 0 else (row >= HD), k_t, 0.0).astype(BF) for hd in heads]

        def back(i, _):
            rows = rows_at(i * BACKWARD_BLOCK, BACKWARD_BLOCK)
            dq_t = jnp.zeros((128, BACKWARD_BLOCK), F32)
            do = dctx[tt, rows, lanes]
            prod = do.astype(F32) * ctx[tt, rows, lanes].astype(F32)
            for h, (qi, _, _, qh, vh) in enumerate(heads):
                qt = tiles[base + qi, rows, :]
                qm = jnp.where(lane_mask(qt.shape, qh), qt, jnp.zeros_like(qt))
                qa = jnp.concatenate([qm, raug[3 * tt + 2 * g + h, rows, :]], axis=1)
                pt = jnp.exp(dot(jnp.concatenate([tiles[base + ki], kf[...]], axis=1), qa, 1, 1))
                vmask = lane_mask(do.shape, vh)
                dom = jnp.where(vmask, do, jnp.zeros_like(do))
                delta = jnp.sum(jnp.where(vmask, prod, 0.0), axis=1, keepdims=True)
                doa = jnp.concatenate([dom, pieces(-delta, do.shape).astype(BF)], axis=1)
                dst = (pt * dot(jnp.concatenate([tiles[base + vi], kf[...]], axis=1), doa, 1, 1)).astype(BF)
                dkv[1] += dot(pt.astype(BF), dom)
                dkv[0] += dot(dst, qm)
                dq_t = dq_t + dot(k_masks[h], dst)
            dq = (dq_t.T * 0.125).astype(BF)
            if g == 0:
                grads[tt, rows, 0:128] = dq
            else:
                grads[tt, rows, 384:512] = dq
            return 0

        lax.fori_loop(lo, hi, back, 0)
        if hi < length // BACKWARD_BLOCK:
            return
        if g == 0:
            grads[tt, :, 128:256] = dkv[0].astype(BF)
            grads[tt, :, 256:384] = dkv[1].astype(BF)
        else:
            grads[tt, :, 384:512] = grads[tt, :, 384:512] + pltpu.roll(dkv[0], 64, 1).astype(BF)
            grads[tt, :, 512:640] = pltpu.roll(dkv[1], 64, 1).astype(BF)

    mid = width // 2

    def qkv_matmul(tt, part):
        low = lax.broadcasted_iota(jnp.int32, (ROW_BLOCK, 128), 1) < HD

        def run(i, _):
            rows = rows_at(i * ROW_BLOCK, ROW_BLOCK)
            if part == 0:
                dW[A_BLK, tt, rows, 0:384] = dot(tbuf[rows, :], grads[tt, :, 0:384]).astype(BF)
            else:
                g = dot(tbuf[rows, :], grads[tt, :, 384:640]).astype(BF)
                dW[A_BLK, tt, rows, 384:512] = g[:, 0:128]
                kept = dW[A_BLK, tt, rows, 512:640]
                dW[A_BLK, tt, rows, 512:640] = jnp.where(low, g[:, 128:256], kept)
            return 0

        lax.fori_loop(0, width // ROW_BLOCK, run, 0)
        row = 10 + 2 * k + tt
        lanes = slice(0, 384) if part == 0 else slice(384, 640)
        vec[pl.ds(row, 1), lanes] = jnp.sum(grads[tt, :, lanes].astype(F32), axis=0, keepdims=True)
        return reduce_one((A_BLK, tt, part * mid, part * mid + mid))

    blocks = length // BACKWARD_BLOCK
    attend_back(0, 0, 0, blocks // 2)
    jc0 = reduce_join(sc0)
    jc1 = reduce_join(sc1)
    attend_back(0, 0, blocks // 2, blocks)
    ra00 = qkv_matmul(0, 0)
    sb0 = reduce_two(rb0)
    reduce_z(jc0)
    reduce_z(jc1)
    attend_back(0, 1)
    ra01 = qkv_matmul(0, 1)
    sb1 = reduce_two(rb1)
    attend_back(1, 0, 0, blocks // 2)
    jb0 = reduce_join(sb0)
    sa00 = reduce_two(ra00)
    attend_back(1, 0, blocks // 2, blocks)
    ra10 = qkv_matmul(1, 0)
    jb1 = reduce_join(sb1)
    reduce_z(jb0)
    sa01 = reduce_two(ra01)
    attend_back(1, 1)
    ra11 = qkv_matmul(1, 1)
    reduce_z(jb1)

    v_base = new("r", 8)
    me = 4 * k + t
    vrecv[pl.ds(me, 1)] = vec[...][None]
    for dev in [(2 * c + 1 - k, t)] + partners[3:]:
        send(vec, vrecv.at[me], v_base + me, dev[0], dev[1])

    rx = exchange(lambda rows: dot(grads[0, rows, 0:640], W[A_BLK, 0, :, 0:640], 1, 1)
                  + dot(grads[1, rows, 0:640], W[A_BLK, 1, :, 0:640], 1, 1), 1)
    for s in range(2):
        for h in range(2):
            arrive(out.at[s, pl.ds(h * piece, piece), :], out_base + 2 * s + h)
    for entry in out_entries:
        pending[:] = [e for e in pending if e is not entry]
        settle(entry)
    dx_base, dx_sends = new("r", 4), new("s", ranks)

    def finish(i, _):
        rx(i)
        rows = rows_at(i * piece, piece)
        obuf[rows, :] = (mix[rows, :] + own[rows, :] + rbuf[1, rows, :].astype(F32)).astype(BF)
        give_back(i, dxr, dx_base, dx_sends)
        return 0

    lax.fori_loop(0, ranks, finish, 0)
    pending.extend(given(dxr, dx_base, dx_sends))
    ja00 = reduce_join(sa00)
    ja01 = reduce_join(sa01)
    sa10 = reduce_two(ra10)
    reduce_z(ja00)
    reduce_z(ja01)
    sa11 = reduce_two(ra11)
    ja10 = reduce_join(sa10)
    reduce_z(ja10)
    ja11 = reduce_join(sa11)

    for j in range(1, 8):
        src = lax.rem(me + j, 8)
        arrive(vrecv.at[src], v_base + src)
    total = vrecv[0]
    for j in range(1, 8):
        total = total + vrecv[j]
    x_base = new("r", 2)
    vrecv2 = vrecv.at[8]
    vrecv3 = vrecv.at[9]
    vrecv[10] = total
    send(vrecv.at[10], vrecv2, x_base, 2 * cx + k, t)
    gc_out[...] = reduce_end(C_BLK)
    reduce_z(ja11)
    arrive(vrecv2, x_base)
    total = total + vrecv[8]
    vrecv[11] = total
    send(vrecv.at[11], vrecv3, x_base + 1, 2 * cy + k, t)
    gb_out[...] = reduce_end(B_BLK)
    arrive(vrecv3, x_base + 1)
    vec_out[...] = total + vrecv[9]
    for s in range(2):
        for h in range(2):
            arrive(dxr.at[s, pl.ds(h * piece, piece), :], dx_base + 2 * s + h)
    ga_out[...] = reduce_end(A_BLK)
    for entry in pending:
        settle(entry)


def fused_layer(tokens, cotangent, parents, segment_ids, w_qkv, w_out, w_up, w_down, vectors):
    local, quarter, width = tokens.shape
    length = segment_ids.shape[1]
    half = length // 2
    shard = w_qkv.shape[1]
    vm = pl.BlockSpec(memory_space=pltpu.VMEM)
    anywhere = pl.BlockSpec(memory_space=pl.ANY)
    rows = list(vectors)
    sems = 224
    return pl.pallas_call(
        layer_kernel,
        name="layer",
        out_shape=(
            jax.ShapeDtypeStruct(tokens.shape, BF),
            jax.ShapeDtypeStruct(tokens.shape, BF),
            jax.ShapeDtypeStruct((shard, width), F32),
            jax.ShapeDtypeStruct((shard, width), F32),
            jax.ShapeDtypeStruct((shard, width), F32),
            jax.ShapeDtypeStruct((16, width), F32),
        ),
        in_specs=[anywhere, anywhere, vm, vm, vm, vm, anywhere, anywhere] + [vm] * len(rows),
        out_specs=(anywhere, anywhere, vm, vm, vm, vm),
        scratch_shapes=[
            pltpu.VMEM((3, 2, width, width), BF),
            pltpu.VMEM((length, width), BF),
            pltpu.VMEM((12, length, 128), BF),
            pltpu.VMEM((2, length, 256), BF),
            pltpu.VMEM((6, length, 128), BF),
            pltpu.VMEM((length, 128), BF),
            pltpu.VMEM((length, 128), BF),
            pltpu.VMEM((half, width), F32),
            pltpu.VMEM((half, 128), F32),
            pltpu.VMEM((length, width), BF),
            pltpu.VMEM((2, length, width), BF),
            pltpu.VMEM((2, length, width), BF),
            pltpu.VMEM((half, width), F32),
            pltpu.VMEM((length, width), BF),
            pltpu.VMEM((length, width), BF),
            pltpu.VMEM((2, length, 256), BF),
            pltpu.VMEM((half, width), F32),
            pltpu.VMEM((2, half, width), BF),
            pltpu.VMEM((2, half, width), BF),
            pltpu.VMEM((half, width), BF),
            pltpu.VMEM((3, 2, width, width), BF),
            pltpu.VMEM((3, 2, 2, 2, shard, width), BF),
            pltpu.VMEM((3, 2, 2, shard, width), BF),
            pltpu.VMEM((3, 2, 2, shard, width), BF),
            pltpu.VMEM((3, 3, shard, width), BF),
            pltpu.VMEM((width, length), BF),
            pltpu.VMEM((2, length, 128), F32),
            pltpu.VMEM((shard, width), BF),
            pltpu.VMEM((2,) + segment_ids.shape, jnp.int32),
            pltpu.VMEM((2,) + parents.shape, jnp.int32),
            pltpu.VMEM((16, width), F32),
            pltpu.VMEM((12, 16, width), F32),
            pltpu.SemaphoreType.DMA((sems,)),
            pltpu.SemaphoreType.DMA((sems,)),
        ],
        compiler_params=pltpu.CompilerParams(collective_id=0, has_side_effects=True, vmem_limit_bytes=63 << 20),
        cost_estimate=pl.CostEstimate(flops=60 * 10**9, bytes_accessed=30 * 10**6, transcendentals=16 * 10**6),
    )(tokens, cotangent, parents, segment_ids, w_qkv, w_out, w_up, w_down, *rows)


def finish_kernel(out, dx_in, ga_in, gb_in, gc_in, vec_in, o_out, o_dx, o_qkv, o_bq, o_bv, o_wout, o_bout, o_g1, o_s1, o_up, o_bup,
                  o_down, o_bdown, o_g2, o_s2, dx, ga, vec, sem):
    copies = [pltpu.make_async_copy(src, dst, sem.at[i]) for i, (src, dst) in enumerate(
        ((dx_in, dx), (ga_in, ga), (vec_in, vec), (out, o_out), (gb_in, o_up), (gc_in, o_down)))]
    for copy in copies:
        copy.start()
    for copy in copies[:3]:
        copy.wait()
    o_dx[...] = dx[...].astype(F32)
    a = ga[...]
    for i, (pair, lo) in enumerate(((0, 384), (128, 448), (256, 512))):
        o_qkv[i] = jnp.concatenate([a[:, pair : pair + 128], a[:, lo : lo + HD]], axis=1)
    o_wout[...] = jnp.concatenate([a[:, 640:768], a[:, 576:640]], axis=1).T
    for ref, row in ((o_g2, 0), (o_s2, 1), (o_bdown, 2), (o_g1, 3), (o_s1, 4), (o_bout, 5)):
        ref[...] = vec[row, :]
    width = vec.shape[1]
    for i in range(4):
        o_bup[i * width : (i + 1) * width] = vec[6 + i, :]
    for ref, pair, lo in ((o_bq, 0, 384), (o_bv, 256, 512)):
        row = [vec[10 + i : 11 + i, :] for i in range(4)]
        parts = [p for r in row for p in (r[:, pair : pair + 128], r[:, lo : lo + HD])]
        ref[...] = jnp.concatenate(parts, axis=1)[0]
    for copy in copies[3:]:
        copy.wait()


def plane_body(tokens, parents, segment_ids, w_qkv, b_q, b_v, w_out, b_out, gain_one, shift_one,
               w_up, b_up, w_down, b_down, gain_two, shift_two, cotangent):
    raw = fused_layer(
        tokens, cotangent, parents, segment_ids, w_qkv.transpose(1, 0, 2), w_out, w_up, w_down.T,
        (b_q, b_v, b_out, gain_one, shift_one, b_up, b_down, gain_two, shift_two))
    vm = pl.BlockSpec(memory_space=pltpu.VMEM)
    anywhere = pl.BlockSpec(memory_space=pl.ANY)
    shard, kinds, part = w_qkv.shape
    vector = jax.ShapeDtypeStruct(b_q.shape, F32)
    outs = pl.pallas_call(
        finish_kernel,
        name="finish",
        out_shape=(
            jax.ShapeDtypeStruct(tokens.shape, BF),
            jax.ShapeDtypeStruct(tokens.shape, F32),
            jax.ShapeDtypeStruct((kinds, shard, part), F32),
            vector, vector,
            jax.ShapeDtypeStruct(w_out.shape, F32),
            vector, vector, vector,
            jax.ShapeDtypeStruct(w_up.shape, F32),
            jax.ShapeDtypeStruct(b_up.shape, F32),
            jax.ShapeDtypeStruct(w_down.shape[::-1], F32),
            vector, vector, vector,
        ),
        in_specs=[anywhere] * 6,
        out_specs=(vm,) * 15,
        scratch_shapes=[pltpu.VMEM(tokens.shape, BF), pltpu.VMEM((shard, 4 * part), F32), pltpu.VMEM((16, 4 * part), F32),
                        pltpu.SemaphoreType.DMA((6,))],
        compiler_params=pltpu.CompilerParams(vmem_limit_bytes=63 << 20),
    )(*raw)
    return (outs[0], outs[1], outs[2].transpose(1, 0, 2), *outs[3:11], outs[11].T, *outs[12:])


def solution(mesh):
    dp, ranks = mesh.shape["dp"], mesh.shape["tensor"]
    return jax.shard_map(
        plane_body if (dp, ranks) == (8, 4) else functools.partial(body, dp, ranks),
        mesh=mesh,
        in_specs=(P("dp", "tensor", None), P("dp", None), P("dp", None), P("dp", None, "tensor"), P(), P(),
                  P("tensor", "dp"), P(), P(), P(), P("dp", "tensor"), P(), P("tensor", "dp"), P(), P(), P(),
                  P("dp", "tensor", None)),
        out_specs=(P("dp", "tensor", None), P("dp", "tensor", None), P("dp", None, "tensor"), P(), P(),
                   P("tensor", "dp"), P(), P(), P(), P("dp", "tensor"), P(), P("tensor", "dp"), P(), P(), P()),
        check_vma=False,
    )
```

```python
import functools

import jax
import jax.numpy as jnp
from jax import lax
from jax.experimental import pallas as pl
from jax.experimental.pallas import tpu as pltpu
from jax.sharding import PartitionSpec as P

HD = 64
SEGS = 4
epsilon = 1e-12
BF = jnp.bfloat16
F32 = jnp.float32
FILL = -1e30
HALF_HEADS = ((0, 1, 2, 0, 0), (0, 1, 2, 1, 1), (3, 4, 5, 0, 1))


def dot(a, b, ca=1, cb=0):
    return lax.dot_general(a, b, (((ca,), (cb,)), ((), ())), preferred_element_type=F32)


def split3(v):
    hi = v.astype(BF).astype(F32)
    mid = (v - hi).astype(BF).astype(F32)
    low = v - hi - mid
    return hi, mid, low


def lane_mask(shape, half):
    lane = lax.broadcasted_iota(jnp.int32, shape, 1)
    return (lane < HD) if half == 0 else (lane >= HD)


def pieces(v, shape):
    lane = lax.broadcasted_iota(jnp.int32, shape, 1)
    hi, mid, low = split3(v)
    return jnp.where(lane == 4, hi, jnp.where(lane == 5, mid, jnp.where(lane == 6, low, 0.0)))


def attention_forward_kernel(x_ref, a_ref, bias_ref, rf_ref, kf_ref, tiles_ref, ctx_ref, raug_ref):
    length = x_ref.shape[0]
    block = 256
    count = length // block

    def project(i, _):
        rows = pl.ds(pl.multiple_of(i * block, block), block)
        xb = x_ref[rows, :]
        for t in range(2):
            m = dot(xb, a_ref[t, :, : 5 * 128]) + bias_ref[t][:, : 5 * 128]
            base = 6 * t
            q3 = m[:, 3 * 128 : 4 * 128]
            v3 = m[:, 4 * 128 : 5 * 128]
            tiles_ref[base, rows, :] = m[:, :128].astype(BF) * jnp.asarray(0.125, BF)
            tiles_ref[base + 1, rows, :] = m[:, 128:256].astype(BF)
            tiles_ref[base + 2, rows, :] = m[:, 256:384].astype(BF)
            tiles_ref[base + 3, rows, :] = q3.astype(BF) * jnp.asarray(0.125, BF)
            tiles_ref[base + 4, rows, :] = pltpu.roll(q3, 64, 1).astype(BF)
            tiles_ref[base + 5, rows, :] = pltpu.roll(v3, 64, 1).astype(BF)
        return 0

    lax.fori_loop(0, count, project, 0)
    ones = jnp.ones((length, 128), BF)

    for t in range(2):
        base = 6 * t

        def attend(i, _, t=t, base=base):
            rows = pl.ds(pl.multiple_of(i * block, block), block)
            rf = rf_ref[rows, :]
            parts = []
            for h, (qi, ki, vi, qh, vh) in enumerate(HALF_HEADS):
                q = tiles_ref[base + qi, rows, :]
                qm = jnp.where(lane_mask(q.shape, qh), q, jnp.zeros_like(q))
                qq = jnp.concatenate([qm, rf], axis=1)
                kk = jnp.concatenate([tiles_ref[base + ki], kf_ref[...]], axis=1)
                s = dot(qq, kk, 1, 1)
                m = jnp.max(s, axis=1, keepdims=True)
                p = jnp.exp(s - m).astype(BF)
                vv = jnp.concatenate([tiles_ref[base + vi], ones], axis=1)
                o = dot(p, vv)
                total = o[:, 128:129]
                ov = jnp.where(lane_mask((block, 128), vh), o[:, :128] / total, 0.0)
                lse = m + jnp.log(total)
                raug_ref[3 * t + h, rows, :] = rf + pieces(-lse, (block, 128)).astype(BF)
                parts.append(ov)
            ctx_ref[2 * t, rows, :] = (parts[0] + parts[1]).astype(BF)
            ctx_ref[2 * t + 1, rows, :] = parts[2].astype(BF)
            return 0

        lax.fori_loop(0, count, attend, 0)


def attention_backward_kernel(tiles_ref, ctx_ref, dctx_ref, raug_ref, kf_ref, out_ref, dk_ref, dv_ref):
    length = kf_ref.shape[0]
    block = 256
    count = length // block
    groups = ((HALF_HEADS[0], HALF_HEADS[1]), (HALF_HEADS[2],))
    for t in range(2):
        base = 6 * t
        for g, heads in enumerate(groups):
            dk_ref[...] = jnp.zeros_like(dk_ref)
            dv_ref[...] = jnp.zeros_like(dv_ref)
            ki = heads[0][1]
            vi = heads[0][2]
            k_t = tiles_ref[base + ki].astype(F32).T
            row = lax.broadcasted_iota(jnp.int32, k_t.shape, 0)
            k_masks = [
                jnp.where((row < HD) if qh == 0 else (row >= HD), k_t, 0.0).astype(BF)
                for (_, _, _, qh, _) in heads
            ]

            def back(i, _, t=t, base=base, g=g, heads=heads, k_masks=k_masks, ki=ki, vi=vi):
                rows = pl.ds(pl.multiple_of(i * block, block), block)
                dq_t = jnp.zeros((128, block), F32)
                do = dctx_ref[2 * t + g, rows, :]
                prod = do.astype(F32) * ctx_ref[2 * t + g, rows, :].astype(F32)
                for h, (qi, _, _, qh, vh) in enumerate(heads):
                    q = tiles_ref[base + qi, rows, :]
                    qm = jnp.where(lane_mask(q.shape, qh), q, jnp.zeros_like(q))
                    qa = jnp.concatenate([qm, raug_ref[3 * t + 2 * g + h, rows, :]], axis=1)
                    ka = jnp.concatenate([tiles_ref[base + ki], kf_ref[...]], axis=1)
                    pt = jnp.exp(dot(ka, qa, 1, 1))
                    vmask = lane_mask(do.shape, vh)
                    dom = jnp.where(vmask, do, jnp.zeros_like(do))
                    delta = jnp.sum(jnp.where(vmask, prod, 0.0), axis=1, keepdims=True)
                    doa = jnp.concatenate([dom, pieces(-delta, do.shape).astype(BF)], axis=1)
                    va = jnp.concatenate([tiles_ref[base + vi], kf_ref[...]], axis=1)
                    dst = (pt * dot(va, doa, 1, 1)).astype(BF)
                    dv_ref[...] += dot(pt.astype(BF), dom)
                    dk_ref[...] += dot(dst, qm)
                    dq_t = dq_t + dot(k_masks[h], dst)
                dq = dq_t.T * 0.125
                if g == 0:
                    out_ref[t, rows, 0:128] = dq.astype(BF)
                else:
                    out_ref[t, rows, 384:512] = dq.astype(BF)
                return 0

            lax.fori_loop(0, count, back, 0)
            if g == 0:
                out_ref[t, :, 128:256] = dk_ref[...].astype(BF)
                out_ref[t, :, 256:384] = dv_ref[...].astype(BF)
            else:
                out_ref[t, :, 384:512] = out_ref[t, :, 384:512] + pltpu.roll(dk_ref[...], 64, 1).astype(BF)
                out_ref[t, :, 512:640] = pltpu.roll(dv_ref[...], 64, 1).astype(BF)


def attention_forward(x, a, bias, rf, kf):
    length = x.shape[0]
    vm = pl.BlockSpec(memory_space=pltpu.VMEM)
    return pl.pallas_call(
        attention_forward_kernel,
        name="attn_fwd",
        out_shape=(
            jax.ShapeDtypeStruct((12, length, 128), BF),
            jax.ShapeDtypeStruct((4, length, 128), BF),
            jax.ShapeDtypeStruct((6, length, 128), BF),
        ),
        in_specs=[vm] * 5,
        out_specs=(vm,) * 3,
        compiler_params=pltpu.CompilerParams(vmem_limit_bytes=48 << 20),
        cost_estimate=pl.CostEstimate(flops=20 * 10**9, bytes_accessed=10 * 10**6, transcendentals=6 * 10**6),
    )(x, a, bias, rf, kf)


def attention_backward(tiles, ctx, dctx, raug, kf):
    length = kf.shape[0]
    vm = pl.BlockSpec(memory_space=pltpu.VMEM)
    return pl.pallas_call(
        attention_backward_kernel,
        name="attn_bwd",
        out_shape=jax.ShapeDtypeStruct((2, length, 640), BF),
        in_specs=[vm] * 5,
        out_specs=vm,
        scratch_shapes=[pltpu.VMEM((length, 128), F32), pltpu.VMEM((length, 128), F32)],
        compiler_params=pltpu.CompilerParams(vmem_limit_bytes=48 << 20),
        cost_estimate=pl.CostEstimate(flops=40 * 10**9, bytes_accessed=10 * 10**6, transcendentals=6 * 10**6),
    )(tiles, ctx, dctx, raug, kf)


def ancestry(parents):
    labels = jnp.arange(SEGS, dtype=jnp.int32)
    step = (parents[:, None] == labels[None, :]).astype(F32)
    reach = jnp.eye(SEGS, dtype=F32)
    total = reach
    for _ in range(SEGS - 1):
        reach = jnp.sum(reach[:, :, None] * step[None, :, :], axis=1)
        total = total + reach
    return (total > 0.5).astype(F32)


def gelu_parts(u):
    cdf = 0.5 * (1.0 + lax.erf(u * (2.0**-0.5)))
    pdf = jnp.exp(-0.5 * u * u) * ((2.0 * jnp.pi) ** -0.5)
    return u * cdf, cdf + u * pdf


def norm_parts(rows):
    center = rows - jnp.mean(rows, axis=-1, keepdims=True)
    inverse = lax.rsqrt(jnp.mean(center * center, axis=-1, keepdims=True) + epsilon)
    return center * inverse, inverse


def norm_back(grad_rows, normed, inverse, gain):
    scaled = grad_rows * gain
    return inverse * (
        scaled
        - jnp.mean(scaled, axis=-1, keepdims=True)
        - normed * jnp.mean(scaled * normed, axis=-1, keepdims=True)
    )


def body(dp, ranks, tokens, parents, segment_ids, w_qkv, b_q, b_v, w_out, b_out, gain_one, shift_one,
         w_up, b_up, w_down, b_down, gain_two, shift_two, cotangent):
    d = lax.axis_index("dp")
    ti = lax.axis_index("tensor")
    k = d % 2
    local, quarter, width = tokens.shape
    half_rows = quarter // 2
    own_rows = ranks * half_rows
    length = 2 * own_rows
    part = w_qkv.shape[2]
    hidden_part = w_up.shape[1]
    shard = w_qkv.shape[0]
    chips = dp // 2
    same_core = [[i for i in range(dp) if i % 2 == c] for c in range(2)]

    def swap(v):
        return lax.ppermute(v, "dp", [(i, i ^ 1) for i in range(dp)])

    def pick(v, index, axis=0):
        return lax.dynamic_index_in_dim(v, index, axis, keepdims=False)

    def join(own, peer, axis=0):
        return jnp.where(k == 0, jnp.stack([own, peer], axis), jnp.stack([peer, own], axis))

    def to_tree(v):
        v = v.reshape(local, 2, half_rows, width)
        mine = pick(v, k, 1)
        other = swap(pick(v, 1 - k, 1))
        trees = join(mine, other).reshape(ranks, half_rows, width)
        return lax.all_to_all(trees, "tensor", 0, 0, tiled=True).reshape(own_rows, width)

    def from_tree(v):
        v = lax.all_to_all(v.reshape(ranks, half_rows, width), "tensor", 0, 0, tiled=True)
        v = v.reshape(2, local, half_rows, width)
        other = swap(pick(v, 1 - k))
        return join(pick(v, k), other, 1).reshape(local, quarter, width)

    heads = w_qkv.reshape(shard, 3, 3, HD)
    q, kk, vv = heads[:, 0], heads[:, 1], heads[:, 2]
    out_t = w_out.T.reshape(shard, 3, HD)
    packed_a = jnp.concatenate(
        [q[:, 0], q[:, 1], kk[:, 0], kk[:, 1], vv[:, 0], vv[:, 1], q[:, 2], kk[:, 2], vv[:, 2],
         out_t[:, 2], out_t[:, 0], out_t[:, 1]], axis=1)

    def gather_weight(w):
        every = lax.all_gather(w, "tensor", axis=0, tiled=False).reshape(2, 2, shard, w.shape[1])
        mine = pick(every, k)
        other = swap(pick(every, 1 - k))
        both = join(mine, other, 1)
        full = lax.all_gather(both, "dp", axis=0, tiled=False, axis_index_groups=same_core)
        return full.transpose(1, 0, 2, 3, 4).reshape(2, chips * 2 * shard, w.shape[1])

    x_own = to_tree(tokens)
    w_a = gather_weight(packed_a)
    w_b = gather_weight(w_up)
    w_c = gather_weight(w_down.T)
    x = join(x_own, swap(x_own)).reshape(length, width)
    cot_own = to_tree(cotangent)

    seg_peer = swap(segment_ids)
    par_peer = swap(parents)
    all_seg = join(segment_ids, seg_peer).reshape(ranks, -1)
    all_par = join(parents, par_peer).reshape(ranks, -1)
    seg = pick(all_seg, ti).reshape(ranks, 2, half_rows).transpose(1, 0, 2).reshape(length)
    par = pick(all_par, ti)
    labels = jnp.arange(SEGS, dtype=jnp.int32)
    hot = (seg[:, None] == labels[None, :]).astype(F32)
    reach_rows = jnp.sum(hot[:, :, None] * ancestry(par)[None], axis=1)
    rf = jnp.concatenate([FILL * (1.0 - reach_rows), jnp.zeros((length, 124), F32)], axis=1).astype(BF)
    kf = jnp.concatenate([hot, jnp.ones((length, 3), F32), jnp.zeros((length, 121), F32)], axis=1).astype(BF)

    def half_vector(b, size):
        return lax.dynamic_slice_in_dim(b, 2 * k * size, 2 * size).reshape(2, size)

    bq = half_vector(b_q, part)
    bv = half_vector(b_v, part)
    zero64 = jnp.zeros((2, HD), F32)
    bias = jnp.concatenate(
        [bq[:, :128], jnp.zeros((2, 128), F32), bv[:, :128], bq[:, 128:], zero64, bv[:, 128:], zero64,
         jnp.zeros((2, 128), F32)], axis=1)[:, None, :]

    tiles, ctx, raug = attention_forward(x, w_a, bias, rf, kf)

    def exchange(partial):
        partial = partial.reshape(2, own_rows, width)
        received = swap(pick(partial, 1 - k).astype(BF))
        return pick(partial, k) + received.astype(F32)

    def spread_rows(v):
        return join(v, swap(v)).reshape(length, width)

    partial = 0.0
    for t in range(2):
        partial = partial + dot(ctx[2 * t + 1], w_a[t, :, 512:640], 1, 1) + dot(ctx[2 * t], w_a[t, :, 640:768], 1, 1)
    attended = exchange(partial)
    n1, r1 = norm_parts(x_own.astype(F32) + attended + b_out)
    hidden = n1 * gain_one + shift_one
    rows_low = spread_rows(hidden.astype(BF))
    up_bias = half_vector(b_up, hidden_part)
    inner = [dot(rows_low, w_b[t]) + up_bias[t] for t in range(2)]
    acts = [gelu_parts(u) for u in inner]
    activated = [a.astype(BF) for a, _ in acts]
    branch = exchange(sum(dot(activated[t], w_c[t], 1, 1) for t in range(2)))
    n2, r2 = norm_parts(hidden + branch + b_down)
    output = n2 * gain_two + shift_two
    g = cot_own.astype(F32)
    gain_two_part = jnp.sum(g * n2, axis=0)
    shift_two_part = jnp.sum(g, axis=0)
    mix_two = norm_back(g, n2, r2, gain_two)
    b_down_part = jnp.sum(mix_two, axis=0)
    two_rows = spread_rows(mix_two.astype(BF))
    d_c = [dot(two_rows, activated[t], 0, 0) for t in range(2)]
    grad_inner = [(dot(two_rows, w_c[t]) * acts[t][1]).astype(BF) for t in range(2)]
    b_up_part = jnp.concatenate([jnp.sum(v.astype(F32), axis=0) for v in grad_inner])
    d_b = [dot(rows_low, grad_inner[t], 0, 0) for t in range(2)]
    grad_hidden = mix_two + exchange(sum(dot(grad_inner[t], w_b[t], 1, 1) for t in range(2)))
    gain_one_part = jnp.sum(grad_hidden * n1, axis=0)
    shift_one_part = jnp.sum(grad_hidden, axis=0)
    mix_one = norm_back(grad_hidden, n1, r1, gain_one)
    b_out_part = jnp.sum(mix_one, axis=0)
    one_rows = spread_rows(mix_one.astype(BF))
    dctx = jnp.stack(
        [dot(one_rows, w_a[t, :, lo : lo + 128]).astype(BF) for t in range(2) for lo in (640, 512)])
    d_tiles = attention_backward(tiles, ctx, dctx, raug, kf)

    def d_a_of(t):
        qkv = dot(x, d_tiles[t], 0, 0)
        o2 = dot(one_rows, ctx[2 * t + 1], 0, 0)
        o01 = dot(one_rows, ctx[2 * t], 0, 0)
        lane = lax.broadcasted_iota(jnp.int32, o2.shape, 1)
        return jnp.concatenate([qkv[:, :512], jnp.where(lane < HD, qkv[:, 512:], o2), o01], axis=1)

    d_a = [d_a_of(t) for t in range(2)]
    lane_zero = jnp.where(jnp.arange(640) < 576, 1.0, 0.0).astype(BF)
    grad_x = exchange(sum(dot(d_tiles[t] * lane_zero, w_a[t, :, :640], 1, 1) for t in range(2)))
    input_grad = from_tree((mix_one + grad_x).astype(BF)).astype(F32)
    out = from_tree(output.astype(BF))

    def scatter_weight(pair):
        v = jnp.stack([p.astype(BF) for p in pair]).reshape(2, chips, 2, shard, width).transpose(1, 2, 0, 3, 4)
        v = v.reshape(chips * 4 * shard, width)
        v = lax.psum_scatter(v, "dp", scatter_dimension=0, tiled=True, axis_index_groups=same_core)
        v = v.reshape(2, 2, shard, width)
        other = swap(pick(v, 1 - k))
        v = join(pick(v, k), other).reshape(ranks * shard, width)
        return lax.psum_scatter(v, "tensor", scatter_dimension=0, tiled=True).astype(F32)

    g_c = scatter_weight(d_c)
    g_b = scatter_weight(d_b)
    g_a = scatter_weight(d_a)
    blk = [g_a[:, i * HD : (i + 1) * HD] for i in range(12)]
    grad_qkv = jnp.stack(
        [jnp.concatenate([blk[0], blk[1], blk[6]], 1), jnp.concatenate([blk[2], blk[3], blk[7]], 1),
         jnp.concatenate([blk[4], blk[5], blk[8]], 1)], axis=1)
    grad_out = jnp.concatenate([blk[10], blk[11], blk[9]], 1).T

    sums = jnp.sum(d_tiles.astype(F32), axis=1)
    bq_part = jnp.concatenate([sums[:, :128], sums[:, 384:448]], axis=1).reshape(-1)
    bv_part = jnp.concatenate([sums[:, 256:384], sums[:, 512:576]], axis=1).reshape(-1)

    def spread(v, size):
        return lax.dynamic_update_slice_in_dim(jnp.zeros((size,), F32), v, k * v.shape[0], 0)

    summed = lax.psum(
        (spread(bq_part, width), spread(bv_part, width), b_out_part, gain_one_part, shift_one_part,
         spread(b_up_part, b_up.shape[0]), b_down_part, gain_two_part, shift_two_part), ("dp", "tensor"))
    return (out, input_grad, grad_qkv, summed[0], summed[1], grad_out, summed[2], summed[3], summed[4],
            g_b, summed[5], g_c.T, summed[6], summed[7], summed[8])


A_BLK, B_BLK, C_BLK = 0, 1, 2
ROW_BLOCK = 256
FORWARD_BLOCK = 512
BACKWARD_BLOCK = 256


def gelu_pair(u):
    t = 1.0 / (1.0 + (0.3275911 * 2.0**-0.5) * jnp.abs(u))
    bell = jnp.exp(-0.5 * u * u)
    poly = jnp.full_like(t, 0.5 * 1.061405429)
    for coef in (-1.453152027, 1.421413741, -0.284496736, 0.254829592):
        poly = poly * t + 0.5 * coef
    tail = poly * t * bell
    cdf = jnp.where(u > 0.0, 1.0 - tail, tail)
    return u * cdf, cdf + u * (bell * ((2.0 * jnp.pi) ** -0.5))


def row_mean(v):
    return jnp.mean(v, axis=-1, keepdims=True)


def layer_kernel(tok, cot_in, par, seg, wqkv, wout, wup, wdown, bq, bv, bout, g1, s1, bup, bdown, g2, s2,
                 out, dxr, ga_out, gb_out, gc_out, vec_out,
                 W, X, tiles, ctx, raug, rf, kf, n1, r1, H, act, gp, mix, G2, G1, dctx, own,
                 sbuf, rbuf, obuf, dW, rs1, rs2, rs3, zbuf, tbuf, dkv, ash, seg_all, par_all, vec, vrecv, vgather,
                 ssem, rsem):
    row_of = {n: ref[...][None, :] for n, ref in (("bout", bout), ("g1", g1), ("s1", s1), ("bdown", bdown),
                                                  ("g2", g2), ("s2", s2))}
    d = lax.axis_index("dp")
    t = lax.axis_index("tensor")
    k = lax.rem(d, 2)
    c = d // 2
    ranks = 4
    cx = c + 1 - 2 * lax.rem(c, 2)
    cy = lax.rem(c + 2, 4)
    cd = 3 - c
    length = X.shape[0]
    half = length // 2
    piece = half // ranks
    width = X.shape[1]
    shard = ash.shape[0]
    pair = 2 * shard
    home = t // 2
    here = k * half
    there = (1 - k) * half
    counters = {"s": 0, "r": 0}
    pending = []

    def new(kind, n=1):
        base = counters[kind]
        counters[kind] = base + n
        return base

    def remote(src, dst, s, r, dd, tt):
        return pltpu.make_async_remote_copy(
            src_ref=src, dst_ref=dst, send_sem=ssem.at[s], recv_sem=rsem.at[r], device_id=(dd, tt),
            device_id_type=pl.DeviceIdType.MESH)

    def send(src, dst, r, dd, tt):
        cp = remote(src, dst, new("s"), r, dd, tt)
        cp.start()
        pending.append((None, cp))

    def send_or_copy(src, dst, r, dd, tt):
        cp = remote(src, dst, new("s"), r, dd, tt)
        mine = jnp.logical_and(dd == d, tt == t)

        @pl.when(mine)
        def _():
            pltpu.make_async_copy(src, dst, rsem.at[r]).start()

        @pl.when(jnp.logical_not(mine))
        def _():
            cp.start()

        pending.append((mine, cp))

    def settle(entry):
        mine, cp = entry
        if mine is None:
            cp.wait_send()
        else:
            @pl.when(jnp.logical_not(mine))
            def _():
                cp.wait_send()

    def arrive(dst, r):
        pltpu.make_async_copy(dst, dst, rsem.at[r]).wait()

    def rows_at(start, n, align=None):
        return pl.ds(pl.multiple_of(start, align or n), n)

    barrier = pltpu.get_barrier_semaphore()
    partners = [(2 * c + 1 - k, t), (2 * cx + k, t), (2 * cy + k, t)]
    for j in range(1, ranks):
        for core in range(2):
            partners.append((2 * c + core, lax.rem(t + j, ranks)))
    for dev in partners:
        pl.semaphore_signal(barrier, inc=1, device_id=dev, device_id_type=pl.DeviceIdType.MESH)

    q_all = wqkv[0].astype(F32)
    k_all = wqkv[1].astype(F32)
    v_all = wqkv[2].astype(F32)
    o_all = wout[...].astype(F32).T
    ash[:, 0:128] = q_all[:, :128].astype(BF)
    ash[:, 128:256] = k_all[:, :128].astype(BF)
    ash[:, 256:384] = v_all[:, :128].astype(BF)
    ash[:, 384:512] = jnp.concatenate([q_all[:, 128:], k_all[:, 128:]], axis=1).astype(BF)
    ash[:, 512:640] = jnp.concatenate([v_all[:, 128:], o_all[:, 128:]], axis=1).astype(BF)
    ash[:, 640:768] = o_all[:, :128].astype(BF)
    pl.semaphore_wait(barrier, len(partners))

    slot = lax.rem(t, 2) * 2 + k
    step = 1 - 2 * k

    def shard_rows(b, tt, kk):
        return W.at[b, tt, rows_at(c * pair + kk * shard, shard), :]

    def send_if(wanted, src, dst, r, dd, tt):
        cp = remote(src, dst, new("s"), r, dd, tt)

        @pl.when(wanted)
        def _():
            cp.start()

        pending.append((jnp.logical_not(wanted), cp))

    def z_own(b, src):
        base = new("r", 4)
        dst = shard_rows(b, lax.rem(t, 2), k)
        for j in (1, -1, 2, -2):
            inside = jnp.logical_and(t + j >= 0, t + j < ranks)
            send_if(inside, src, dst, base + slot, 2 * c + home, lax.rem(t + j + ranks, ranks))
        send_or_copy(src, dst, base + slot, 2 * c + home, t)
        return base

    def z_near(b, base):
        for kk in range(2):
            arrive(shard_rows(b, 1 - k, kk), base + 2 * (1 - k) + kk)

    def z_far(b, base):
        for kk in range(2):
            rows = shard_rows(b, k, kk)
            arrive(rows, base + 2 * k + kk)
            send_if(t == 2 - k, rows, rows, base + 2 * k + kk, d, lax.rem(t + step + ranks, ranks))

    def plane_rows(b, far, chip):
        return W.at[b, k if far else 1 - k, rows_at(chip * pair, pair), :]

    def plane_send(b):
        near, far = new("r", 3), new("r", 3)
        n_rows, f_rows = plane_rows(b, False, c), plane_rows(b, True, c)
        send(n_rows, n_rows, near, 2 * cx + k, t)
        send(f_rows, f_rows, far + 1, 2 * cy + k, t)
        send(n_rows, n_rows, near + 1, 2 * cy + k, t)
        send(f_rows, f_rows, far, 2 * cx + k, t)
        return near, far

    def plane_forward(b, near, far):
        rows = plane_rows(b, False, cx)
        arrive(rows, near)
        send(rows, rows, near + 2, 2 * cy + k, t)
        rows = plane_rows(b, True, cy)
        arrive(rows, far + 1)
        send(rows, rows, far + 2, 2 * cx + k, t)

    def plane_wait(b, near, far):
        arrive(plane_rows(b, False, cy), near + 1)
        arrive(plane_rows(b, True, cx), far)
        arrive(plane_rows(b, False, cd), near + 2)
        arrive(plane_rows(b, True, cd), far + 2)

    seg_base = new("r", 2)
    for i, (src, dst) in enumerate(((seg, seg_all), (par, par_all))):
        send(src, dst.at[k], seg_base + i, 2 * c + 1 - k, t)
        dst[pl.ds(k, 1)] = src[...][None]
    def tree_send(src, dst):
        base = new("r", 4)
        for s in range(2):
            for h in range(2):
                send_or_copy(src.at[s, pl.ds(h * piece, piece), :], dst(h), base + t, 2 * c + h, 2 * k + s)
        return base

    za = z_own(A_BLK, ash)
    zb = z_own(B_BLK, wup)
    tok_base = tree_send(tok, lambda h: X.at[rows_at(h * half + t * piece, piece), :])

    arrive(seg_all.at[1 - k], seg_base)
    arrive(par_all.at[1 - k], seg_base + 1)
    lane1 = lax.broadcasted_iota(jnp.int32, (1, 128), 1)
    both = par_all[pl.ds(home, 1)][0]
    second = lax.rem(t, 2) == 1
    parents = jnp.where(second, both[1:2, :], both[0:1, :])
    par_of = [jnp.broadcast_to(parents[:, j : j + 1], (1, 128)) for j in range(SEGS)]
    reach_rows = []
    for s in range(SEGS):
        now = jnp.full((1, 128), s, jnp.int32)
        seen = lane1 == s
        for _ in range(SEGS - 1):
            now = functools.reduce(lambda acc, j: jnp.where(now == j, par_of[j], acc), range(SEGS), now)
            seen = jnp.logical_or(seen, lane1 == now)
        reach_rows.append(jnp.where(lane1 < SEGS, jnp.where(seen, 0.0, FILL), 0.0))
    lane_f = lax.broadcasted_iota(jnp.int32, (piece, 128), 1).astype(F32)
    for h in range(2):
        for q in range(ranks):
            both = seg_all[pl.ds(home, 1), :, pl.ds((2 * q + h) * piece, piece)][0].astype(F32)
            part = jnp.where(second, both[1:2, :], both[0:1, :])
            segs = jnp.broadcast_to(part, (piece, piece)).T
            rows = pl.ds(h * half + q * piece, piece)
            table = jnp.zeros((piece, 128), F32)
            for s in range(SEGS):
                table = jnp.where(segs == s, jnp.broadcast_to(reach_rows[s], (piece, 128)), table)
            rf[rows, :] = table.astype(BF)
            hot = jnp.where(lane_f < SEGS, jnp.where(segs == lane_f, 1.0, 0.0), jnp.where(lane_f < SEGS + 3, 1.0, 0.0))
            kf[rows, :] = hot.astype(BF)

    z_near(A_BLK, za)
    z_far(A_BLK, za)
    pa = plane_send(A_BLK)
    z_near(B_BLK, zb)
    z_far(B_BLK, zb)
    plane_forward(A_BLK, *pa)
    pb = plane_send(B_BLK)
    zc = z_own(C_BLK, wdown)
    fwd_base = new("r", 4)
    for j in range(ranks):
        q = lax.rem(t + j, ranks)
        mine = X.at[rows_at(here + q * piece, piece), :]
        arrive(mine, tok_base + q)
        send(mine, mine, fwd_base + q, 2 * c + 1 - k, t)
    plane_wait(A_BLK, *pa)

    def half_lanes(ref):
        row = ref[...][None, :]
        return jnp.where(k == 0, row[:, : width // 2], row[:, width // 2 :])

    bq2, bv2 = half_lanes(bq), half_lanes(bv)
    zero64 = jnp.zeros((1, HD), F32)
    biases = []
    for tt in range(2):
        lo = 192 * tt
        biases.append((bq2[:, lo : lo + 128], bv2[:, lo : lo + 128],
                       jnp.concatenate([bq2[:, lo + 128 : lo + 192], zero64], axis=1),
                       jnp.concatenate([bv2[:, lo + 128 : lo + 192], zero64], axis=1)))
    eighth = jnp.asarray(0.125, BF)

    def project(start):
        def run(i, _):
            rows = rows_at(start + i * ROW_BLOCK, ROW_BLOCK)
            xb = X[rows, :]
            for tt in range(2):
                m = dot(xb, W[A_BLK, tt, :, 0:640])
                b_q01, b_v01, b_q2, b_v2 = biases[tt]
                base = 6 * tt
                q3 = m[:, 384:512] + b_q2
                v3 = m[:, 512:640] + b_v2
                tiles[base, rows, :] = (m[:, 0:128] + b_q01).astype(BF) * eighth
                tiles[base + 1, rows, :] = m[:, 128:256].astype(BF)
                tiles[base + 2, rows, :] = (m[:, 256:384] + b_v01).astype(BF)
                tiles[base + 3, rows, :] = q3.astype(BF) * eighth
                tiles[base + 4, rows, :] = pltpu.roll(q3, 64, 1).astype(BF)
                tiles[base + 5, rows, :] = pltpu.roll(v3, 64, 1).astype(BF)
            return 0

        lax.fori_loop(0, half // ROW_BLOCK, run, 0)

    project(here)
    plane_forward(B_BLK, *pb)
    for q in range(ranks):
        arrive(X.at[rows_at(there + q * piece, piece), :], fwd_base + q)
    project(there)

    ones = jnp.ones((length, 128), BF)

    def attend_all(tt, lo, hi):
        base = 6 * tt

        def attend(i, _):
            rows = rows_at(i * FORWARD_BLOCK, FORWARD_BLOCK)
            rfb = rf[rows, :]
            parts = []

            def score(h):
                qi, ki, _, qh, _ = HALF_HEADS[h]
                qt = tiles[base + qi, rows, :]
                qm = jnp.where(lane_mask(qt.shape, qh), qt, jnp.zeros_like(qt))
                return dot(jnp.concatenate([qm, rfb], axis=1), jnp.concatenate([tiles[base + ki], kf[...]], axis=1), 1, 1)

            def soften(s):
                top = jnp.max(s, axis=1, keepdims=True)
                return top, jnp.exp(s - top).astype(BF)

            def mix_values(h, top, p):
                vi, vh = HALF_HEADS[h][2], HALF_HEADS[h][4]
                o = dot(p, jnp.concatenate([tiles[base + vi], ones], axis=1))
                total = o[:, 128:129]
                parts.append(jnp.where(lane_mask((FORWARD_BLOCK, 128), vh), o[:, :128] / total, 0.0))
                lse = top + jnp.log(total)
                raug[3 * tt + h, rows, :] = rfb + pieces(-lse, (FORWARD_BLOCK, 128)).astype(BF)

            s0 = score(0)
            s1 = score(1)
            e0 = soften(s0)
            s2 = score(2)
            mix_values(0, *e0)
            e1 = soften(s1)
            mix_values(1, *e1)
            e2 = soften(s2)
            mix_values(2, *e2)
            ctx[tt, rows, 0:128] = parts[2].astype(BF)
            ctx[tt, rows, 128:256] = (parts[0] + parts[1]).astype(BF)
            return 0

        lax.fori_loop(lo, hi, attend, 0)

    blocks = length // FORWARD_BLOCK
    attend_all(0, 0, blocks // 2)
    z_near(C_BLK, zc)
    z_far(C_BLK, zc)
    pc = plane_send(C_BLK)
    cot_base = tree_send(cot_in, lambda h: dW.at[A_BLK, 0, rows_at(t * piece, piece), :])
    attend_all(0, blocks // 2, blocks)
    attend_all(1, 0, blocks)
    plane_forward(C_BLK, *pc)

    exchanged = []

    def exchange(compute, index):
        blocks = half // ROW_BLOCK
        r_base, s_base = new("r", blocks), new("s", blocks)
        if len(exchanged) >= 2:
            for entry in exchanged[-2]:
                pending[:] = [e for e in pending if e is not entry]
                settle(entry)

        def copy_of(i):
            rows = rows_at(i * ROW_BLOCK, ROW_BLOCK)
            return remote(sbuf.at[index, rows, :], rbuf.at[index, rows, :], s_base + i, r_base + i, 2 * c + 1 - k, t)

        def give(i, _):
            sbuf[index, rows_at(i * ROW_BLOCK, ROW_BLOCK), :] = compute(
                rows_at(there + i * ROW_BLOCK, ROW_BLOCK)).astype(BF)
            copy_of(i).start()
            return 0

        lax.fori_loop(0, blocks, give, 0)
        entries = [(None, copy_of(i)) for i in range(blocks)]
        exchanged.append(entries)
        pending.extend(entries)

        def keep(i, _):
            own[rows_at(i * ROW_BLOCK, ROW_BLOCK), :] = compute(rows_at(here + i * ROW_BLOCK, ROW_BLOCK))
            return 0

        lax.fori_loop(0, blocks, keep, 0)

        def ready(i):
            per = ROW_BLOCK // piece

            @pl.when(lax.rem(i, per) == 0)
            def _():
                arrive(rbuf.at[index, rows_at(i * piece, ROW_BLOCK, piece), :], r_base + i // per)

        return ready

    def over_pieces(step, buffer):
        base = new("r", ranks)
        s_base = new("s", ranks)
        def one(i, _):
            rows = rows_at(i * piece, piece)
            full = rows_at(here + i * piece, piece)
            buffer[full, :] = step(rows, i)
            remote(buffer.at[full, :], buffer.at[full, :], s_base + i, base + i, 2 * c + 1 - k, t).start()
            return 0
        lax.fori_loop(0, ranks, one, 0)
        for i in range(ranks):
            full = rows_at(here + i * piece, piece)
            pending.append((None, remote(buffer.at[full, :], buffer.at[full, :], s_base + i, base + i, 2 * c + 1 - k, t)))
        return base

    def wait_pieces(buffer, base):
        for i in range(ranks):
            arrive(buffer.at[rows_at(there + i * piece, piece), :], base + i)

    ra = exchange(lambda rows: dot(ctx[0, rows, :], W[A_BLK, 0, :, 512:768], 1, 1)
                  + dot(ctx[1, rows, :], W[A_BLK, 1, :, 512:768], 1, 1), 0)

    def norm_one(rows, i):
        ra(i)
        x_rows = X[rows_at(here + rows.start, piece), :].astype(F32)
        z = x_rows + own[rows, :] + rbuf[0, rows, :].astype(F32) + row_of['bout']
        center = z - row_mean(z)
        inverse = lax.rsqrt(row_mean(center * center) + epsilon)
        normed = center * inverse
        n1[rows, :] = normed
        r1[rows, :] = jnp.broadcast_to(inverse, (piece, 128))
        return (normed * row_of['g1'] + row_of['s1']).astype(BF)

    hb = over_pieces(norm_one, H)
    plane_wait(B_BLK, *pb)

    up_row = bup[...][None, :]
    up_bias = [jnp.where(k == 0, up_row[:, tt * width : (tt + 1) * width],
                         up_row[:, (2 + tt) * width : (3 + tt) * width]) for tt in range(2)]

    def up(start):
        def run(i, _):
            rows = rows_at(start + i * ROW_BLOCK, ROW_BLOCK)
            for tt in range(2):
                bias = up_bias[tt]
                value, slope = gelu_pair(dot(H[rows, :], W[B_BLK, tt]) + bias)
                act[tt, rows, :] = value.astype(BF)
                gp[tt, rows, :] = slope.astype(BF)
            return 0

        lax.fori_loop(0, half // ROW_BLOCK, run, 0)

    up(here)
    wait_pieces(H, hb)
    up(there)
    plane_wait(C_BLK, *pc)
    rb = exchange(lambda rows: dot(act[0, rows, :], W[C_BLK, 0], 1, 1) + dot(act[1, rows, :], W[C_BLK, 1], 1, 1), 1)
    for q in range(ranks):
        arrive(dW.at[A_BLK, 0, pl.ds(q * piece, piece), :], cot_base + q)
    def piece_back(i, target, r_base, s_base):
        return remote(obuf.at[rows_at(i * piece, piece), :],
                      target.at[lax.rem(t, 2), rows_at(k * piece, piece), :],
                      s_base + i, r_base + lax.rem(t, 2) * 2 + k, 2 * c + home, i)

    def give_back(i, target, r_base, s_base):
        cp = piece_back(i, target, r_base, s_base)
        mine = jnp.logical_and(home == k, t == i)

        @pl.when(mine)
        def _():
            pltpu.make_async_copy(obuf.at[rows_at(i * piece, piece), :],
                                  target.at[lax.rem(t, 2), rows_at(k * piece, piece), :],
                                  rsem.at[r_base + lax.rem(t, 2) * 2 + k]).start()

        @pl.when(jnp.logical_not(mine))
        def _():
            cp.start()

    def given(target, r_base, s_base):
        return [(jnp.logical_and(home == k, t == i), piece_back(i, target, r_base, s_base)) for i in range(ranks)]

    out_base, out_sends = new("r", 4), new("s", ranks)
    vec[...] = jnp.zeros_like(vec)

    def col_add(row, v):
        vec[row : row + 1, :] = vec[row : row + 1, :] + jnp.sum(v, axis=0, keepdims=True)

    def norm_two(rows, i):
        rb(i)
        z = n1[rows, :] * row_of['g1'] + row_of['s1'] + own[rows, :] + rbuf[1, rows, :].astype(F32) + row_of['bdown']
        center = z - row_mean(z)
        inverse = lax.rsqrt(row_mean(center * center) + epsilon)
        normed = center * inverse
        obuf[rows, :] = (normed * row_of['g2'] + row_of['s2']).astype(BF)
        give_back(i, out, out_base, out_sends)
        g = dW[A_BLK, 0, rows, :].astype(F32)
        col_add(0, g * normed)
        col_add(1, g)
        gg = g * row_of['g2']
        back = inverse * (gg - row_mean(gg) - normed * row_mean(gg * normed))
        col_add(2, back)
        mix[rows, :] = back
        return back.astype(BF)

    g2b = over_pieces(norm_two, G2)
    out_entries = given(out, out_base, out_sends)
    pending.extend(out_entries)

    def transpose_half(src, start):
        def run(i, _):
            rows = rows_at(start + i * piece, piece)
            tbuf[:, rows] = src[rows, :].astype(F32).T.astype(BF)
            return 0

        lax.fori_loop(0, half // piece, run, 0)

    def transpose_into(src):
        transpose_half(src, 0)
        transpose_half(src, half)

    def grad_rows(part, chip, kk):
        b, tt, lo, hi = part
        return dW.at[b, tt, rows_at(chip * pair + kk * shard, shard), lo:hi]

    def reduce_one(part):
        b, tt, lo, hi = part
        base = new("r", 4)
        for i, chip in enumerate((cd, cy)):
            send(grad_rows(part, chip, 0), rs1.at[b, tt, 0, i, :, lo:hi], base + i, 2 * cy + k, t)
        for i, chip in enumerate((cd, cx)):
            send(grad_rows(part, chip, 1), rs1.at[b, tt, 1, i, :, lo:hi], base + 2 + i, 2 * cx + k, t)
        return part, base

    def add_rows(part, chip, kk, received):
        b, tt, lo, hi = part
        rows = rows_at(chip * pair + kk * shard, shard)
        dW[b, tt, rows, lo:hi] = (dW[b, tt, rows, lo:hi].astype(F32) + received.astype(F32)).astype(BF)

    def reduce_two(state):
        part, base = state
        b, tt, lo, hi = part
        nxt = new("r", 2)
        for kk, other in ((0, cx), (1, cy)):
            arrive(rs1.at[b, tt, kk, 0, :, lo:hi], base + 2 * kk)
            add_rows(part, other, kk, rs1[b, tt, kk, 0, :, lo:hi])
            send(grad_rows(part, other, kk), rs2.at[b, tt, kk, :, lo:hi], nxt + kk, 2 * other + k, t)
        for kk in range(2):
            arrive(rs1.at[b, tt, kk, 1, :, lo:hi], base + 2 * kk + 1)
            add_rows(part, c, kk, rs1[b, tt, kk, 1, :, lo:hi])
        return part, nxt

    outer = t == (ranks - 1) * (1 - k)
    joiner = t == 1 + (1 - k)
    inward = t + 2 * k - 1
    z_bases = {}

    def reduce_join(state):
        part, nxt = state
        b, tt, lo, hi = part
        base = new("r", 2)
        for kk in range(2):
            arrive(rs2.at[b, tt, kk, :, lo:hi], nxt + kk)
            add_rows(part, c, kk, rs2[b, tt, kk, :, lo:hi])
            send_if(outer, grad_rows(part, c, kk), rs3.at[b, tt, kk, :, lo:hi], base + kk, d,
                    lax.rem(inward + ranks, ranks))
        return part, base

    def reduce_z(state):
        part, base = state
        b, tt, lo, hi = part
        if (b, lo) not in z_bases:
            z_bases[(b, lo)] = new("r", 3)
        z_base = z_bases[(b, lo)]
        for kk in range(2):
            @pl.when(joiner)
            def _(kk=kk):
                arrive(rs3.at[b, tt, kk, :, lo:hi], base + kk)
                add_rows(part, c, kk, rs3[b, tt, kk, :, lo:hi])

            from_slot = lax.rem(t - k + ranks, ranks)
            target = zbuf.at[b, jnp.minimum(from_slot, 2), :, lo:hi]
            cp = remote(grad_rows(part, c, kk), target, new("s"), z_base + jnp.minimum(from_slot, 2),
                        2 * c + kk, 2 * k + tt)
            mine = jnp.logical_and(kk == k, t == 2 * k + tt)

            @pl.when(mine)
            def _(kk=kk):
                pltpu.make_async_copy(grad_rows(part, c, kk), target,
                                      rsem.at[z_base + jnp.minimum(from_slot, 2)]).start()

            away = jnp.logical_and(jnp.logical_not(mine), jnp.logical_not(outer))

            @pl.when(away)
            def _(cp=cp):
                cp.start()

            pending.append((jnp.logical_not(away), cp))

    def reduce_end(b):
        for (blk, lo), base in z_bases.items():
            if blk == b:
                hi = lo + (width if (b, width // 2) not in z_bases else width // 2)
                for q in range(3):
                    arrive(zbuf.at[b, q, :, lo:hi], base + q)
        total = zbuf[b, 0].astype(F32)
        for q in range(1, 3):
            total = total + zbuf[b, q].astype(F32)
        return total

    def grad_matmul(b, tt, right):
        def run(i, _):
            rows = rows_at(i * ROW_BLOCK, ROW_BLOCK)
            dW[b, tt, rows, :] = dot(tbuf[rows, :], right[tt]).astype(BF)
            return 0

        lax.fori_loop(0, width // ROW_BLOCK, run, 0)

    transpose_half(G2, here)
    wait_pieces(G2, g2b)
    transpose_half(G2, there)
    grad_matmul(C_BLK, 0, act)
    rc0 = reduce_one((C_BLK, 0, 0, width))
    grad_matmul(C_BLK, 1, act)
    rc1 = reduce_one((C_BLK, 1, 0, width))

    def back_up(i, _):
        rows = rows_at(i * ROW_BLOCK, ROW_BLOCK)
        for tt in range(2):
            gi = (dot(G2[rows, :], W[C_BLK, tt]) * gp[tt, rows, :].astype(F32)).astype(BF)
            gp[tt, rows, :] = gi
            row = 6 + 2 * k + tt
            vec[pl.ds(row, 1), :] = vec[pl.ds(row, 1), :] + jnp.sum(gi.astype(F32), axis=0, keepdims=True)
        return 0

    lax.fori_loop(0, length // ROW_BLOCK, back_up, 0)
    rh = exchange(lambda rows: dot(gp[0, rows, :], W[B_BLK, 0], 1, 1) + dot(gp[1, rows, :], W[B_BLK, 1], 1, 1), 0)
    transpose_into(H)

    def norm_one_back(rows, i):
        rh(i)
        grad = mix[rows, :] + own[rows, :] + rbuf[0, rows, :].astype(F32)
        normed = n1[rows, :]
        col_add(3, grad * normed)
        col_add(4, grad)
        hh = grad * row_of['g1']
        back = r1[rows, 0:1] * (hh - row_mean(hh) - normed * row_mean(hh * normed))
        col_add(5, back)
        mix[rows, :] = back
        return back.astype(BF)

    g1b = over_pieces(norm_one_back, G1)
    grad_matmul(B_BLK, 0, gp)
    sc0 = reduce_two(rc0)
    rb0 = reduce_one((B_BLK, 0, 0, width))
    grad_matmul(B_BLK, 1, gp)
    sc1 = reduce_two(rc1)
    rb1 = reduce_one((B_BLK, 1, 0, width))

    def back_context(start):
        def run(i, _):
            rows = rows_at(start + i * ROW_BLOCK, ROW_BLOCK)
            for tt in range(2):
                dctx[tt, rows, :] = dot(G1[rows, :], W[A_BLK, tt, :, 512:768]).astype(BF)
            return 0

        lax.fori_loop(0, half // ROW_BLOCK, run, 0)

    back_context(here)
    wait_pieces(G1, g1b)
    back_context(there)
    transpose_into(G1)

    def out_matmul(i, _):
        rows = rows_at(i * ROW_BLOCK, ROW_BLOCK)
        for tt in range(2):
            dW[A_BLK, tt, rows, 512:768] = dot(tbuf[rows, :], ctx[tt]).astype(BF)
        return 0

    lax.fori_loop(0, width // ROW_BLOCK, out_matmul, 0)
    transpose_into(X)

    grads = act

    def attend_back(tt, g, lo=0, hi=length // BACKWARD_BLOCK):
        base = 6 * tt
        heads = HALF_HEADS[0:2] if g == 0 else HALF_HEADS[2:3]
        lanes = slice(128, 256) if g == 0 else slice(0, 128)
        if lo == 0:
            dkv[...] = jnp.zeros_like(dkv)
        ki, vi = heads[0][1], heads[0][2]
        k_t = tiles[base + ki].astype(F32).T
        row = lax.broadcasted_iota(jnp.int32, k_t.shape, 0)
        k_masks = [jnp.where((row < HD) if hd[3] == 0 else (row >= HD), k_t, 0.0).astype(BF) for hd in heads]

        def back(i, _):
            rows = rows_at(i * BACKWARD_BLOCK, BACKWARD_BLOCK)
            dq_t = jnp.zeros((128, BACKWARD_BLOCK), F32)
            do = dctx[tt, rows, lanes]
            prod = do.astype(F32) * ctx[tt, rows, lanes].astype(F32)
            for h, (qi, _, _, qh, vh) in enumerate(heads):
                qt = tiles[base + qi, rows, :]
                qm = jnp.where(lane_mask(qt.shape, qh), qt, jnp.zeros_like(qt))
                qa = jnp.concatenate([qm, raug[3 * tt + 2 * g + h, rows, :]], axis=1)
                pt = jnp.exp(dot(jnp.concatenate([tiles[base + ki], kf[...]], axis=1), qa, 1, 1))
                vmask = lane_mask(do.shape, vh)
                dom = jnp.where(vmask, do, jnp.zeros_like(do))
                delta = jnp.sum(jnp.where(vmask, prod, 0.0), axis=1, keepdims=True)
                doa = jnp.concatenate([dom, pieces(-delta, do.shape).astype(BF)], axis=1)
                dst = (pt * dot(jnp.concatenate([tiles[base + vi], kf[...]], axis=1), doa, 1, 1)).astype(BF)
                dkv[1] += dot(pt.astype(BF), dom)
                dkv[0] += dot(dst, qm)
                dq_t = dq_t + dot(k_masks[h], dst)
            dq = (dq_t.T * 0.125).astype(BF)
            if g == 0:
                grads[tt, rows, 0:128] = dq
            else:
                grads[tt, rows, 384:512] = dq
            return 0

        lax.fori_loop(lo, hi, back, 0)
        if hi < length // BACKWARD_BLOCK:
            return
        if g == 0:
            grads[tt, :, 128:256] = dkv[0].astype(BF)
            grads[tt, :, 256:384] = dkv[1].astype(BF)
        else:
            grads[tt, :, 384:512] = grads[tt, :, 384:512] + pltpu.roll(dkv[0], 64, 1).astype(BF)
            grads[tt, :, 512:640] = pltpu.roll(dkv[1], 64, 1).astype(BF)

    mid = width // 2

    def qkv_matmul(tt, part):
        low = lax.broadcasted_iota(jnp.int32, (ROW_BLOCK, 128), 1) < HD

        def run(i, _):
            rows = rows_at(i * ROW_BLOCK, ROW_BLOCK)
            if part == 0:
                dW[A_BLK, tt, rows, 0:384] = dot(tbuf[rows, :], grads[tt, :, 0:384]).astype(BF)
            else:
                g = dot(tbuf[rows, :], grads[tt, :, 384:640]).astype(BF)
                dW[A_BLK, tt, rows, 384:512] = g[:, 0:128]
                kept = dW[A_BLK, tt, rows, 512:640]
                dW[A_BLK, tt, rows, 512:640] = jnp.where(low, g[:, 128:256], kept)
            return 0

        lax.fori_loop(0, width // ROW_BLOCK, run, 0)
        row = 10 + 2 * k + tt
        lanes = slice(0, 384) if part == 0 else slice(384, 640)
        vec[pl.ds(row, 1), lanes] = jnp.sum(grads[tt, :, lanes].astype(F32), axis=0, keepdims=True)
        return reduce_one((A_BLK, tt, part * mid, part * mid + mid))

    blocks = length // BACKWARD_BLOCK
    attend_back(0, 0, 0, blocks // 2)
    jc0 = reduce_join(sc0)
    attend_back(0, 0, blocks // 2, blocks)
    jc1 = reduce_join(sc1)
    ra00 = qkv_matmul(0, 0)
    sb0 = reduce_two(rb0)
    reduce_z(jc0)
    attend_back(0, 1)
    ra01 = qkv_matmul(0, 1)
    sb1 = reduce_two(rb1)
    reduce_z(jc1)
    attend_back(1, 0, 0, blocks // 2)
    jb0 = reduce_join(sb0)
    sa00 = reduce_two(ra00)
    attend_back(1, 0, blocks // 2, blocks)
    ra10 = qkv_matmul(1, 0)
    jb1 = reduce_join(sb1)
    reduce_z(jb0)
    sa01 = reduce_two(ra01)
    attend_back(1, 1, 0, blocks // 2)
    ja00 = reduce_join(sa00)
    reduce_z(jb1)
    attend_back(1, 1, blocks // 2, blocks)
    ra11 = qkv_matmul(1, 1)

    v_base = new("r", 8)
    send(vec, vrecv.at[0], v_base, 2 * c + 1 - k, t)
    ja01 = reduce_join(sa01)
    sa10 = reduce_two(ra10)
    my_rows = pl.ds(pl.multiple_of(8 * k, 8), 8)
    arrive(vrecv.at[0], v_base)
    chip_total = vrecv.at[1]
    chip_total[...] = vec[...] + vrecv[0]
    vgather[pl.ds(t, 1)] = chip_total[my_rows, :][None]
    for j in range(1, ranks):
        send(chip_total.at[my_rows, :], vgather.at[t], v_base + 1 + t, d, lax.rem(t + j, ranks))
    reduce_z(ja00)
    rx = exchange(lambda rows: dot(grads[0, rows, 0:640], W[A_BLK, 0, :, 0:640], 1, 1)
                  + dot(grads[1, rows, 0:640], W[A_BLK, 1, :, 0:640], 1, 1), 1)
    for s in range(2):
        for h in range(2):
            arrive(out.at[s, pl.ds(h * piece, piece), :], out_base + 2 * s + h)
    for entry in out_entries:
        pending[:] = [e for e in pending if e is not entry]
        settle(entry)
    reduce_z(ja01)
    ja10 = reduce_join(sa10)
    dx_base, dx_sends = new("r", 4), new("s", ranks)

    def finish(i, _):
        rx(i)
        rows = rows_at(i * piece, piece)
        obuf[rows, :] = (mix[rows, :] + own[rows, :] + rbuf[1, rows, :].astype(F32)).astype(BF)
        give_back(i, dxr, dx_base, dx_sends)
        return 0

    lax.fori_loop(0, ranks, finish, 0)
    pending.extend(given(dxr, dx_base, dx_sends))
    sa11 = reduce_two(ra11)
    ja11 = reduce_join(sa11)
    gc_out[...] = reduce_end(C_BLK)
    gb_out[...] = reduce_end(B_BLK)

    for j in range(1, ranks):
        src = lax.rem(t + j, ranks)
        arrive(vgather.at[src], v_base + 1 + src)
    total = vgather[0]
    for j in range(1, ranks):
        total = total + vgather[j]
    vgather[4] = total
    send(vgather.at[4], vgather.at[5], v_base + 5, 2 * cx + k, t)
    reduce_z(ja10)
    arrive(vgather.at[5], v_base + 5)
    total = total + vgather[5]
    vgather[6] = total
    send(vgather.at[6], vgather.at[7], v_base + 6, 2 * cy + k, t)
    reduce_z(ja11)
    arrive(vgather.at[7], v_base + 6)
    final = vrecv.at[2]
    final[my_rows, :] = total + vgather[7]
    send(final.at[my_rows, :], final.at[my_rows, :], v_base + 7, 2 * c + 1 - k, t)
    for s in range(2):
        for h in range(2):
            arrive(dxr.at[s, pl.ds(h * piece, piece), :], dx_base + 2 * s + h)
    ga_out[...] = reduce_end(A_BLK)
    arrive(final.at[pl.ds(pl.multiple_of(8 * (1 - k), 8), 8), :], v_base + 7)
    vec_out[...] = final[...]
    for entry in pending:
        settle(entry)


def fused_layer(tokens, cotangent, parents, segment_ids, w_qkv, w_out, w_up, w_down, vectors):
    local, quarter, width = tokens.shape
    length = segment_ids.shape[1]
    half = length // 2
    shard = w_qkv.shape[1]
    vm = pl.BlockSpec(memory_space=pltpu.VMEM)
    anywhere = pl.BlockSpec(memory_space=pl.ANY)
    rows = list(vectors)
    sems = 224
    return pl.pallas_call(
        layer_kernel,
        name="layer",
        out_shape=(
            jax.ShapeDtypeStruct(tokens.shape, BF),
            jax.ShapeDtypeStruct(tokens.shape, BF),
            jax.ShapeDtypeStruct((shard, width), F32),
            jax.ShapeDtypeStruct((shard, width), F32),
            jax.ShapeDtypeStruct((shard, width), F32),
            jax.ShapeDtypeStruct((16, width), F32),
        ),
        in_specs=[anywhere, anywhere, vm, vm, vm, vm, anywhere, anywhere] + [vm] * len(rows),
        out_specs=(anywhere, anywhere, vm, vm, vm, vm),
        scratch_shapes=[
            pltpu.VMEM((3, 2, width, width), BF),
            pltpu.VMEM((length, width), BF),
            pltpu.VMEM((12, length, 128), BF),
            pltpu.VMEM((2, length, 256), BF),
            pltpu.VMEM((6, length, 128), BF),
            pltpu.VMEM((length, 128), BF),
            pltpu.VMEM((length, 128), BF),
            pltpu.VMEM((half, width), F32),
            pltpu.VMEM((half, 128), F32),
            pltpu.VMEM((length, width), BF),
            pltpu.VMEM((2, length, width), BF),
            pltpu.VMEM((2, length, width), BF),
            pltpu.VMEM((half, width), F32),
            pltpu.VMEM((length, width), BF),
            pltpu.VMEM((length, width), BF),
            pltpu.VMEM((2, length, 256), BF),
            pltpu.VMEM((half, width), F32),
            pltpu.VMEM((2, half, width), BF),
            pltpu.VMEM((2, half, width), BF),
            pltpu.VMEM((half, width), BF),
            pltpu.VMEM((3, 2, width, width), BF),
            pltpu.VMEM((3, 2, 2, 2, shard, width), BF),
            pltpu.VMEM((3, 2, 2, shard, width), BF),
            pltpu.VMEM((3, 2, 2, shard, width), BF),
            pltpu.VMEM((3, 3, shard, width), BF),
            pltpu.VMEM((width, length), BF),
            pltpu.VMEM((2, length, 128), F32),
            pltpu.VMEM((shard, width), BF),
            pltpu.VMEM((2,) + segment_ids.shape, jnp.int32),
            pltpu.VMEM((2,) + parents.shape, jnp.int32),
            pltpu.VMEM((16, width), F32),
            pltpu.VMEM((3, 16, width), F32),
            pltpu.VMEM((8, 8, width), F32),
            pltpu.SemaphoreType.DMA((sems,)),
            pltpu.SemaphoreType.DMA((sems,)),
        ],
        compiler_params=pltpu.CompilerParams(collective_id=0, has_side_effects=True, vmem_limit_bytes=63 << 20),
        cost_estimate=pl.CostEstimate(flops=60 * 10**9, bytes_accessed=30 * 10**6, transcendentals=16 * 10**6),
    )(tokens, cotangent, parents, segment_ids, w_qkv, w_out, w_up, w_down, *rows)


def finish_kernel(out, dx_in, ga_in, gb_in, gc_in, vec_in, o_out, o_dx, o_qkv, o_bq, o_bv, o_wout, o_bout, o_g1, o_s1, o_up, o_bup,
                  o_down, o_bdown, o_g2, o_s2, dx, ga, vec, sem):
    copies = [pltpu.make_async_copy(src, dst, sem.at[i]) for i, (src, dst) in enumerate(
        ((dx_in, dx), (ga_in, ga), (vec_in, vec), (out, o_out), (gb_in, o_up), (gc_in, o_down)))]
    for copy in copies:
        copy.start()
    for copy in copies[:3]:
        copy.wait()
    o_dx[...] = dx[...].astype(F32)
    a = ga[...]
    for i, (pair, lo) in enumerate(((0, 384), (128, 448), (256, 512))):
        o_qkv[i] = jnp.concatenate([a[:, pair : pair + 128], a[:, lo : lo + HD]], axis=1)
    o_wout[...] = jnp.concatenate([a[:, 640:768], a[:, 576:640]], axis=1).T
    for ref, row in ((o_g2, 0), (o_s2, 1), (o_bdown, 2), (o_g1, 3), (o_s1, 4), (o_bout, 5)):
        ref[...] = vec[row, :]
    width = vec.shape[1]
    for i in range(4):
        o_bup[i * width : (i + 1) * width] = vec[6 + i, :]
    for ref, pair, lo in ((o_bq, 0, 384), (o_bv, 256, 512)):
        row = [vec[10 + i : 11 + i, :] for i in range(4)]
        parts = [p for r in row for p in (r[:, pair : pair + 128], r[:, lo : lo + HD])]
        ref[...] = jnp.concatenate(parts, axis=1)[0]
    for copy in copies[3:]:
        copy.wait()


def plane_body(tokens, parents, segment_ids, w_qkv, b_q, b_v, w_out, b_out, gain_one, shift_one,
               w_up, b_up, w_down, b_down, gain_two, shift_two, cotangent):
    raw = fused_layer(
        tokens, cotangent, parents, segment_ids, w_qkv.transpose(1, 0, 2), w_out, w_up, w_down.T,
        (b_q, b_v, b_out, gain_one, shift_one, b_up, b_down, gain_two, shift_two))
    vm = pl.BlockSpec(memory_space=pltpu.VMEM)
    anywhere = pl.BlockSpec(memory_space=pl.ANY)
    shard, kinds, part = w_qkv.shape
    vector = jax.ShapeDtypeStruct(b_q.shape, F32)
    outs = pl.pallas_call(
        finish_kernel,
        name="finish",
        out_shape=(
            jax.ShapeDtypeStruct(tokens.shape, BF),
            jax.ShapeDtypeStruct(tokens.shape, F32),
            jax.ShapeDtypeStruct((kinds, shard, part), F32),
            vector, vector,
            jax.ShapeDtypeStruct(w_out.shape, F32),
            vector, vector, vector,
            jax.ShapeDtypeStruct(w_up.shape, F32),
            jax.ShapeDtypeStruct(b_up.shape, F32),
            jax.ShapeDtypeStruct(w_down.shape[::-1], F32),
            vector, vector, vector,
        ),
        in_specs=[anywhere] * 6,
        out_specs=(vm,) * 15,
        scratch_shapes=[pltpu.VMEM(tokens.shape, BF), pltpu.VMEM((shard, 4 * part), F32), pltpu.VMEM((16, 4 * part), F32),
                        pltpu.SemaphoreType.DMA((6,))],
        compiler_params=pltpu.CompilerParams(vmem_limit_bytes=63 << 20),
    )(*raw)
    return (outs[0], outs[1], outs[2].transpose(1, 0, 2), *outs[3:11], outs[11].T, *outs[12:])


def solution(mesh):
    dp, ranks = mesh.shape["dp"], mesh.shape["tensor"]
    return jax.shard_map(
        plane_body if (dp, ranks) == (8, 4) else functools.partial(body, dp, ranks),
        mesh=mesh,
        in_specs=(P("dp", "tensor", None), P("dp", None), P("dp", None), P("dp", None, "tensor"), P(), P(),
                  P("tensor", "dp"), P(), P(), P(), P("dp", "tensor"), P(), P("tensor", "dp"), P(), P(), P(),
                  P("dp", "tensor", None)),
        out_specs=(P("dp", "tensor", None), P("dp", "tensor", None), P("dp", None, "tensor"), P(), P(),
                   P("tensor", "dp"), P(), P(), P(), P("dp", "tensor"), P(), P("tensor", "dp"), P(), P(), P()),
        check_vma=False,
    )
```

```python
import functools

import jax
import jax.numpy as jnp
from jax import lax
from jax.experimental import pallas as pl
from jax.experimental.pallas import tpu as pltpu
from jax.sharding import PartitionSpec as P

HD = 64
SEGS = 4
epsilon = 1e-12
BF = jnp.bfloat16
F32 = jnp.float32
FILL = -1e30
HALF_HEADS = ((0, 1, 2, 0, 0), (0, 1, 2, 1, 1), (3, 4, 5, 0, 1))


def dot(a, b, ca=1, cb=0):
    return lax.dot_general(a, b, (((ca,), (cb,)), ((), ())), preferred_element_type=F32)


def split3(v):
    hi = v.astype(BF).astype(F32)
    mid = (v - hi).astype(BF).astype(F32)
    low = v - hi - mid
    return hi, mid, low


def lane_mask(shape, half):
    lane = lax.broadcasted_iota(jnp.int32, shape, 1)
    return (lane < HD) if half == 0 else (lane >= HD)


def pieces(v, shape):
    lane = lax.broadcasted_iota(jnp.int32, shape, 1)
    hi, mid, low = split3(v)
    return jnp.where(lane == 4, hi, jnp.where(lane == 5, mid, jnp.where(lane == 6, low, 0.0)))


def attention_forward_kernel(x_ref, a_ref, bias_ref, rf_ref, kf_ref, tiles_ref, ctx_ref, raug_ref):
    length = x_ref.shape[0]
    block = 256
    count = length // block

    def project(i, _):
        rows = pl.ds(pl.multiple_of(i * block, block), block)
        xb = x_ref[rows, :]
        for t in range(2):
            m = dot(xb, a_ref[t, :, : 5 * 128]) + bias_ref[t][:, : 5 * 128]
            base = 6 * t
            q3 = m[:, 3 * 128 : 4 * 128]
            v3 = m[:, 4 * 128 : 5 * 128]
            tiles_ref[base, rows, :] = m[:, :128].astype(BF) * jnp.asarray(0.125, BF)
            tiles_ref[base + 1, rows, :] = m[:, 128:256].astype(BF)
            tiles_ref[base + 2, rows, :] = m[:, 256:384].astype(BF)
            tiles_ref[base + 3, rows, :] = q3.astype(BF) * jnp.asarray(0.125, BF)
            tiles_ref[base + 4, rows, :] = pltpu.roll(q3, 64, 1).astype(BF)
            tiles_ref[base + 5, rows, :] = pltpu.roll(v3, 64, 1).astype(BF)
        return 0

    lax.fori_loop(0, count, project, 0)
    ones = jnp.ones((length, 128), BF)

    for t in range(2):
        base = 6 * t

        def attend(i, _, t=t, base=base):
            rows = pl.ds(pl.multiple_of(i * block, block), block)
            rf = rf_ref[rows, :]
            parts = []
            for h, (qi, ki, vi, qh, vh) in enumerate(HALF_HEADS):
                q = tiles_ref[base + qi, rows, :]
                qm = jnp.where(lane_mask(q.shape, qh), q, jnp.zeros_like(q))
                qq = jnp.concatenate([qm, rf], axis=1)
                kk = jnp.concatenate([tiles_ref[base + ki], kf_ref[...]], axis=1)
                s = dot(qq, kk, 1, 1)
                m = jnp.max(s, axis=1, keepdims=True)
                p = jnp.exp(s - m).astype(BF)
                vv = jnp.concatenate([tiles_ref[base + vi], ones], axis=1)
                o = dot(p, vv)
                total = o[:, 128:129]
                ov = jnp.where(lane_mask((block, 128), vh), o[:, :128] / total, 0.0)
                lse = m + jnp.log(total)
                raug_ref[3 * t + h, rows, :] = rf + pieces(-lse, (block, 128)).astype(BF)
                parts.append(ov)
            ctx_ref[2 * t, rows, :] = (parts[0] + parts[1]).astype(BF)
            ctx_ref[2 * t + 1, rows, :] = parts[2].astype(BF)
            return 0

        lax.fori_loop(0, count, attend, 0)


def attention_backward_kernel(tiles_ref, ctx_ref, dctx_ref, raug_ref, kf_ref, out_ref, dk_ref, dv_ref):
    length = kf_ref.shape[0]
    block = 256
    count = length // block
    groups = ((HALF_HEADS[0], HALF_HEADS[1]), (HALF_HEADS[2],))
    for t in range(2):
        base = 6 * t
        for g, heads in enumerate(groups):
            dk_ref[...] = jnp.zeros_like(dk_ref)
            dv_ref[...] = jnp.zeros_like(dv_ref)
            ki = heads[0][1]
            vi = heads[0][2]
            k_t = tiles_ref[base + ki].astype(F32).T
            row = lax.broadcasted_iota(jnp.int32, k_t.shape, 0)
            k_masks = [
                jnp.where((row < HD) if qh == 0 else (row >= HD), k_t, 0.0).astype(BF)
                for (_, _, _, qh, _) in heads
            ]

            def back(i, _, t=t, base=base, g=g, heads=heads, k_masks=k_masks, ki=ki, vi=vi):
                rows = pl.ds(pl.multiple_of(i * block, block), block)
                dq_t = jnp.zeros((128, block), F32)
                do = dctx_ref[2 * t + g, rows, :]
                prod = do.astype(F32) * ctx_ref[2 * t + g, rows, :].astype(F32)
                for h, (qi, _, _, qh, vh) in enumerate(heads):
                    q = tiles_ref[base + qi, rows, :]
                    qm = jnp.where(lane_mask(q.shape, qh), q, jnp.zeros_like(q))
                    qa = jnp.concatenate([qm, raug_ref[3 * t + 2 * g + h, rows, :]], axis=1)
                    ka = jnp.concatenate([tiles_ref[base + ki], kf_ref[...]], axis=1)
                    pt = jnp.exp(dot(ka, qa, 1, 1))
                    vmask = lane_mask(do.shape, vh)
                    dom = jnp.where(vmask, do, jnp.zeros_like(do))
                    delta = jnp.sum(jnp.where(vmask, prod, 0.0), axis=1, keepdims=True)
                    doa = jnp.concatenate([dom, pieces(-delta, do.shape).astype(BF)], axis=1)
                    va = jnp.concatenate([tiles_ref[base + vi], kf_ref[...]], axis=1)
                    dst = (pt * dot(va, doa, 1, 1)).astype(BF)
                    dv_ref[...] += dot(pt.astype(BF), dom)
                    dk_ref[...] += dot(dst, qm)
                    dq_t = dq_t + dot(k_masks[h], dst)
                dq = dq_t.T * 0.125
                if g == 0:
                    out_ref[t, rows, 0:128] = dq.astype(BF)
                else:
                    out_ref[t, rows, 384:512] = dq.astype(BF)
                return 0

            lax.fori_loop(0, count, back, 0)
            if g == 0:
                out_ref[t, :, 128:256] = dk_ref[...].astype(BF)
                out_ref[t, :, 256:384] = dv_ref[...].astype(BF)
            else:
                out_ref[t, :, 384:512] = out_ref[t, :, 384:512] + pltpu.roll(dk_ref[...], 64, 1).astype(BF)
                out_ref[t, :, 512:640] = pltpu.roll(dv_ref[...], 64, 1).astype(BF)


def attention_forward(x, a, bias, rf, kf):
    length = x.shape[0]
    vm = pl.BlockSpec(memory_space=pltpu.VMEM)
    return pl.pallas_call(
        attention_forward_kernel,
        name="attn_fwd",
        out_shape=(
            jax.ShapeDtypeStruct((12, length, 128), BF),
            jax.ShapeDtypeStruct((4, length, 128), BF),
            jax.ShapeDtypeStruct((6, length, 128), BF),
        ),
        in_specs=[vm] * 5,
        out_specs=(vm,) * 3,
        compiler_params=pltpu.CompilerParams(vmem_limit_bytes=48 << 20),
        cost_estimate=pl.CostEstimate(flops=20 * 10**9, bytes_accessed=10 * 10**6, transcendentals=6 * 10**6),
    )(x, a, bias, rf, kf)


def attention_backward(tiles, ctx, dctx, raug, kf):
    length = kf.shape[0]
    vm = pl.BlockSpec(memory_space=pltpu.VMEM)
    return pl.pallas_call(
        attention_backward_kernel,
        name="attn_bwd",
        out_shape=jax.ShapeDtypeStruct((2, length, 640), BF),
        in_specs=[vm] * 5,
        out_specs=vm,
        scratch_shapes=[pltpu.VMEM((length, 128), F32), pltpu.VMEM((length, 128), F32)],
        compiler_params=pltpu.CompilerParams(vmem_limit_bytes=48 << 20),
        cost_estimate=pl.CostEstimate(flops=40 * 10**9, bytes_accessed=10 * 10**6, transcendentals=6 * 10**6),
    )(tiles, ctx, dctx, raug, kf)


def ancestry(parents):
    labels = jnp.arange(SEGS, dtype=jnp.int32)
    step = (parents[:, None] == labels[None, :]).astype(F32)
    reach = jnp.eye(SEGS, dtype=F32)
    total = reach
    for _ in range(SEGS - 1):
        reach = jnp.sum(reach[:, :, None] * step[None, :, :], axis=1)
        total = total + reach
    return (total > 0.5).astype(F32)


def gelu_parts(u):
    cdf = 0.5 * (1.0 + lax.erf(u * (2.0**-0.5)))
    pdf = jnp.exp(-0.5 * u * u) * ((2.0 * jnp.pi) ** -0.5)
    return u * cdf, cdf + u * pdf


def norm_parts(rows):
    center = rows - jnp.mean(rows, axis=-1, keepdims=True)
    inverse = lax.rsqrt(jnp.mean(center * center, axis=-1, keepdims=True) + epsilon)
    return center * inverse, inverse


def norm_back(grad_rows, normed, inverse, gain):
    scaled = grad_rows * gain
    return inverse * (
        scaled
        - jnp.mean(scaled, axis=-1, keepdims=True)
        - normed * jnp.mean(scaled * normed, axis=-1, keepdims=True)
    )


def body(dp, ranks, tokens, parents, segment_ids, w_qkv, b_q, b_v, w_out, b_out, gain_one, shift_one,
         w_up, b_up, w_down, b_down, gain_two, shift_two, cotangent):
    d = lax.axis_index("dp")
    ti = lax.axis_index("tensor")
    k = d % 2
    local, quarter, width = tokens.shape
    half_rows = quarter // 2
    own_rows = ranks * half_rows
    length = 2 * own_rows
    part = w_qkv.shape[2]
    hidden_part = w_up.shape[1]
    shard = w_qkv.shape[0]
    chips = dp // 2
    same_core = [[i for i in range(dp) if i % 2 == c] for c in range(2)]

    def swap(v):
        return lax.ppermute(v, "dp", [(i, i ^ 1) for i in range(dp)])

    def pick(v, index, axis=0):
        return lax.dynamic_index_in_dim(v, index, axis, keepdims=False)

    def join(own, peer, axis=0):
        return jnp.where(k == 0, jnp.stack([own, peer], axis), jnp.stack([peer, own], axis))

    def to_tree(v):
        v = v.reshape(local, 2, half_rows, width)
        mine = pick(v, k, 1)
        other = swap(pick(v, 1 - k, 1))
        trees = join(mine, other).reshape(ranks, half_rows, width)
        return lax.all_to_all(trees, "tensor", 0, 0, tiled=True).reshape(own_rows, width)

    def from_tree(v):
        v = lax.all_to_all(v.reshape(ranks, half_rows, width), "tensor", 0, 0, tiled=True)
        v = v.reshape(2, local, half_rows, width)
        other = swap(pick(v, 1 - k))
        return join(pick(v, k), other, 1).reshape(local, quarter, width)

    heads = w_qkv.reshape(shard, 3, 3, HD)
    q, kk, vv = heads[:, 0], heads[:, 1], heads[:, 2]
    out_t = w_out.T.reshape(shard, 3, HD)
    packed_a = jnp.concatenate(
        [q[:, 0], q[:, 1], kk[:, 0], kk[:, 1], vv[:, 0], vv[:, 1], q[:, 2], kk[:, 2], vv[:, 2],
         out_t[:, 2], out_t[:, 0], out_t[:, 1]], axis=1)

    def gather_weight(w):
        every = lax.all_gather(w, "tensor", axis=0, tiled=False).reshape(2, 2, shard, w.shape[1])
        mine = pick(every, k)
        other = swap(pick(every, 1 - k))
        both = join(mine, other, 1)
        full = lax.all_gather(both, "dp", axis=0, tiled=False, axis_index_groups=same_core)
        return full.transpose(1, 0, 2, 3, 4).reshape(2, chips * 2 * shard, w.shape[1])

    x_own = to_tree(tokens)
    w_a = gather_weight(packed_a)
    w_b = gather_weight(w_up)
    w_c = gather_weight(w_down.T)
    x = join(x_own, swap(x_own)).reshape(length, width)
    cot_own = to_tree(cotangent)

    seg_peer = swap(segment_ids)
    par_peer = swap(parents)
    all_seg = join(segment_ids, seg_peer).reshape(ranks, -1)
    all_par = join(parents, par_peer).reshape(ranks, -1)
    seg = pick(all_seg, ti).reshape(ranks, 2, half_rows).transpose(1, 0, 2).reshape(length)
    par = pick(all_par, ti)
    labels = jnp.arange(SEGS, dtype=jnp.int32)
    hot = (seg[:, None] == labels[None, :]).astype(F32)
    reach_rows = jnp.sum(hot[:, :, None] * ancestry(par)[None], axis=1)
    rf = jnp.concatenate([FILL * (1.0 - reach_rows), jnp.zeros((length, 124), F32)], axis=1).astype(BF)
    kf = jnp.concatenate([hot, jnp.ones((length, 3), F32), jnp.zeros((length, 121), F32)], axis=1).astype(BF)

    def half_vector(b, size):
        return lax.dynamic_slice_in_dim(b, 2 * k * size, 2 * size).reshape(2, size)

    bq = half_vector(b_q, part)
    bv = half_vector(b_v, part)
    zero64 = jnp.zeros((2, HD), F32)
    bias = jnp.concatenate(
        [bq[:, :128], jnp.zeros((2, 128), F32), bv[:, :128], bq[:, 128:], zero64, bv[:, 128:], zero64,
         jnp.zeros((2, 128), F32)], axis=1)[:, None, :]

    tiles, ctx, raug = attention_forward(x, w_a, bias, rf, kf)

    def exchange(partial):
        partial = partial.reshape(2, own_rows, width)
        received = swap(pick(partial, 1 - k).astype(BF))
        return pick(partial, k) + received.astype(F32)

    def spread_rows(v):
        return join(v, swap(v)).reshape(length, width)

    partial = 0.0
    for t in range(2):
        partial = partial + dot(ctx[2 * t + 1], w_a[t, :, 512:640], 1, 1) + dot(ctx[2 * t], w_a[t, :, 640:768], 1, 1)
    attended = exchange(partial)
    n1, r1 = norm_parts(x_own.astype(F32) + attended + b_out)
    hidden = n1 * gain_one + shift_one
    rows_low = spread_rows(hidden.astype(BF))
    up_bias = half_vector(b_up, hidden_part)
    inner = [dot(rows_low, w_b[t]) + up_bias[t] for t in range(2)]
    acts = [gelu_parts(u) for u in inner]
    activated = [a.astype(BF) for a, _ in acts]
    branch = exchange(sum(dot(activated[t], w_c[t], 1, 1) for t in range(2)))
    n2, r2 = norm_parts(hidden + branch + b_down)
    output = n2 * gain_two + shift_two
    g = cot_own.astype(F32)
    gain_two_part = jnp.sum(g * n2, axis=0)
    shift_two_part = jnp.sum(g, axis=0)
    mix_two = norm_back(g, n2, r2, gain_two)
    b_down_part = jnp.sum(mix_two, axis=0)
    two_rows = spread_rows(mix_two.astype(BF))
    d_c = [dot(two_rows, activated[t], 0, 0) for t in range(2)]
    grad_inner = [(dot(two_rows, w_c[t]) * acts[t][1]).astype(BF) for t in range(2)]
    b_up_part = jnp.concatenate([jnp.sum(v.astype(F32), axis=0) for v in grad_inner])
    d_b = [dot(rows_low, grad_inner[t], 0, 0) for t in range(2)]
    grad_hidden = mix_two + exchange(sum(dot(grad_inner[t], w_b[t], 1, 1) for t in range(2)))
    gain_one_part = jnp.sum(grad_hidden * n1, axis=0)
    shift_one_part = jnp.sum(grad_hidden, axis=0)
    mix_one = norm_back(grad_hidden, n1, r1, gain_one)
    b_out_part = jnp.sum(mix_one, axis=0)
    one_rows = spread_rows(mix_one.astype(BF))
    dctx = jnp.stack(
        [dot(one_rows, w_a[t, :, lo : lo + 128]).astype(BF) for t in range(2) for lo in (640, 512)])
    d_tiles = attention_backward(tiles, ctx, dctx, raug, kf)

    def d_a_of(t):
        qkv = dot(x, d_tiles[t], 0, 0)
        o2 = dot(one_rows, ctx[2 * t + 1], 0, 0)
        o01 = dot(one_rows, ctx[2 * t], 0, 0)
        lane = lax.broadcasted_iota(jnp.int32, o2.shape, 1)
        return jnp.concatenate([qkv[:, :512], jnp.where(lane < HD, qkv[:, 512:], o2), o01], axis=1)

    d_a = [d_a_of(t) for t in range(2)]
    lane_zero = jnp.where(jnp.arange(640) < 576, 1.0, 0.0).astype(BF)
    grad_x = exchange(sum(dot(d_tiles[t] * lane_zero, w_a[t, :, :640], 1, 1) for t in range(2)))
    input_grad = from_tree((mix_one + grad_x).astype(BF)).astype(F32)
    out = from_tree(output.astype(BF))

    def scatter_weight(pair):
        v = jnp.stack([p.astype(BF) for p in pair]).reshape(2, chips, 2, shard, width).transpose(1, 2, 0, 3, 4)
        v = v.reshape(chips * 4 * shard, width)
        v = lax.psum_scatter(v, "dp", scatter_dimension=0, tiled=True, axis_index_groups=same_core)
        v = v.reshape(2, 2, shard, width)
        other = swap(pick(v, 1 - k))
        v = join(pick(v, k), other).reshape(ranks * shard, width)
        return lax.psum_scatter(v, "tensor", scatter_dimension=0, tiled=True).astype(F32)

    g_c = scatter_weight(d_c)
    g_b = scatter_weight(d_b)
    g_a = scatter_weight(d_a)
    blk = [g_a[:, i * HD : (i + 1) * HD] for i in range(12)]
    grad_qkv = jnp.stack(
        [jnp.concatenate([blk[0], blk[1], blk[6]], 1), jnp.concatenate([blk[2], blk[3], blk[7]], 1),
         jnp.concatenate([blk[4], blk[5], blk[8]], 1)], axis=1)
    grad_out = jnp.concatenate([blk[10], blk[11], blk[9]], 1).T

    sums = jnp.sum(d_tiles.astype(F32), axis=1)
    bq_part = jnp.concatenate([sums[:, :128], sums[:, 384:448]], axis=1).reshape(-1)
    bv_part = jnp.concatenate([sums[:, 256:384], sums[:, 512:576]], axis=1).reshape(-1)

    def spread(v, size):
        return lax.dynamic_update_slice_in_dim(jnp.zeros((size,), F32), v, k * v.shape[0], 0)

    summed = lax.psum(
        (spread(bq_part, width), spread(bv_part, width), b_out_part, gain_one_part, shift_one_part,
         spread(b_up_part, b_up.shape[0]), b_down_part, gain_two_part, shift_two_part), ("dp", "tensor"))
    return (out, input_grad, grad_qkv, summed[0], summed[1], grad_out, summed[2], summed[3], summed[4],
            g_b, summed[5], g_c.T, summed[6], summed[7], summed[8])


A_BLK, B_BLK, C_BLK = 0, 1, 2
ROW_BLOCK = 256
FORWARD_BLOCK = 512
BACKWARD_BLOCK = 256


def gelu_pair(u):
    t = 1.0 / (1.0 + (0.3275911 * 2.0**-0.5) * jnp.abs(u))
    bell = jnp.exp(-0.5 * u * u)
    poly = jnp.full_like(t, 0.5 * 1.061405429)
    for coef in (-1.453152027, 1.421413741, -0.284496736, 0.254829592):
        poly = poly * t + 0.5 * coef
    tail = poly * t * bell
    cdf = jnp.where(u > 0.0, 1.0 - tail, tail)
    return u * cdf, cdf + u * (bell * ((2.0 * jnp.pi) ** -0.5))


def row_mean(v):
    return jnp.mean(v, axis=-1, keepdims=True)


def layer_kernel(tok, cot_in, par, seg, wqkv, wout, wup, wdown, bq, bv, bout, g1, s1, bup, bdown, g2, s2,
                 out, dxr, ga_out, gb_out, gc_out, vec_out,
                 W, X, tiles, ctx, raug, rf, kf, n1, r1, H, act, gp, mix, G2, G1, dctx, own,
                 sbuf, rbuf, obuf, dW, rs1, rs2, rs3, zbuf, tbuf, dkv, ash, seg_all, par_all, vec, vrecv, vgather,
                 ssem, rsem):
    row_of = {n: ref[...][None, :] for n, ref in (("bout", bout), ("g1", g1), ("s1", s1), ("bdown", bdown),
                                                  ("g2", g2), ("s2", s2))}
    d = lax.axis_index("dp")
    t = lax.axis_index("tensor")
    k = lax.rem(d, 2)
    c = d // 2
    ranks = 4
    cx = c + 1 - 2 * lax.rem(c, 2)
    cy = lax.rem(c + 2, 4)
    cd = 3 - c
    length = X.shape[0]
    half = length // 2
    piece = half // ranks
    width = X.shape[1]
    shard = ash.shape[0]
    pair = 2 * shard
    home = t // 2
    here = k * half
    there = (1 - k) * half
    counters = {"s": 0, "r": 0}
    pending = []

    def new(kind, n=1):
        base = counters[kind]
        counters[kind] = base + n
        return base

    def remote(src, dst, s, r, dd, tt):
        return pltpu.make_async_remote_copy(
            src_ref=src, dst_ref=dst, send_sem=ssem.at[s], recv_sem=rsem.at[r], device_id=(dd, tt),
            device_id_type=pl.DeviceIdType.MESH)

    def send(src, dst, r, dd, tt):
        cp = remote(src, dst, new("s"), r, dd, tt)
        cp.start()
        pending.append((None, cp))

    def send_or_copy(src, dst, r, dd, tt):
        cp = remote(src, dst, new("s"), r, dd, tt)
        mine = jnp.logical_and(dd == d, tt == t)

        @pl.when(mine)
        def _():
            pltpu.make_async_copy(src, dst, rsem.at[r]).start()

        @pl.when(jnp.logical_not(mine))
        def _():
            cp.start()

        pending.append((mine, cp))

    def settle(entry):
        mine, cp = entry
        if mine is None:
            cp.wait_send()
        else:
            @pl.when(jnp.logical_not(mine))
            def _():
                cp.wait_send()

    def arrive(dst, r):
        pltpu.make_async_copy(dst, dst, rsem.at[r]).wait()

    def rows_at(start, n, align=None):
        return pl.ds(pl.multiple_of(start, align or n), n)

    barrier = pltpu.get_barrier_semaphore()
    partners = [(2 * c + 1 - k, t), (2 * cx + k, t), (2 * cy + k, t)]
    for j in range(1, ranks):
        for core in range(2):
            partners.append((2 * c + core, lax.rem(t + j, ranks)))
    for dev in partners:
        pl.semaphore_signal(barrier, inc=1, device_id=dev, device_id_type=pl.DeviceIdType.MESH)

    q_all = wqkv[0].astype(F32)
    k_all = wqkv[1].astype(F32)
    v_all = wqkv[2].astype(F32)
    o_all = wout[...].astype(F32).T
    ash[:, 0:128] = q_all[:, :128].astype(BF)
    ash[:, 128:256] = k_all[:, :128].astype(BF)
    ash[:, 256:384] = v_all[:, :128].astype(BF)
    ash[:, 384:512] = jnp.concatenate([q_all[:, 128:], k_all[:, 128:]], axis=1).astype(BF)
    ash[:, 512:640] = jnp.concatenate([v_all[:, 128:], o_all[:, 128:]], axis=1).astype(BF)
    ash[:, 640:768] = o_all[:, :128].astype(BF)
    pl.semaphore_wait(barrier, len(partners))

    slot = lax.rem(t, 2) * 2 + k
    step = 1 - 2 * k

    def shard_rows(b, tt, kk):
        return W.at[b, tt, rows_at(c * pair + kk * shard, shard), :]

    def send_if(wanted, src, dst, r, dd, tt):
        cp = remote(src, dst, new("s"), r, dd, tt)

        @pl.when(wanted)
        def _():
            cp.start()

        pending.append((jnp.logical_not(wanted), cp))

    def z_own(b, src):
        base = new("r", 4)
        dst = shard_rows(b, lax.rem(t, 2), k)
        for j in (1, -1, 2, -2):
            inside = jnp.logical_and(t + j >= 0, t + j < ranks)
            send_if(inside, src, dst, base + slot, 2 * c + home, lax.rem(t + j + ranks, ranks))
        send_or_copy(src, dst, base + slot, 2 * c + home, t)
        return base

    def z_near(b, base):
        for kk in range(2):
            arrive(shard_rows(b, 1 - k, kk), base + 2 * (1 - k) + kk)

    def z_far(b, base):
        for kk in range(2):
            rows = shard_rows(b, k, kk)
            arrive(rows, base + 2 * k + kk)
            send_if(t == 2 - k, rows, rows, base + 2 * k + kk, d, lax.rem(t + step + ranks, ranks))

    def plane_rows(b, far, chip):
        return W.at[b, k if far else 1 - k, rows_at(chip * pair, pair), :]

    def plane_send(b):
        near, far = new("r", 3), new("r", 3)
        n_rows, f_rows = plane_rows(b, False, c), plane_rows(b, True, c)
        send(n_rows, n_rows, near, 2 * cx + k, t)
        send(f_rows, f_rows, far + 1, 2 * cy + k, t)
        send(n_rows, n_rows, near + 1, 2 * cy + k, t)
        send(f_rows, f_rows, far, 2 * cx + k, t)
        return near, far

    def plane_forward(b, near, far):
        rows = plane_rows(b, False, cx)
        arrive(rows, near)
        send(rows, rows, near + 2, 2 * cy + k, t)
        rows = plane_rows(b, True, cy)
        arrive(rows, far + 1)
        send(rows, rows, far + 2, 2 * cx + k, t)

    def plane_wait(b, near, far):
        arrive(plane_rows(b, False, cy), near + 1)
        arrive(plane_rows(b, True, cx), far)
        arrive(plane_rows(b, False, cd), near + 2)
        arrive(plane_rows(b, True, cd), far + 2)

    seg_base = new("r", 2)
    for i, (src, dst) in enumerate(((seg, seg_all), (par, par_all))):
        send(src, dst.at[k], seg_base + i, 2 * c + 1 - k, t)
        dst[pl.ds(k, 1)] = src[...][None]
    def tree_send(src, dst):
        base = new("r", 4)
        for s in range(2):
            for h in range(2):
                send_or_copy(src.at[s, pl.ds(h * piece, piece), :], dst(h), base + t, 2 * c + h, 2 * k + s)
        return base

    za = z_own(A_BLK, ash)
    zb = z_own(B_BLK, wup)
    tok_base = tree_send(tok, lambda h: X.at[rows_at(h * half + t * piece, piece), :])

    arrive(seg_all.at[1 - k], seg_base)
    arrive(par_all.at[1 - k], seg_base + 1)
    lane1 = lax.broadcasted_iota(jnp.int32, (1, 128), 1)
    both = par_all[pl.ds(home, 1)][0]
    second = lax.rem(t, 2) == 1
    parents = jnp.where(second, both[1:2, :], both[0:1, :])
    par_of = [jnp.broadcast_to(parents[:, j : j + 1], (1, 128)) for j in range(SEGS)]
    reach_rows = []
    for s in range(SEGS):
        now = jnp.full((1, 128), s, jnp.int32)
        seen = lane1 == s
        for _ in range(SEGS - 1):
            now = functools.reduce(lambda acc, j: jnp.where(now == j, par_of[j], acc), range(SEGS), now)
            seen = jnp.logical_or(seen, lane1 == now)
        reach_rows.append(jnp.where(lane1 < SEGS, jnp.where(seen, 0.0, FILL), 0.0))
    lane_f = lax.broadcasted_iota(jnp.int32, (piece, 128), 1).astype(F32)
    for h in range(2):
        for q in range(ranks):
            both = seg_all[pl.ds(home, 1), :, pl.ds((2 * q + h) * piece, piece)][0].astype(F32)
            part = jnp.where(second, both[1:2, :], both[0:1, :])
            segs = jnp.broadcast_to(part, (piece, piece)).T
            rows = pl.ds(h * half + q * piece, piece)
            table = jnp.zeros((piece, 128), F32)
            for s in range(SEGS):
                table = jnp.where(segs == s, jnp.broadcast_to(reach_rows[s], (piece, 128)), table)
            rf[rows, :] = table.astype(BF)
            hot = jnp.where(lane_f < SEGS, jnp.where(segs == lane_f, 1.0, 0.0), jnp.where(lane_f < SEGS + 3, 1.0, 0.0))
            kf[rows, :] = hot.astype(BF)

    z_near(A_BLK, za)
    z_far(A_BLK, za)
    pa = plane_send(A_BLK)
    z_near(B_BLK, zb)
    z_far(B_BLK, zb)
    plane_forward(A_BLK, *pa)
    pb = plane_send(B_BLK)
    zc = z_own(C_BLK, wdown)
    fwd_base = new("r", 4)
    for j in range(ranks):
        q = lax.rem(t + j, ranks)
        mine = X.at[rows_at(here + q * piece, piece), :]
        arrive(mine, tok_base + q)
        send(mine, mine, fwd_base + q, 2 * c + 1 - k, t)
    plane_wait(A_BLK, *pa)

    def half_lanes(ref):
        row = ref[...][None, :]
        return jnp.where(k == 0, row[:, : width // 2], row[:, width // 2 :])

    bq2, bv2 = half_lanes(bq), half_lanes(bv)
    zero64 = jnp.zeros((1, HD), F32)
    biases = []
    for tt in range(2):
        lo = 192 * tt
        biases.append((bq2[:, lo : lo + 128], bv2[:, lo : lo + 128],
                       jnp.concatenate([bq2[:, lo + 128 : lo + 192], zero64], axis=1),
                       jnp.concatenate([bv2[:, lo + 128 : lo + 192], zero64], axis=1)))
    eighth = jnp.asarray(0.125, BF)

    def project(start):
        def run(i, _):
            rows = rows_at(start + i * ROW_BLOCK, ROW_BLOCK)
            xb = X[rows, :]
            for tt in range(2):
                m = dot(xb, W[A_BLK, tt, :, 0:640])
                b_q01, b_v01, b_q2, b_v2 = biases[tt]
                base = 6 * tt
                q3 = m[:, 384:512] + b_q2
                v3 = m[:, 512:640] + b_v2
                tiles[base, rows, :] = (m[:, 0:128] + b_q01).astype(BF) * eighth
                tiles[base + 1, rows, :] = m[:, 128:256].astype(BF)
                tiles[base + 2, rows, :] = (m[:, 256:384] + b_v01).astype(BF)
                tiles[base + 3, rows, :] = q3.astype(BF) * eighth
                tiles[base + 4, rows, :] = pltpu.roll(q3, 64, 1).astype(BF)
                tiles[base + 5, rows, :] = pltpu.roll(v3, 64, 1).astype(BF)
            return 0

        lax.fori_loop(0, half // ROW_BLOCK, run, 0)

    project(here)
    plane_forward(B_BLK, *pb)
    for q in range(ranks):
        arrive(X.at[rows_at(there + q * piece, piece), :], fwd_base + q)
    project(there)

    ones = jnp.ones((length, 128), BF)

    def attend_all(tt, lo, hi):
        base = 6 * tt

        def attend(i, _):
            rows = rows_at(i * FORWARD_BLOCK, FORWARD_BLOCK)
            rfb = rf[rows, :]
            parts = []

            def score(h):
                qi, ki, _, qh, _ = HALF_HEADS[h]
                qt = tiles[base + qi, rows, :]
                qm = jnp.where(lane_mask(qt.shape, qh), qt, jnp.zeros_like(qt))
                return dot(jnp.concatenate([qm, rfb], axis=1), jnp.concatenate([tiles[base + ki], kf[...]], axis=1), 1, 1)

            def soften(s):
                top = jnp.max(s, axis=1, keepdims=True)
                return top, jnp.exp(s - top).astype(BF)

            def mix_values(h, top, p):
                vi, vh = HALF_HEADS[h][2], HALF_HEADS[h][4]
                o = dot(p, jnp.concatenate([tiles[base + vi], ones], axis=1))
                total = o[:, 128:129]
                parts.append(jnp.where(lane_mask((FORWARD_BLOCK, 128), vh), o[:, :128] / total, 0.0))
                lse = top + jnp.log(total)
                raug[3 * tt + h, rows, :] = rfb + pieces(-lse, (FORWARD_BLOCK, 128)).astype(BF)

            s0 = score(0)
            s1 = score(1)
            e0 = soften(s0)
            s2 = score(2)
            mix_values(0, *e0)
            e1 = soften(s1)
            mix_values(1, *e1)
            e2 = soften(s2)
            mix_values(2, *e2)
            ctx[tt, rows, 0:128] = parts[2].astype(BF)
            ctx[tt, rows, 128:256] = (parts[0] + parts[1]).astype(BF)
            return 0

        lax.fori_loop(lo, hi, attend, 0)

    blocks = length // FORWARD_BLOCK
    attend_all(0, 0, blocks // 2)
    z_near(C_BLK, zc)
    z_far(C_BLK, zc)
    pc = plane_send(C_BLK)
    cot_base = tree_send(cot_in, lambda h: dW.at[A_BLK, 0, rows_at(t * piece, piece), :])
    attend_all(0, blocks // 2, blocks)
    attend_all(1, 0, blocks)
    plane_forward(C_BLK, *pc)

    exchanged = []

    def exchange(compute, index):
        blocks = half // ROW_BLOCK
        r_base, s_base = new("r", blocks), new("s", blocks)
        if len(exchanged) >= 2:
            for entry in exchanged[-2]:
                pending[:] = [e for e in pending if e is not entry]
                settle(entry)

        def copy_of(i):
            rows = rows_at(i * ROW_BLOCK, ROW_BLOCK)
            return remote(sbuf.at[index, rows, :], rbuf.at[index, rows, :], s_base + i, r_base + i, 2 * c + 1 - k, t)

        def give(i, _):
            sbuf[index, rows_at(i * ROW_BLOCK, ROW_BLOCK), :] = compute(
                rows_at(there + i * ROW_BLOCK, ROW_BLOCK)).astype(BF)
            copy_of(i).start()
            return 0

        lax.fori_loop(0, blocks, give, 0)
        entries = [(None, copy_of(i)) for i in range(blocks)]
        exchanged.append(entries)
        pending.extend(entries)

        def keep(i, _):
            own[rows_at(i * ROW_BLOCK, ROW_BLOCK), :] = compute(rows_at(here + i * ROW_BLOCK, ROW_BLOCK))
            return 0

        lax.fori_loop(0, blocks, keep, 0)

        def ready(i):
            per = ROW_BLOCK // piece

            @pl.when(lax.rem(i, per) == 0)
            def _():
                arrive(rbuf.at[index, rows_at(i * piece, ROW_BLOCK, piece), :], r_base + i // per)

        return ready

    def over_pieces(step, buffer):
        base = new("r", ranks)
        s_base = new("s", ranks)
        def one(i, _):
            rows = rows_at(i * piece, piece)
            full = rows_at(here + i * piece, piece)
            buffer[full, :] = step(rows, i)
            remote(buffer.at[full, :], buffer.at[full, :], s_base + i, base + i, 2 * c + 1 - k, t).start()
            return 0
        lax.fori_loop(0, ranks, one, 0)
        for i in range(ranks):
            full = rows_at(here + i * piece, piece)
            pending.append((None, remote(buffer.at[full, :], buffer.at[full, :], s_base + i, base + i, 2 * c + 1 - k, t)))
        return base

    def wait_pieces(buffer, base):
        for i in range(ranks):
            arrive(buffer.at[rows_at(there + i * piece, piece), :], base + i)

    ra = exchange(lambda rows: dot(ctx[0, rows, :], W[A_BLK, 0, :, 512:768], 1, 1)
                  + dot(ctx[1, rows, :], W[A_BLK, 1, :, 512:768], 1, 1), 0)

    def norm_one(rows, i):
        ra(i)
        x_rows = X[rows_at(here + rows.start, piece), :].astype(F32)
        z = x_rows + own[rows, :] + rbuf[0, rows, :].astype(F32) + row_of['bout']
        center = z - row_mean(z)
        inverse = lax.rsqrt(row_mean(center * center) + epsilon)
        normed = center * inverse
        n1[rows, :] = normed
        r1[rows, :] = jnp.broadcast_to(inverse, (piece, 128))
        return (normed * row_of['g1'] + row_of['s1']).astype(BF)

    hb = over_pieces(norm_one, H)
    plane_wait(B_BLK, *pb)

    up_row = bup[...][None, :]
    up_bias = [jnp.where(k == 0, up_row[:, tt * width : (tt + 1) * width],
                         up_row[:, (2 + tt) * width : (3 + tt) * width]) for tt in range(2)]

    def up(start):
        def run(i, _):
            rows = rows_at(start + i * ROW_BLOCK, ROW_BLOCK)
            for tt in range(2):
                bias = up_bias[tt]
                value, slope = gelu_pair(dot(H[rows, :], W[B_BLK, tt]) + bias)
                act[tt, rows, :] = value.astype(BF)
                gp[tt, rows, :] = slope.astype(BF)
            return 0

        lax.fori_loop(0, half // ROW_BLOCK, run, 0)

    up(here)
    wait_pieces(H, hb)
    up(there)
    plane_wait(C_BLK, *pc)
    rb = exchange(lambda rows: dot(act[0, rows, :], W[C_BLK, 0], 1, 1) + dot(act[1, rows, :], W[C_BLK, 1], 1, 1), 1)
    for q in range(ranks):
        arrive(dW.at[A_BLK, 0, pl.ds(q * piece, piece), :], cot_base + q)
    def piece_back(i, target, r_base, s_base):
        return remote(obuf.at[rows_at(i * piece, piece), :],
                      target.at[lax.rem(t, 2), rows_at(k * piece, piece), :],
                      s_base + i, r_base + lax.rem(t, 2) * 2 + k, 2 * c + home, i)

    def give_back(i, target, r_base, s_base):
        cp = piece_back(i, target, r_base, s_base)
        mine = jnp.logical_and(home == k, t == i)

        @pl.when(mine)
        def _():
            pltpu.make_async_copy(obuf.at[rows_at(i * piece, piece), :],
                                  target.at[lax.rem(t, 2), rows_at(k * piece, piece), :],
                                  rsem.at[r_base + lax.rem(t, 2) * 2 + k]).start()

        @pl.when(jnp.logical_not(mine))
        def _():
            cp.start()

    def given(target, r_base, s_base):
        return [(jnp.logical_and(home == k, t == i), piece_back(i, target, r_base, s_base)) for i in range(ranks)]

    out_base, out_sends = new("r", 4), new("s", ranks)
    vec[...] = jnp.zeros_like(vec)

    def col_add(row, v):
        vec[row : row + 1, :] = vec[row : row + 1, :] + jnp.sum(v, axis=0, keepdims=True)

    def norm_two(rows, i):
        rb(i)
        z = n1[rows, :] * row_of['g1'] + row_of['s1'] + own[rows, :] + rbuf[1, rows, :].astype(F32) + row_of['bdown']
        center = z - row_mean(z)
        inverse = lax.rsqrt(row_mean(center * center) + epsilon)
        normed = center * inverse
        obuf[rows, :] = (normed * row_of['g2'] + row_of['s2']).astype(BF)
        give_back(i, out, out_base, out_sends)
        g = dW[A_BLK, 0, rows, :].astype(F32)
        col_add(0, g * normed)
        col_add(1, g)
        gg = g * row_of['g2']
        back = inverse * (gg - row_mean(gg) - normed * row_mean(gg * normed))
        col_add(2, back)
        mix[rows, :] = back
        return back.astype(BF)

    g2b = over_pieces(norm_two, G2)
    out_entries = given(out, out_base, out_sends)
    pending.extend(out_entries)

    def transpose_half(src, start):
        def run(i, _):
            rows = rows_at(start + i * piece, piece)
            tbuf[:, rows] = src[rows, :].astype(F32).T.astype(BF)
            return 0

        lax.fori_loop(0, half // piece, run, 0)

    def transpose_into(src):
        transpose_half(src, 0)
        transpose_half(src, half)

    def grad_rows(part, chip, kk):
        b, tt, lo, hi = part
        return dW.at[b, tt, rows_at(chip * pair + kk * shard, shard), lo:hi]

    def reduce_one(part):
        b, tt, lo, hi = part
        base = new("r", 4)
        for i, chip in enumerate((cd, cy)):
            send(grad_rows(part, chip, 0), rs1.at[b, tt, 0, i, :, lo:hi], base + i, 2 * cy + k, t)
        for i, chip in enumerate((cd, cx)):
            send(grad_rows(part, chip, 1), rs1.at[b, tt, 1, i, :, lo:hi], base + 2 + i, 2 * cx + k, t)
        return part, base

    def add_rows(part, chip, kk, received):
        b, tt, lo, hi = part
        rows = rows_at(chip * pair + kk * shard, shard)
        dW[b, tt, rows, lo:hi] = (dW[b, tt, rows, lo:hi].astype(F32) + received.astype(F32)).astype(BF)

    def reduce_two(state):
        part, base = state
        b, tt, lo, hi = part
        nxt = new("r", 2)
        for kk, other in ((0, cx), (1, cy)):
            arrive(rs1.at[b, tt, kk, 0, :, lo:hi], base + 2 * kk)
            add_rows(part, other, kk, rs1[b, tt, kk, 0, :, lo:hi])
            send(grad_rows(part, other, kk), rs2.at[b, tt, kk, :, lo:hi], nxt + kk, 2 * other + k, t)
        for kk in range(2):
            arrive(rs1.at[b, tt, kk, 1, :, lo:hi], base + 2 * kk + 1)
            add_rows(part, c, kk, rs1[b, tt, kk, 1, :, lo:hi])
        return part, nxt

    outer = t == (ranks - 1) * (1 - k)
    joiner = t == 1 + (1 - k)
    inward = t + 2 * k - 1
    z_bases = {}

    def reduce_join(state):
        part, nxt = state
        b, tt, lo, hi = part
        base = new("r", 2)
        for kk in range(2):
            arrive(rs2.at[b, tt, kk, :, lo:hi], nxt + kk)
            add_rows(part, c, kk, rs2[b, tt, kk, :, lo:hi])
            send_if(outer, grad_rows(part, c, kk), rs3.at[b, tt, kk, :, lo:hi], base + kk, d,
                    lax.rem(inward + ranks, ranks))
        return part, base

    def reduce_z(state):
        part, base = state
        b, tt, lo, hi = part
        if (b, lo) not in z_bases:
            z_bases[(b, lo)] = new("r", 3)
        z_base = z_bases[(b, lo)]
        for kk in range(2):
            @pl.when(joiner)
            def _(kk=kk):
                arrive(rs3.at[b, tt, kk, :, lo:hi], base + kk)
                add_rows(part, c, kk, rs3[b, tt, kk, :, lo:hi])

            from_slot = lax.rem(t - k + ranks, ranks)
            target = zbuf.at[b, jnp.minimum(from_slot, 2), :, lo:hi]
            cp = remote(grad_rows(part, c, kk), target, new("s"), z_base + jnp.minimum(from_slot, 2),
                        2 * c + kk, 2 * k + tt)
            mine = jnp.logical_and(kk == k, t == 2 * k + tt)

            @pl.when(mine)
            def _(kk=kk):
                pltpu.make_async_copy(grad_rows(part, c, kk), target,
                                      rsem.at[z_base + jnp.minimum(from_slot, 2)]).start()

            away = jnp.logical_and(jnp.logical_not(mine), jnp.logical_not(outer))

            @pl.when(away)
            def _(cp=cp):
                cp.start()

            pending.append((jnp.logical_not(away), cp))

    def reduce_end(b):
        for (blk, lo), base in z_bases.items():
            if blk == b:
                hi = lo + (width if (b, width // 2) not in z_bases else width // 2)
                for q in range(3):
                    arrive(zbuf.at[b, q, :, lo:hi], base + q)
        total = zbuf[b, 0].astype(F32)
        for q in range(1, 3):
            total = total + zbuf[b, q].astype(F32)
        return total

    def grad_matmul(b, tt, right):
        def run(i, _):
            rows = rows_at(i * ROW_BLOCK, ROW_BLOCK)
            dW[b, tt, rows, :] = dot(tbuf[rows, :], right[tt]).astype(BF)
            return 0

        lax.fori_loop(0, width // ROW_BLOCK, run, 0)

    transpose_half(G2, here)
    wait_pieces(G2, g2b)
    transpose_half(G2, there)
    grad_matmul(C_BLK, 0, act)
    rc0 = reduce_one((C_BLK, 0, 0, width))
    grad_matmul(C_BLK, 1, act)
    rc1 = reduce_one((C_BLK, 1, 0, width))

    def back_up(i, _):
        rows = rows_at(i * ROW_BLOCK, ROW_BLOCK)
        for tt in range(2):
            gi = (dot(G2[rows, :], W[C_BLK, tt]) * gp[tt, rows, :].astype(F32)).astype(BF)
            gp[tt, rows, :] = gi
            row = 6 + 2 * k + tt
            vec[pl.ds(row, 1), :] = vec[pl.ds(row, 1), :] + jnp.sum(gi.astype(F32), axis=0, keepdims=True)
        return 0

    lax.fori_loop(0, length // ROW_BLOCK, back_up, 0)
    rh = exchange(lambda rows: dot(gp[0, rows, :], W[B_BLK, 0], 1, 1) + dot(gp[1, rows, :], W[B_BLK, 1], 1, 1), 0)
    transpose_into(H)

    def norm_one_back(rows, i):
        rh(i)
        grad = mix[rows, :] + own[rows, :] + rbuf[0, rows, :].astype(F32)
        normed = n1[rows, :]
        col_add(3, grad * normed)
        col_add(4, grad)
        hh = grad * row_of['g1']
        back = r1[rows, 0:1] * (hh - row_mean(hh) - normed * row_mean(hh * normed))
        col_add(5, back)
        mix[rows, :] = back
        return back.astype(BF)

    g1b = over_pieces(norm_one_back, G1)
    grad_matmul(B_BLK, 0, gp)
    sc0 = reduce_two(rc0)
    rb0 = reduce_one((B_BLK, 0, 0, width))
    grad_matmul(B_BLK, 1, gp)
    sc1 = reduce_two(rc1)
    rb1 = reduce_one((B_BLK, 1, 0, width))

    def back_context(start):
        def run(i, _):
            rows = rows_at(start + i * ROW_BLOCK, ROW_BLOCK)
            for tt in range(2):
                dctx[tt, rows, :] = dot(G1[rows, :], W[A_BLK, tt, :, 512:768]).astype(BF)
            return 0

        lax.fori_loop(0, half // ROW_BLOCK, run, 0)

    back_context(here)
    wait_pieces(G1, g1b)
    back_context(there)
    transpose_into(G1)

    def out_matmul(i, _):
        rows = rows_at(i * ROW_BLOCK, ROW_BLOCK)
        for tt in range(2):
            dW[A_BLK, tt, rows, 512:768] = dot(tbuf[rows, :], ctx[tt]).astype(BF)
        return 0

    lax.fori_loop(0, width // ROW_BLOCK, out_matmul, 0)
    transpose_into(X)

    grads = act

    def attend_back(tt, g, lo=0, hi=length // BACKWARD_BLOCK):
        base = 6 * tt
        heads = HALF_HEADS[0:2] if g == 0 else HALF_HEADS[2:3]
        lanes = slice(128, 256) if g == 0 else slice(0, 128)
        if lo == 0:
            dkv[...] = jnp.zeros_like(dkv)
        ki, vi = heads[0][1], heads[0][2]
        k_t = tiles[base + ki].astype(F32).T
        row = lax.broadcasted_iota(jnp.int32, k_t.shape, 0)
        k_masks = [jnp.where((row < HD) if hd[3] == 0 else (row >= HD), k_t, 0.0).astype(BF) for hd in heads]

        def back(i, _):
            rows = rows_at(i * BACKWARD_BLOCK, BACKWARD_BLOCK)
            dq_t = jnp.zeros((128, BACKWARD_BLOCK), F32)
            do = dctx[tt, rows, lanes]
            prod = do.astype(F32) * ctx[tt, rows, lanes].astype(F32)
            for h, (qi, _, _, qh, vh) in enumerate(heads):
                qt = tiles[base + qi, rows, :]
                qm = jnp.where(lane_mask(qt.shape, qh), qt, jnp.zeros_like(qt))
                qa = jnp.concatenate([qm, raug[3 * tt + 2 * g + h, rows, :]], axis=1)
                pt = jnp.exp(dot(jnp.concatenate([tiles[base + ki], kf[...]], axis=1), qa, 1, 1))
                vmask = lane_mask(do.shape, vh)
                dom = jnp.where(vmask, do, jnp.zeros_like(do))
                delta = jnp.sum(jnp.where(vmask, prod, 0.0), axis=1, keepdims=True)
                doa = jnp.concatenate([dom, pieces(-delta, do.shape).astype(BF)], axis=1)
                dst = (pt * dot(jnp.concatenate([tiles[base + vi], kf[...]], axis=1), doa, 1, 1)).astype(BF)
                dkv[1] += dot(pt.astype(BF), dom)
                dkv[0] += dot(dst, qm)
                dq_t = dq_t + dot(k_masks[h], dst)
            dq = (dq_t.T * 0.125).astype(BF)
            if g == 0:
                grads[tt, rows, 0:128] = dq
            else:
                grads[tt, rows, 384:512] = dq
            return 0

        lax.fori_loop(lo, hi, back, 0)
        if hi < length // BACKWARD_BLOCK:
            return
        if g == 0:
            grads[tt, :, 128:256] = dkv[0].astype(BF)
            grads[tt, :, 256:384] = dkv[1].astype(BF)
        else:
            grads[tt, :, 384:512] = grads[tt, :, 384:512] + pltpu.roll(dkv[0], 64, 1).astype(BF)
            grads[tt, :, 512:640] = pltpu.roll(dkv[1], 64, 1).astype(BF)

    mid = width // 2

    def qkv_matmul(tt, part):
        low = lax.broadcasted_iota(jnp.int32, (ROW_BLOCK, 128), 1) < HD

        def run(i, _):
            rows = rows_at(i * ROW_BLOCK, ROW_BLOCK)
            if part == 0:
                dW[A_BLK, tt, rows, 0:384] = dot(tbuf[rows, :], grads[tt, :, 0:384]).astype(BF)
            else:
                g = dot(tbuf[rows, :], grads[tt, :, 384:640]).astype(BF)
                dW[A_BLK, tt, rows, 384:512] = g[:, 0:128]
                kept = dW[A_BLK, tt, rows, 512:640]
                dW[A_BLK, tt, rows, 512:640] = jnp.where(low, g[:, 128:256], kept)
            return 0

        lax.fori_loop(0, width // ROW_BLOCK, run, 0)
        row = 10 + 2 * k + tt
        lanes = slice(0, 384) if part == 0 else slice(384, 640)
        vec[pl.ds(row, 1), lanes] = jnp.sum(grads[tt, :, lanes].astype(F32), axis=0, keepdims=True)
        return reduce_one((A_BLK, tt, part * mid, part * mid + mid))

    blocks = length // BACKWARD_BLOCK
    attend_back(0, 0)
    ra00 = qkv_matmul(0, 0)
    jc0 = reduce_join(sc0)
    jc1 = reduce_join(sc1)
    sb0 = reduce_two(rb0)
    reduce_z(jc0)
    attend_back(0, 1)
    ra01 = qkv_matmul(0, 1)
    sb1 = reduce_two(rb1)
    reduce_z(jc1)
    attend_back(1, 0, 0, blocks // 2)
    jb0 = reduce_join(sb0)
    sa00 = reduce_two(ra00)
    attend_back(1, 0, blocks // 2, blocks)
    ra10 = qkv_matmul(1, 0)
    jb1 = reduce_join(sb1)
    reduce_z(jb0)
    sa01 = reduce_two(ra01)
    attend_back(1, 1)
    ra11 = qkv_matmul(1, 1)
    ja00 = reduce_join(sa00)
    reduce_z(jb1)

    v_base = new("r", 8)
    send(vec, vrecv.at[0], v_base, 2 * c + 1 - k, t)
    ja01 = reduce_join(sa01)
    sa10 = reduce_two(ra10)
    my_rows = pl.ds(pl.multiple_of(8 * k, 8), 8)
    arrive(vrecv.at[0], v_base)
    chip_total = vrecv.at[1]
    chip_total[...] = vec[...] + vrecv[0]
    vgather[pl.ds(t, 1)] = chip_total[my_rows, :][None]
    for j in range(1, ranks):
        send(chip_total.at[my_rows, :], vgather.at[t], v_base + 1 + t, d, lax.rem(t + j, ranks))
    reduce_z(ja00)
    rx = exchange(lambda rows: dot(grads[0, rows, 0:640], W[A_BLK, 0, :, 0:640], 1, 1)
                  + dot(grads[1, rows, 0:640], W[A_BLK, 1, :, 0:640], 1, 1), 1)
    for s in range(2):
        for h in range(2):
            arrive(out.at[s, pl.ds(h * piece, piece), :], out_base + 2 * s + h)
    for entry in out_entries:
        pending[:] = [e for e in pending if e is not entry]
        settle(entry)
    reduce_z(ja01)
    ja10 = reduce_join(sa10)
    dx_base, dx_sends = new("r", 4), new("s", ranks)

    def finish(i, _):
        rx(i)
        rows = rows_at(i * piece, piece)
        obuf[rows, :] = (mix[rows, :] + own[rows, :] + rbuf[1, rows, :].astype(F32)).astype(BF)
        give_back(i, dxr, dx_base, dx_sends)
        return 0

    lax.fori_loop(0, ranks, finish, 0)
    pending.extend(given(dxr, dx_base, dx_sends))
    sa11 = reduce_two(ra11)
    ja11 = reduce_join(sa11)
    gc_out[...] = reduce_end(C_BLK)
    gb_out[...] = reduce_end(B_BLK)

    for j in range(1, ranks):
        src = lax.rem(t + j, ranks)
        arrive(vgather.at[src], v_base + 1 + src)
    total = vgather[0]
    for j in range(1, ranks):
        total = total + vgather[j]
    vgather[4] = total
    send(vgather.at[4], vgather.at[5], v_base + 5, 2 * cx + k, t)
    reduce_z(ja10)
    arrive(vgather.at[5], v_base + 5)
    total = total + vgather[5]
    vgather[6] = total
    send(vgather.at[6], vgather.at[7], v_base + 6, 2 * cy + k, t)
    reduce_z(ja11)
    arrive(vgather.at[7], v_base + 6)
    final = vrecv.at[2]
    final[my_rows, :] = total + vgather[7]
    send(final.at[my_rows, :], final.at[my_rows, :], v_base + 7, 2 * c + 1 - k, t)
    for s in range(2):
        for h in range(2):
            arrive(dxr.at[s, pl.ds(h * piece, piece), :], dx_base + 2 * s + h)
    ga_out[...] = reduce_end(A_BLK)
    arrive(final.at[pl.ds(pl.multiple_of(8 * (1 - k), 8), 8), :], v_base + 7)
    vec_out[...] = final[...]
    for entry in pending:
        settle(entry)


def fused_layer(tokens, cotangent, parents, segment_ids, w_qkv, w_out, w_up, w_down, vectors):
    local, quarter, width = tokens.shape
    length = segment_ids.shape[1]
    half = length // 2
    shard = w_qkv.shape[1]
    vm = pl.BlockSpec(memory_space=pltpu.VMEM)
    anywhere = pl.BlockSpec(memory_space=pl.ANY)
    rows = list(vectors)
    sems = 224
    return pl.pallas_call(
        layer_kernel,
        name="layer",
        out_shape=(
            jax.ShapeDtypeStruct(tokens.shape, BF),
            jax.ShapeDtypeStruct(tokens.shape, BF),
            jax.ShapeDtypeStruct((shard, width), F32),
            jax.ShapeDtypeStruct((shard, width), F32),
            jax.ShapeDtypeStruct((shard, width), F32),
            jax.ShapeDtypeStruct((16, width), F32),
        ),
        in_specs=[anywhere, anywhere, vm, vm, vm, vm, anywhere, anywhere] + [vm] * len(rows),
        out_specs=(anywhere, anywhere, vm, vm, vm, vm),
        scratch_shapes=[
            pltpu.VMEM((3, 2, width, width), BF),
            pltpu.VMEM((length, width), BF),
            pltpu.VMEM((12, length, 128), BF),
            pltpu.VMEM((2, length, 256), BF),
            pltpu.VMEM((6, length, 128), BF),
            pltpu.VMEM((length, 128), BF),
            pltpu.VMEM((length, 128), BF),
            pltpu.VMEM((half, width), F32),
            pltpu.VMEM((half, 128), F32),
            pltpu.VMEM((length, width), BF),
            pltpu.VMEM((2, length, width), BF),
            pltpu.VMEM((2, length, width), BF),
            pltpu.VMEM((half, width), F32),
            pltpu.VMEM((length, width), BF),
            pltpu.VMEM((length, width), BF),
            pltpu.VMEM((2, length, 256), BF),
            pltpu.VMEM((half, width), F32),
            pltpu.VMEM((2, half, width), BF),
            pltpu.VMEM((2, half, width), BF),
            pltpu.VMEM((half, width), BF),
            pltpu.VMEM((3, 2, width, width), BF),
            pltpu.VMEM((3, 2, 2, 2, shard, width), BF),
            pltpu.VMEM((3, 2, 2, shard, width), BF),
            pltpu.VMEM((3, 2, 2, shard, width), BF),
            pltpu.VMEM((3, 3, shard, width), BF),
            pltpu.VMEM((width, length), BF),
            pltpu.VMEM((2, length, 128), F32),
            pltpu.VMEM((shard, width), BF),
            pltpu.VMEM((2,) + segment_ids.shape, jnp.int32),
            pltpu.VMEM((2,) + parents.shape, jnp.int32),
            pltpu.VMEM((16, width), F32),
            pltpu.VMEM((3, 16, width), F32),
            pltpu.VMEM((8, 8, width), F32),
            pltpu.SemaphoreType.DMA((sems,)),
            pltpu.SemaphoreType.DMA((sems,)),
        ],
        compiler_params=pltpu.CompilerParams(collective_id=0, has_side_effects=True, vmem_limit_bytes=63 << 20),
        cost_estimate=pl.CostEstimate(flops=60 * 10**9, bytes_accessed=30 * 10**6, transcendentals=16 * 10**6),
    )(tokens, cotangent, parents, segment_ids, w_qkv, w_out, w_up, w_down, *rows)


def finish_kernel(out, dx_in, ga_in, gb_in, gc_in, vec_in, o_out, o_dx, o_qkv, o_bq, o_bv, o_wout, o_bout, o_g1, o_s1, o_up, o_bup,
                  o_down, o_bdown, o_g2, o_s2, dx, ga, vec, sem):
    copies = [pltpu.make_async_copy(src, dst, sem.at[i]) for i, (src, dst) in enumerate(
        ((dx_in, dx), (ga_in, ga), (vec_in, vec), (out, o_out), (gb_in, o_up), (gc_in, o_down)))]
    for copy in copies:
        copy.start()
    for copy in copies[:3]:
        copy.wait()
    o_dx[...] = dx[...].astype(F32)
    a = ga[...]
    for i, (pair, lo) in enumerate(((0, 384), (128, 448), (256, 512))):
        o_qkv[i] = jnp.concatenate([a[:, pair : pair + 128], a[:, lo : lo + HD]], axis=1)
    o_wout[...] = jnp.concatenate([a[:, 640:768], a[:, 576:640]], axis=1).T
    for ref, row in ((o_g2, 0), (o_s2, 1), (o_bdown, 2), (o_g1, 3), (o_s1, 4), (o_bout, 5)):
        ref[...] = vec[row, :]
    width = vec.shape[1]
    for i in range(4):
        o_bup[i * width : (i + 1) * width] = vec[6 + i, :]
    for ref, pair, lo in ((o_bq, 0, 384), (o_bv, 256, 512)):
        row = [vec[10 + i : 11 + i, :] for i in range(4)]
        parts = [p for r in row for p in (r[:, pair : pair + 128], r[:, lo : lo + HD])]
        ref[...] = jnp.concatenate(parts, axis=1)[0]
    for copy in copies[3:]:
        copy.wait()


def plane_body(tokens, parents, segment_ids, w_qkv, b_q, b_v, w_out, b_out, gain_one, shift_one,
               w_up, b_up, w_down, b_down, gain_two, shift_two, cotangent):
    raw = fused_layer(
        tokens, cotangent, parents, segment_ids, w_qkv.transpose(1, 0, 2), w_out, w_up, w_down.T,
        (b_q, b_v, b_out, gain_one, shift_one, b_up, b_down, gain_two, shift_two))
    vm = pl.BlockSpec(memory_space=pltpu.VMEM)
    anywhere = pl.BlockSpec(memory_space=pl.ANY)
    shard, kinds, part = w_qkv.shape
    vector = jax.ShapeDtypeStruct(b_q.shape, F32)
    outs = pl.pallas_call(
        finish_kernel,
        name="finish",
        out_shape=(
            jax.ShapeDtypeStruct(tokens.shape, BF),
            jax.ShapeDtypeStruct(tokens.shape, F32),
            jax.ShapeDtypeStruct((kinds, shard, part), F32),
            vector, vector,
            jax.ShapeDtypeStruct(w_out.shape, F32),
            vector, vector, vector,
            jax.ShapeDtypeStruct(w_up.shape, F32),
            jax.ShapeDtypeStruct(b_up.shape, F32),
            jax.ShapeDtypeStruct(w_down.shape[::-1], F32),
            vector, vector, vector,
        ),
        in_specs=[anywhere] * 6,
        out_specs=(vm,) * 15,
        scratch_shapes=[pltpu.VMEM(tokens.shape, BF), pltpu.VMEM((shard, 4 * part), F32), pltpu.VMEM((16, 4 * part), F32),
                        pltpu.SemaphoreType.DMA((6,))],
        compiler_params=pltpu.CompilerParams(vmem_limit_bytes=63 << 20),
    )(*raw)
    return (outs[0], outs[1], outs[2].transpose(1, 0, 2), *outs[3:11], outs[11].T, *outs[12:])


def solution(mesh):
    dp, ranks = mesh.shape["dp"], mesh.shape["tensor"]
    return jax.shard_map(
        plane_body if (dp, ranks) == (8, 4) else functools.partial(body, dp, ranks),
        mesh=mesh,
        in_specs=(P("dp", "tensor", None), P("dp", None), P("dp", None), P("dp", None, "tensor"), P(), P(),
                  P("tensor", "dp"), P(), P(), P(), P("dp", "tensor"), P(), P("tensor", "dp"), P(), P(), P(),
                  P("dp", "tensor", None)),
        out_specs=(P("dp", "tensor", None), P("dp", "tensor", None), P("dp", None, "tensor"), P(), P(),
                   P("tensor", "dp"), P(), P(), P(), P("dp", "tensor"), P(), P("tensor", "dp"), P(), P(), P()),
        check_vma=False,
    )
```

```python
import functools

import jax
import jax.numpy as jnp
from jax import lax
from jax.experimental import pallas as pl
from jax.experimental.pallas import tpu as pltpu
from jax.sharding import PartitionSpec as P

HD = 64
SEGS = 4
epsilon = 1e-12
BF = jnp.bfloat16
F32 = jnp.float32
FILL = -1e30
HALF_HEADS = ((0, 1, 2, 0, 0), (0, 1, 2, 1, 1), (3, 4, 5, 0, 1))


def dot(a, b, ca=1, cb=0):
    return lax.dot_general(a, b, (((ca,), (cb,)), ((), ())), preferred_element_type=F32)


def split3(v):
    hi = v.astype(BF).astype(F32)
    mid = (v - hi).astype(BF).astype(F32)
    low = v - hi - mid
    return hi, mid, low


def lane_mask(shape, half):
    lane = lax.broadcasted_iota(jnp.int32, shape, 1)
    return (lane < HD) if half == 0 else (lane >= HD)


def pieces(v, shape):
    lane = lax.broadcasted_iota(jnp.int32, shape, 1)
    hi, mid, low = split3(v)
    return jnp.where(lane == 4, hi, jnp.where(lane == 5, mid, jnp.where(lane == 6, low, 0.0)))


def attention_forward_kernel(x_ref, a_ref, bias_ref, rf_ref, kf_ref, tiles_ref, ctx_ref, raug_ref):
    length = x_ref.shape[0]
    block = 256
    count = length // block

    def project(i, _):
        rows = pl.ds(pl.multiple_of(i * block, block), block)
        xb = x_ref[rows, :]
        for t in range(2):
            m = dot(xb, a_ref[t, :, : 5 * 128]) + bias_ref[t][:, : 5 * 128]
            base = 6 * t
            q3 = m[:, 3 * 128 : 4 * 128]
            v3 = m[:, 4 * 128 : 5 * 128]
            tiles_ref[base, rows, :] = m[:, :128].astype(BF) * jnp.asarray(0.125, BF)
            tiles_ref[base + 1, rows, :] = m[:, 128:256].astype(BF)
            tiles_ref[base + 2, rows, :] = m[:, 256:384].astype(BF)
            tiles_ref[base + 3, rows, :] = q3.astype(BF) * jnp.asarray(0.125, BF)
            tiles_ref[base + 4, rows, :] = pltpu.roll(q3, 64, 1).astype(BF)
            tiles_ref[base + 5, rows, :] = pltpu.roll(v3, 64, 1).astype(BF)
        return 0

    lax.fori_loop(0, count, project, 0)
    ones = jnp.ones((length, 128), BF)

    for t in range(2):
        base = 6 * t

        def attend(i, _, t=t, base=base):
            rows = pl.ds(pl.multiple_of(i * block, block), block)
            rf = rf_ref[rows, :]
            parts = []
            for h, (qi, ki, vi, qh, vh) in enumerate(HALF_HEADS):
                q = tiles_ref[base + qi, rows, :]
                qm = jnp.where(lane_mask(q.shape, qh), q, jnp.zeros_like(q))
                qq = jnp.concatenate([qm, rf], axis=1)
                kk = jnp.concatenate([tiles_ref[base + ki], kf_ref[...]], axis=1)
                s = dot(qq, kk, 1, 1)
                m = jnp.max(s, axis=1, keepdims=True)
                p = jnp.exp(s - m).astype(BF)
                vv = jnp.concatenate([tiles_ref[base + vi], ones], axis=1)
                o = dot(p, vv)
                total = o[:, 128:129]
                ov = jnp.where(lane_mask((block, 128), vh), o[:, :128] / total, 0.0)
                lse = m + jnp.log(total)
                raug_ref[3 * t + h, rows, :] = rf + pieces(-lse, (block, 128)).astype(BF)
                parts.append(ov)
            ctx_ref[2 * t, rows, :] = (parts[0] + parts[1]).astype(BF)
            ctx_ref[2 * t + 1, rows, :] = parts[2].astype(BF)
            return 0

        lax.fori_loop(0, count, attend, 0)


def attention_backward_kernel(tiles_ref, ctx_ref, dctx_ref, raug_ref, kf_ref, out_ref, dk_ref, dv_ref):
    length = kf_ref.shape[0]
    block = 256
    count = length // block
    groups = ((HALF_HEADS[0], HALF_HEADS[1]), (HALF_HEADS[2],))
    for t in range(2):
        base = 6 * t
        for g, heads in enumerate(groups):
            dk_ref[...] = jnp.zeros_like(dk_ref)
            dv_ref[...] = jnp.zeros_like(dv_ref)
            ki = heads[0][1]
            vi = heads[0][2]
            k_t = tiles_ref[base + ki].astype(F32).T
            row = lax.broadcasted_iota(jnp.int32, k_t.shape, 0)
            k_masks = [
                jnp.where((row < HD) if qh == 0 else (row >= HD), k_t, 0.0).astype(BF)
                for (_, _, _, qh, _) in heads
            ]

            def back(i, _, t=t, base=base, g=g, heads=heads, k_masks=k_masks, ki=ki, vi=vi):
                rows = pl.ds(pl.multiple_of(i * block, block), block)
                dq_t = jnp.zeros((128, block), F32)
                do = dctx_ref[2 * t + g, rows, :]
                prod = do.astype(F32) * ctx_ref[2 * t + g, rows, :].astype(F32)
                for h, (qi, _, _, qh, vh) in enumerate(heads):
                    q = tiles_ref[base + qi, rows, :]
                    qm = jnp.where(lane_mask(q.shape, qh), q, jnp.zeros_like(q))
                    qa = jnp.concatenate([qm, raug_ref[3 * t + 2 * g + h, rows, :]], axis=1)
                    ka = jnp.concatenate([tiles_ref[base + ki], kf_ref[...]], axis=1)
                    pt = jnp.exp(dot(ka, qa, 1, 1))
                    vmask = lane_mask(do.shape, vh)
                    dom = jnp.where(vmask, do, jnp.zeros_like(do))
                    delta = jnp.sum(jnp.where(vmask, prod, 0.0), axis=1, keepdims=True)
                    doa = jnp.concatenate([dom, pieces(-delta, do.shape).astype(BF)], axis=1)
                    va = jnp.concatenate([tiles_ref[base + vi], kf_ref[...]], axis=1)
                    dst = (pt * dot(va, doa, 1, 1)).astype(BF)
                    dv_ref[...] += dot(pt.astype(BF), dom)
                    dk_ref[...] += dot(dst, qm)
                    dq_t = dq_t + dot(k_masks[h], dst)
                dq = dq_t.T * 0.125
                if g == 0:
                    out_ref[t, rows, 0:128] = dq.astype(BF)
                else:
                    out_ref[t, rows, 384:512] = dq.astype(BF)
                return 0

            lax.fori_loop(0, count, back, 0)
            if g == 0:
                out_ref[t, :, 128:256] = dk_ref[...].astype(BF)
                out_ref[t, :, 256:384] = dv_ref[...].astype(BF)
            else:
                out_ref[t, :, 384:512] = out_ref[t, :, 384:512] + pltpu.roll(dk_ref[...], 64, 1).astype(BF)
                out_ref[t, :, 512:640] = pltpu.roll(dv_ref[...], 64, 1).astype(BF)


def attention_forward(x, a, bias, rf, kf):
    length = x.shape[0]
    vm = pl.BlockSpec(memory_space=pltpu.VMEM)
    return pl.pallas_call(
        attention_forward_kernel,
        name="attn_fwd",
        out_shape=(
            jax.ShapeDtypeStruct((12, length, 128), BF),
            jax.ShapeDtypeStruct((4, length, 128), BF),
            jax.ShapeDtypeStruct((6, length, 128), BF),
        ),
        in_specs=[vm] * 5,
        out_specs=(vm,) * 3,
        compiler_params=pltpu.CompilerParams(vmem_limit_bytes=48 << 20),
        cost_estimate=pl.CostEstimate(flops=20 * 10**9, bytes_accessed=10 * 10**6, transcendentals=6 * 10**6),
    )(x, a, bias, rf, kf)


def attention_backward(tiles, ctx, dctx, raug, kf):
    length = kf.shape[0]
    vm = pl.BlockSpec(memory_space=pltpu.VMEM)
    return pl.pallas_call(
        attention_backward_kernel,
        name="attn_bwd",
        out_shape=jax.ShapeDtypeStruct((2, length, 640), BF),
        in_specs=[vm] * 5,
        out_specs=vm,
        scratch_shapes=[pltpu.VMEM((length, 128), F32), pltpu.VMEM((length, 128), F32)],
        compiler_params=pltpu.CompilerParams(vmem_limit_bytes=48 << 20),
        cost_estimate=pl.CostEstimate(flops=40 * 10**9, bytes_accessed=10 * 10**6, transcendentals=6 * 10**6),
    )(tiles, ctx, dctx, raug, kf)


def ancestry(parents):
    labels = jnp.arange(SEGS, dtype=jnp.int32)
    step = (parents[:, None] == labels[None, :]).astype(F32)
    reach = jnp.eye(SEGS, dtype=F32)
    total = reach
    for _ in range(SEGS - 1):
        reach = jnp.sum(reach[:, :, None] * step[None, :, :], axis=1)
        total = total + reach
    return (total > 0.5).astype(F32)


def gelu_parts(u):
    cdf = 0.5 * (1.0 + lax.erf(u * (2.0**-0.5)))
    pdf = jnp.exp(-0.5 * u * u) * ((2.0 * jnp.pi) ** -0.5)
    return u * cdf, cdf + u * pdf


def norm_parts(rows):
    center = rows - jnp.mean(rows, axis=-1, keepdims=True)
    inverse = lax.rsqrt(jnp.mean(center * center, axis=-1, keepdims=True) + epsilon)
    return center * inverse, inverse


def norm_back(grad_rows, normed, inverse, gain):
    scaled = grad_rows * gain
    return inverse * (
        scaled
        - jnp.mean(scaled, axis=-1, keepdims=True)
        - normed * jnp.mean(scaled * normed, axis=-1, keepdims=True)
    )


def body(dp, ranks, tokens, parents, segment_ids, w_qkv, b_q, b_v, w_out, b_out, gain_one, shift_one,
         w_up, b_up, w_down, b_down, gain_two, shift_two, cotangent):
    d = lax.axis_index("dp")
    ti = lax.axis_index("tensor")
    k = d % 2
    local, quarter, width = tokens.shape
    half_rows = quarter // 2
    own_rows = ranks * half_rows
    length = 2 * own_rows
    part = w_qkv.shape[2]
    hidden_part = w_up.shape[1]
    shard = w_qkv.shape[0]
    chips = dp // 2
    same_core = [[i for i in range(dp) if i % 2 == c] for c in range(2)]

    def swap(v):
        return lax.ppermute(v, "dp", [(i, i ^ 1) for i in range(dp)])

    def pick(v, index, axis=0):
        return lax.dynamic_index_in_dim(v, index, axis, keepdims=False)

    def join(own, peer, axis=0):
        return jnp.where(k == 0, jnp.stack([own, peer], axis), jnp.stack([peer, own], axis))

    def to_tree(v):
        v = v.reshape(local, 2, half_rows, width)
        mine = pick(v, k, 1)
        other = swap(pick(v, 1 - k, 1))
        trees = join(mine, other).reshape(ranks, half_rows, width)
        return lax.all_to_all(trees, "tensor", 0, 0, tiled=True).reshape(own_rows, width)

    def from_tree(v):
        v = lax.all_to_all(v.reshape(ranks, half_rows, width), "tensor", 0, 0, tiled=True)
        v = v.reshape(2, local, half_rows, width)
        other = swap(pick(v, 1 - k))
        return join(pick(v, k), other, 1).reshape(local, quarter, width)

    heads = w_qkv.reshape(shard, 3, 3, HD)
    q, kk, vv = heads[:, 0], heads[:, 1], heads[:, 2]
    out_t = w_out.T.reshape(shard, 3, HD)
    packed_a = jnp.concatenate(
        [q[:, 0], q[:, 1], kk[:, 0], kk[:, 1], vv[:, 0], vv[:, 1], q[:, 2], kk[:, 2], vv[:, 2],
         out_t[:, 2], out_t[:, 0], out_t[:, 1]], axis=1)

    def gather_weight(w):
        every = lax.all_gather(w, "tensor", axis=0, tiled=False).reshape(2, 2, shard, w.shape[1])
        mine = pick(every, k)
        other = swap(pick(every, 1 - k))
        both = join(mine, other, 1)
        full = lax.all_gather(both, "dp", axis=0, tiled=False, axis_index_groups=same_core)
        return full.transpose(1, 0, 2, 3, 4).reshape(2, chips * 2 * shard, w.shape[1])

    x_own = to_tree(tokens)
    w_a = gather_weight(packed_a)
    w_b = gather_weight(w_up)
    w_c = gather_weight(w_down.T)
    x = join(x_own, swap(x_own)).reshape(length, width)
    cot_own = to_tree(cotangent)

    seg_peer = swap(segment_ids)
    par_peer = swap(parents)
    all_seg = join(segment_ids, seg_peer).reshape(ranks, -1)
    all_par = join(parents, par_peer).reshape(ranks, -1)
    seg = pick(all_seg, ti).reshape(ranks, 2, half_rows).transpose(1, 0, 2).reshape(length)
    par = pick(all_par, ti)
    labels = jnp.arange(SEGS, dtype=jnp.int32)
    hot = (seg[:, None] == labels[None, :]).astype(F32)
    reach_rows = jnp.sum(hot[:, :, None] * ancestry(par)[None], axis=1)
    rf = jnp.concatenate([FILL * (1.0 - reach_rows), jnp.zeros((length, 124), F32)], axis=1).astype(BF)
    kf = jnp.concatenate([hot, jnp.ones((length, 3), F32), jnp.zeros((length, 121), F32)], axis=1).astype(BF)

    def half_vector(b, size):
        return lax.dynamic_slice_in_dim(b, 2 * k * size, 2 * size).reshape(2, size)

    bq = half_vector(b_q, part)
    bv = half_vector(b_v, part)
    zero64 = jnp.zeros((2, HD), F32)
    bias = jnp.concatenate(
        [bq[:, :128], jnp.zeros((2, 128), F32), bv[:, :128], bq[:, 128:], zero64, bv[:, 128:], zero64,
         jnp.zeros((2, 128), F32)], axis=1)[:, None, :]

    tiles, ctx, raug = attention_forward(x, w_a, bias, rf, kf)

    def exchange(partial):
        partial = partial.reshape(2, own_rows, width)
        received = swap(pick(partial, 1 - k).astype(BF))
        return pick(partial, k) + received.astype(F32)

    def spread_rows(v):
        return join(v, swap(v)).reshape(length, width)

    partial = 0.0
    for t in range(2):
        partial = partial + dot(ctx[2 * t + 1], w_a[t, :, 512:640], 1, 1) + dot(ctx[2 * t], w_a[t, :, 640:768], 1, 1)
    attended = exchange(partial)
    n1, r1 = norm_parts(x_own.astype(F32) + attended + b_out)
    hidden = n1 * gain_one + shift_one
    rows_low = spread_rows(hidden.astype(BF))
    up_bias = half_vector(b_up, hidden_part)
    inner = [dot(rows_low, w_b[t]) + up_bias[t] for t in range(2)]
    acts = [gelu_parts(u) for u in inner]
    activated = [a.astype(BF) for a, _ in acts]
    branch = exchange(sum(dot(activated[t], w_c[t], 1, 1) for t in range(2)))
    n2, r2 = norm_parts(hidden + branch + b_down)
    output = n2 * gain_two + shift_two
    g = cot_own.astype(F32)
    gain_two_part = jnp.sum(g * n2, axis=0)
    shift_two_part = jnp.sum(g, axis=0)
    mix_two = norm_back(g, n2, r2, gain_two)
    b_down_part = jnp.sum(mix_two, axis=0)
    two_rows = spread_rows(mix_two.astype(BF))
    d_c = [dot(two_rows, activated[t], 0, 0) for t in range(2)]
    grad_inner = [(dot(two_rows, w_c[t]) * acts[t][1]).astype(BF) for t in range(2)]
    b_up_part = jnp.concatenate([jnp.sum(v.astype(F32), axis=0) for v in grad_inner])
    d_b = [dot(rows_low, grad_inner[t], 0, 0) for t in range(2)]
    grad_hidden = mix_two + exchange(sum(dot(grad_inner[t], w_b[t], 1, 1) for t in range(2)))
    gain_one_part = jnp.sum(grad_hidden * n1, axis=0)
    shift_one_part = jnp.sum(grad_hidden, axis=0)
    mix_one = norm_back(grad_hidden, n1, r1, gain_one)
    b_out_part = jnp.sum(mix_one, axis=0)
    one_rows = spread_rows(mix_one.astype(BF))
    dctx = jnp.stack(
        [dot(one_rows, w_a[t, :, lo : lo + 128]).astype(BF) for t in range(2) for lo in (640, 512)])
    d_tiles = attention_backward(tiles, ctx, dctx, raug, kf)

    def d_a_of(t):
        qkv = dot(x, d_tiles[t], 0, 0)
        o2 = dot(one_rows, ctx[2 * t + 1], 0, 0)
        o01 = dot(one_rows, ctx[2 * t], 0, 0)
        lane = lax.broadcasted_iota(jnp.int32, o2.shape, 1)
        return jnp.concatenate([qkv[:, :512], jnp.where(lane < HD, qkv[:, 512:], o2), o01], axis=1)

    d_a = [d_a_of(t) for t in range(2)]
    lane_zero = jnp.where(jnp.arange(640) < 576, 1.0, 0.0).astype(BF)
    grad_x = exchange(sum(dot(d_tiles[t] * lane_zero, w_a[t, :, :640], 1, 1) for t in range(2)))
    input_grad = from_tree((mix_one + grad_x).astype(BF)).astype(F32)
    out = from_tree(output.astype(BF))

    def scatter_weight(pair):
        v = jnp.stack([p.astype(BF) for p in pair]).reshape(2, chips, 2, shard, width).transpose(1, 2, 0, 3, 4)
        v = v.reshape(chips * 4 * shard, width)
        v = lax.psum_scatter(v, "dp", scatter_dimension=0, tiled=True, axis_index_groups=same_core)
        v = v.reshape(2, 2, shard, width)
        other = swap(pick(v, 1 - k))
        v = join(pick(v, k), other).reshape(ranks * shard, width)
        return lax.psum_scatter(v, "tensor", scatter_dimension=0, tiled=True).astype(F32)

    g_c = scatter_weight(d_c)
    g_b = scatter_weight(d_b)
    g_a = scatter_weight(d_a)
    blk = [g_a[:, i * HD : (i + 1) * HD] for i in range(12)]
    grad_qkv = jnp.stack(
        [jnp.concatenate([blk[0], blk[1], blk[6]], 1), jnp.concatenate([blk[2], blk[3], blk[7]], 1),
         jnp.concatenate([blk[4], blk[5], blk[8]], 1)], axis=1)
    grad_out = jnp.concatenate([blk[10], blk[11], blk[9]], 1).T

    sums = jnp.sum(d_tiles.astype(F32), axis=1)
    bq_part = jnp.concatenate([sums[:, :128], sums[:, 384:448]], axis=1).reshape(-1)
    bv_part = jnp.concatenate([sums[:, 256:384], sums[:, 512:576]], axis=1).reshape(-1)

    def spread(v, size):
        return lax.dynamic_update_slice_in_dim(jnp.zeros((size,), F32), v, k * v.shape[0], 0)

    summed = lax.psum(
        (spread(bq_part, width), spread(bv_part, width), b_out_part, gain_one_part, shift_one_part,
         spread(b_up_part, b_up.shape[0]), b_down_part, gain_two_part, shift_two_part), ("dp", "tensor"))
    return (out, input_grad, grad_qkv, summed[0], summed[1], grad_out, summed[2], summed[3], summed[4],
            g_b, summed[5], g_c.T, summed[6], summed[7], summed[8])


A_BLK, B_BLK, C_BLK = 0, 1, 2
ROW_BLOCK = 256
FORWARD_BLOCK = 512
BACKWARD_BLOCK = 256


def gelu_pair(u):
    t = 1.0 / (1.0 + (0.3275911 * 2.0**-0.5) * jnp.abs(u))
    bell = jnp.exp(-0.5 * u * u)
    poly = jnp.full_like(t, 0.5 * 1.061405429)
    for coef in (-1.453152027, 1.421413741, -0.284496736, 0.254829592):
        poly = poly * t + 0.5 * coef
    tail = poly * t * bell
    cdf = jnp.where(u > 0.0, 1.0 - tail, tail)
    return u * cdf, cdf + u * (bell * ((2.0 * jnp.pi) ** -0.5))


def row_mean(v):
    return jnp.mean(v, axis=-1, keepdims=True)


def layer_kernel(tok, cot_in, par, seg, wqkv, wout, wup, wdown, bq, bv, bout, g1, s1, bup, bdown, g2, s2,
                 out, dxr, ga_out, gb_out, gc_out, vec_out,
                 W, X, tiles, ctx, raug, rf, kf, n1, r1, H, act, gp, mix, G2, G1, dctx, own,
                 sbuf, rbuf, obuf, dW, rs1, rs2, rs3, zbuf, tbuf, dkv, ash, seg_all, par_all, vec, vrecv, vgather,
                 ssem, rsem):
    row_of = {n: ref[...][None, :] for n, ref in (("bout", bout), ("g1", g1), ("s1", s1), ("bdown", bdown),
                                                  ("g2", g2), ("s2", s2))}
    d = lax.axis_index("dp")
    t = lax.axis_index("tensor")
    k = lax.rem(d, 2)
    c = d // 2
    ranks = 4
    cx = c + 1 - 2 * lax.rem(c, 2)
    cy = lax.rem(c + 2, 4)
    cd = 3 - c
    length = X.shape[0]
    half = length // 2
    piece = half // ranks
    width = X.shape[1]
    shard = ash.shape[0]
    pair = 2 * shard
    home = t // 2
    here = k * half
    there = (1 - k) * half
    counters = {"s": 0, "r": 0}
    pending = []

    def new(kind, n=1):
        base = counters[kind]
        counters[kind] = base + n
        return base

    def remote(src, dst, s, r, dd, tt):
        return pltpu.make_async_remote_copy(
            src_ref=src, dst_ref=dst, send_sem=ssem.at[s], recv_sem=rsem.at[r], device_id=(dd, tt),
            device_id_type=pl.DeviceIdType.MESH)

    def send(src, dst, r, dd, tt):
        cp = remote(src, dst, new("s"), r, dd, tt)
        cp.start()
        pending.append((None, cp))

    def send_or_copy(src, dst, r, dd, tt):
        cp = remote(src, dst, new("s"), r, dd, tt)
        mine = jnp.logical_and(dd == d, tt == t)

        @pl.when(mine)
        def _():
            pltpu.make_async_copy(src, dst, rsem.at[r]).start()

        @pl.when(jnp.logical_not(mine))
        def _():
            cp.start()

        pending.append((mine, cp))

    def settle(entry):
        mine, cp = entry
        if mine is None:
            cp.wait_send()
        else:
            @pl.when(jnp.logical_not(mine))
            def _():
                cp.wait_send()

    def arrive(dst, r):
        pltpu.make_async_copy(dst, dst, rsem.at[r]).wait()

    def rows_at(start, n, align=None):
        return pl.ds(pl.multiple_of(start, align or n), n)

    barrier = pltpu.get_barrier_semaphore()
    partners = [(2 * c + 1 - k, t), (2 * cx + k, t), (2 * cy + k, t)]
    for j in range(1, ranks):
        for core in range(2):
            partners.append((2 * c + core, lax.rem(t + j, ranks)))
    for dev in partners:
        pl.semaphore_signal(barrier, inc=1, device_id=dev, device_id_type=pl.DeviceIdType.MESH)

    q_all = wqkv[0].astype(F32)
    k_all = wqkv[1].astype(F32)
    v_all = wqkv[2].astype(F32)
    o_all = wout[...].astype(F32).T
    ash[:, 0:128] = q_all[:, :128].astype(BF)
    ash[:, 128:256] = k_all[:, :128].astype(BF)
    ash[:, 256:384] = v_all[:, :128].astype(BF)
    ash[:, 384:512] = jnp.concatenate([q_all[:, 128:], k_all[:, 128:]], axis=1).astype(BF)
    ash[:, 512:640] = jnp.concatenate([v_all[:, 128:], o_all[:, 128:]], axis=1).astype(BF)
    ash[:, 640:768] = o_all[:, :128].astype(BF)
    pl.semaphore_wait(barrier, len(partners))

    slot = lax.rem(t, 2) * 2 + k
    step = 1 - 2 * k

    def shard_rows(b, tt, kk):
        return W.at[b, tt, rows_at(c * pair + kk * shard, shard), :]

    def send_if(wanted, src, dst, r, dd, tt):
        cp = remote(src, dst, new("s"), r, dd, tt)

        @pl.when(wanted)
        def _():
            cp.start()

        pending.append((jnp.logical_not(wanted), cp))

    def z_own(b, src):
        base = new("r", 4)
        dst = shard_rows(b, lax.rem(t, 2), k)
        for j in (1, -1, 2, -2):
            inside = jnp.logical_and(t + j >= 0, t + j < ranks)
            send_if(inside, src, dst, base + slot, 2 * c + home, lax.rem(t + j + ranks, ranks))
        send_or_copy(src, dst, base + slot, 2 * c + home, t)
        return base

    def z_near(b, base):
        for kk in range(2):
            arrive(shard_rows(b, 1 - k, kk), base + 2 * (1 - k) + kk)

    def z_far(b, base):
        for kk in range(2):
            rows = shard_rows(b, k, kk)
            arrive(rows, base + 2 * k + kk)
            send_if(t == 2 - k, rows, rows, base + 2 * k + kk, d, lax.rem(t + step + ranks, ranks))

    def plane_rows(b, far, chip):
        return W.at[b, k if far else 1 - k, rows_at(chip * pair, pair), :]

    def plane_send(b):
        near, far = new("r", 3), new("r", 3)
        n_rows, f_rows = plane_rows(b, False, c), plane_rows(b, True, c)
        send(n_rows, n_rows, near, 2 * cx + k, t)
        send(f_rows, f_rows, far + 1, 2 * cy + k, t)
        send(n_rows, n_rows, near + 1, 2 * cy + k, t)
        send(f_rows, f_rows, far, 2 * cx + k, t)
        return near, far

    def plane_forward(b, near, far):
        rows = plane_rows(b, False, cx)
        arrive(rows, near)
        send(rows, rows, near + 2, 2 * cy + k, t)
        rows = plane_rows(b, True, cy)
        arrive(rows, far + 1)
        send(rows, rows, far + 2, 2 * cx + k, t)

    def plane_wait(b, near, far):
        arrive(plane_rows(b, False, cy), near + 1)
        arrive(plane_rows(b, True, cx), far)
        arrive(plane_rows(b, False, cd), near + 2)
        arrive(plane_rows(b, True, cd), far + 2)

    seg_base = new("r", 2)
    for i, (src, dst) in enumerate(((seg, seg_all), (par, par_all))):
        send(src, dst.at[k], seg_base + i, 2 * c + 1 - k, t)
        dst[pl.ds(k, 1)] = src[...][None]
    def tree_send(src, dst):
        base = new("r", 4)
        for s in range(2):
            for h in range(2):
                send_or_copy(src.at[s, pl.ds(h * piece, piece), :], dst(h), base + t, 2 * c + h, 2 * k + s)
        return base

    za = z_own(A_BLK, ash)
    zb = z_own(B_BLK, wup)
    tok_base = tree_send(tok, lambda h: X.at[rows_at(h * half + t * piece, piece), :])

    arrive(seg_all.at[1 - k], seg_base)
    arrive(par_all.at[1 - k], seg_base + 1)
    lane1 = lax.broadcasted_iota(jnp.int32, (1, 128), 1)
    both = par_all[pl.ds(home, 1)][0]
    second = lax.rem(t, 2) == 1
    parents = jnp.where(second, both[1:2, :], both[0:1, :])
    par_of = [jnp.broadcast_to(parents[:, j : j + 1], (1, 128)) for j in range(SEGS)]
    reach_rows = []
    for s in range(SEGS):
        now = jnp.full((1, 128), s, jnp.int32)
        seen = lane1 == s
        for _ in range(SEGS - 1):
            now = functools.reduce(lambda acc, j: jnp.where(now == j, par_of[j], acc), range(SEGS), now)
            seen = jnp.logical_or(seen, lane1 == now)
        reach_rows.append(jnp.where(lane1 < SEGS, jnp.where(seen, 0.0, FILL), 0.0))
    lane_f = lax.broadcasted_iota(jnp.int32, (piece, 128), 1).astype(F32)
    for h in range(2):
        for q in range(ranks):
            both = seg_all[pl.ds(home, 1), :, pl.ds((2 * q + h) * piece, piece)][0].astype(F32)
            part = jnp.where(second, both[1:2, :], both[0:1, :])
            segs = jnp.broadcast_to(part, (piece, piece)).T
            rows = pl.ds(h * half + q * piece, piece)
            table = jnp.zeros((piece, 128), F32)
            for s in range(SEGS):
                table = jnp.where(segs == s, jnp.broadcast_to(reach_rows[s], (piece, 128)), table)
            rf[rows, :] = table.astype(BF)
            hot = jnp.where(lane_f < SEGS, jnp.where(segs == lane_f, 1.0, 0.0), jnp.where(lane_f < SEGS + 3, 1.0, 0.0))
            kf[rows, :] = hot.astype(BF)

    z_near(A_BLK, za)
    z_far(A_BLK, za)
    pa = plane_send(A_BLK)
    z_near(B_BLK, zb)
    z_far(B_BLK, zb)
    plane_forward(A_BLK, *pa)
    pb = plane_send(B_BLK)
    zc = z_own(C_BLK, wdown)
    fwd_base = new("r", 4)
    for j in range(ranks):
        q = lax.rem(t + j, ranks)
        mine = X.at[rows_at(here + q * piece, piece), :]
        arrive(mine, tok_base + q)
        send(mine, mine, fwd_base + q, 2 * c + 1 - k, t)
    plane_wait(A_BLK, *pa)

    def half_lanes(ref):
        row = ref[...][None, :]
        return jnp.where(k == 0, row[:, : width // 2], row[:, width // 2 :])

    bq2, bv2 = half_lanes(bq), half_lanes(bv)
    zero64 = jnp.zeros((1, HD), F32)
    biases = []
    for tt in range(2):
        lo = 192 * tt
        biases.append((bq2[:, lo : lo + 128], bv2[:, lo : lo + 128],
                       jnp.concatenate([bq2[:, lo + 128 : lo + 192], zero64], axis=1),
                       jnp.concatenate([bv2[:, lo + 128 : lo + 192], zero64], axis=1)))
    eighth = jnp.asarray(0.125, BF)

    def project(start):
        def run(i, _):
            rows = rows_at(start + i * ROW_BLOCK, ROW_BLOCK)
            xb = X[rows, :]
            for tt in range(2):
                m = dot(xb, W[A_BLK, tt, :, 0:640])
                b_q01, b_v01, b_q2, b_v2 = biases[tt]
                base = 6 * tt
                q3 = m[:, 384:512] + b_q2
                v3 = m[:, 512:640] + b_v2
                tiles[base, rows, :] = (m[:, 0:128] + b_q01).astype(BF) * eighth
                tiles[base + 1, rows, :] = m[:, 128:256].astype(BF)
                tiles[base + 2, rows, :] = (m[:, 256:384] + b_v01).astype(BF)
                tiles[base + 3, rows, :] = q3.astype(BF) * eighth
                tiles[base + 4, rows, :] = pltpu.roll(q3, 64, 1).astype(BF)
                tiles[base + 5, rows, :] = pltpu.roll(v3, 64, 1).astype(BF)
            return 0

        lax.fori_loop(0, half // ROW_BLOCK, run, 0)

    project(here)
    plane_forward(B_BLK, *pb)
    for q in range(ranks):
        arrive(X.at[rows_at(there + q * piece, piece), :], fwd_base + q)
    project(there)

    ones = jnp.ones((length, 128), BF)

    def attend_all(tt, lo, hi):
        base = 6 * tt

        def attend(i, _):
            rows = rows_at(i * FORWARD_BLOCK, FORWARD_BLOCK)
            rfb = rf[rows, :]
            parts = []

            def score(h):
                qi, ki, _, qh, _ = HALF_HEADS[h]
                qt = tiles[base + qi, rows, :]
                qm = jnp.where(lane_mask(qt.shape, qh), qt, jnp.zeros_like(qt))
                return dot(jnp.concatenate([qm, rfb], axis=1), jnp.concatenate([tiles[base + ki], kf[...]], axis=1), 1, 1)

            def soften(s):
                top = jnp.max(s, axis=1, keepdims=True)
                return top, jnp.exp(s - top).astype(BF)

            def mix_values(h, top, p):
                vi, vh = HALF_HEADS[h][2], HALF_HEADS[h][4]
                o = dot(p, jnp.concatenate([tiles[base + vi], ones], axis=1))
                total = o[:, 128:129]
                parts.append(jnp.where(lane_mask((FORWARD_BLOCK, 128), vh), o[:, :128] / total, 0.0))
                lse = top + jnp.log(total)
                raug[3 * tt + h, rows, :] = rfb + pieces(-lse, (FORWARD_BLOCK, 128)).astype(BF)

            s0 = score(0)
            s1 = score(1)
            e0 = soften(s0)
            s2 = score(2)
            mix_values(0, *e0)
            e1 = soften(s1)
            mix_values(1, *e1)
            e2 = soften(s2)
            mix_values(2, *e2)
            ctx[tt, rows, 0:128] = parts[2].astype(BF)
            ctx[tt, rows, 128:256] = (parts[0] + parts[1]).astype(BF)
            return 0

        lax.fori_loop(lo, hi, attend, 0)

    blocks = length // FORWARD_BLOCK
    attend_all(0, 0, blocks // 2)
    z_near(C_BLK, zc)
    z_far(C_BLK, zc)
    pc = plane_send(C_BLK)
    cot_base = tree_send(cot_in, lambda h: dW.at[A_BLK, 0, rows_at(t * piece, piece), :])
    attend_all(0, blocks // 2, blocks)
    attend_all(1, 0, blocks)
    plane_forward(C_BLK, *pc)

    exchanged = []

    def exchange(compute, index):
        blocks = half // ROW_BLOCK
        r_base, s_base = new("r", blocks), new("s", blocks)
        if len(exchanged) >= 2:
            for entry in exchanged[-2]:
                pending[:] = [e for e in pending if e is not entry]
                settle(entry)

        def copy_of(i):
            rows = rows_at(i * ROW_BLOCK, ROW_BLOCK)
            return remote(sbuf.at[index, rows, :], rbuf.at[index, rows, :], s_base + i, r_base + i, 2 * c + 1 - k, t)

        def give(i, _):
            sbuf[index, rows_at(i * ROW_BLOCK, ROW_BLOCK), :] = compute(
                rows_at(there + i * ROW_BLOCK, ROW_BLOCK)).astype(BF)
            copy_of(i).start()
            return 0

        lax.fori_loop(0, blocks, give, 0)
        entries = [(None, copy_of(i)) for i in range(blocks)]
        exchanged.append(entries)
        pending.extend(entries)

        def keep(i, _):
            own[rows_at(i * ROW_BLOCK, ROW_BLOCK), :] = compute(rows_at(here + i * ROW_BLOCK, ROW_BLOCK))
            return 0

        lax.fori_loop(0, blocks, keep, 0)

        def ready(i):
            per = ROW_BLOCK // piece

            @pl.when(lax.rem(i, per) == 0)
            def _():
                arrive(rbuf.at[index, rows_at(i * piece, ROW_BLOCK, piece), :], r_base + i // per)

        return ready

    def over_pieces(step, buffer):
        base = new("r", ranks)
        s_base = new("s", ranks)
        def one(i, _):
            rows = rows_at(i * piece, piece)
            full = rows_at(here + i * piece, piece)
            buffer[full, :] = step(rows, i)
            remote(buffer.at[full, :], buffer.at[full, :], s_base + i, base + i, 2 * c + 1 - k, t).start()
            return 0
        lax.fori_loop(0, ranks, one, 0)
        for i in range(ranks):
            full = rows_at(here + i * piece, piece)
            pending.append((None, remote(buffer.at[full, :], buffer.at[full, :], s_base + i, base + i, 2 * c + 1 - k, t)))
        return base

    def wait_pieces(buffer, base):
        for i in range(ranks):
            arrive(buffer.at[rows_at(there + i * piece, piece), :], base + i)

    ra = exchange(lambda rows: dot(ctx[0, rows, :], W[A_BLK, 0, :, 512:768], 1, 1)
                  + dot(ctx[1, rows, :], W[A_BLK, 1, :, 512:768], 1, 1), 0)

    def norm_one(rows, i):
        ra(i)
        x_rows = X[rows_at(here + rows.start, piece), :].astype(F32)
        z = x_rows + own[rows, :] + rbuf[0, rows, :].astype(F32) + row_of['bout']
        center = z - row_mean(z)
        inverse = lax.rsqrt(row_mean(center * center) + epsilon)
        normed = center * inverse
        n1[rows, :] = normed
        r1[rows, :] = jnp.broadcast_to(inverse, (piece, 128))
        return (normed * row_of['g1'] + row_of['s1']).astype(BF)

    hb = over_pieces(norm_one, H)
    plane_wait(B_BLK, *pb)

    up_row = bup[...][None, :]
    up_bias = [jnp.where(k == 0, up_row[:, tt * width : (tt + 1) * width],
                         up_row[:, (2 + tt) * width : (3 + tt) * width]) for tt in range(2)]

    def up(start):
        def run(i, _):
            rows = rows_at(start + i * ROW_BLOCK, ROW_BLOCK)
            for tt in range(2):
                bias = up_bias[tt]
                value, slope = gelu_pair(dot(H[rows, :], W[B_BLK, tt]) + bias)
                act[tt, rows, :] = value.astype(BF)
                gp[tt, rows, :] = slope.astype(BF)
            return 0

        lax.fori_loop(0, half // ROW_BLOCK, run, 0)

    up(here)
    wait_pieces(H, hb)
    up(there)
    plane_wait(C_BLK, *pc)
    rb = exchange(lambda rows: dot(act[0, rows, :], W[C_BLK, 0], 1, 1) + dot(act[1, rows, :], W[C_BLK, 1], 1, 1), 1)
    for q in range(ranks):
        arrive(dW.at[A_BLK, 0, pl.ds(q * piece, piece), :], cot_base + q)
    def piece_back(i, target, r_base, s_base):
        return remote(obuf.at[rows_at(i * piece, piece), :],
                      target.at[lax.rem(t, 2), rows_at(k * piece, piece), :],
                      s_base + i, r_base + lax.rem(t, 2) * 2 + k, 2 * c + home, i)

    def give_back(i, target, r_base, s_base):
        cp = piece_back(i, target, r_base, s_base)
        mine = jnp.logical_and(home == k, t == i)

        @pl.when(mine)
        def _():
            pltpu.make_async_copy(obuf.at[rows_at(i * piece, piece), :],
                                  target.at[lax.rem(t, 2), rows_at(k * piece, piece), :],
                                  rsem.at[r_base + lax.rem(t, 2) * 2 + k]).start()

        @pl.when(jnp.logical_not(mine))
        def _():
            cp.start()

    def given(target, r_base, s_base):
        return [(jnp.logical_and(home == k, t == i), piece_back(i, target, r_base, s_base)) for i in range(ranks)]

    out_base, out_sends = new("r", 4), new("s", ranks)
    vec[...] = jnp.zeros_like(vec)

    def col_add(row, v):
        vec[row : row + 1, :] = vec[row : row + 1, :] + jnp.sum(v, axis=0, keepdims=True)

    def norm_two(rows, i):
        rb(i)
        z = n1[rows, :] * row_of['g1'] + row_of['s1'] + own[rows, :] + rbuf[1, rows, :].astype(F32) + row_of['bdown']
        center = z - row_mean(z)
        inverse = lax.rsqrt(row_mean(center * center) + epsilon)
        normed = center * inverse
        obuf[rows, :] = (normed * row_of['g2'] + row_of['s2']).astype(BF)
        give_back(i, out, out_base, out_sends)
        g = dW[A_BLK, 0, rows, :].astype(F32)
        col_add(0, g * normed)
        col_add(1, g)
        gg = g * row_of['g2']
        back = inverse * (gg - row_mean(gg) - normed * row_mean(gg * normed))
        col_add(2, back)
        mix[rows, :] = back
        return back.astype(BF)

    g2b = over_pieces(norm_two, G2)
    out_entries = given(out, out_base, out_sends)
    pending.extend(out_entries)

    def transpose_half(src, start):
        def run(i, _):
            rows = rows_at(start + i * piece, piece)
            tbuf[:, rows] = src[rows, :].astype(F32).T.astype(BF)
            return 0

        lax.fori_loop(0, half // piece, run, 0)

    def transpose_into(src):
        transpose_half(src, 0)
        transpose_half(src, half)

    def grad_rows(part, chip, kk):
        b, tt, lo, hi = part
        return dW.at[b, tt, rows_at(chip * pair + kk * shard, shard), lo:hi]

    def reduce_one(part):
        b, tt, lo, hi = part
        base = new("r", 4)
        for i, chip in enumerate((cd, cy)):
            send(grad_rows(part, chip, 0), rs1.at[b, tt, 0, i, :, lo:hi], base + i, 2 * cy + k, t)
        for i, chip in enumerate((cd, cx)):
            send(grad_rows(part, chip, 1), rs1.at[b, tt, 1, i, :, lo:hi], base + 2 + i, 2 * cx + k, t)
        return part, base

    def add_rows(part, chip, kk, received):
        b, tt, lo, hi = part
        rows = rows_at(chip * pair + kk * shard, shard)
        dW[b, tt, rows, lo:hi] = (dW[b, tt, rows, lo:hi].astype(F32) + received.astype(F32)).astype(BF)

    def reduce_two(state):
        part, base = state
        b, tt, lo, hi = part
        nxt = new("r", 2)
        for kk, other in ((0, cx), (1, cy)):
            arrive(rs1.at[b, tt, kk, 0, :, lo:hi], base + 2 * kk)
            add_rows(part, other, kk, rs1[b, tt, kk, 0, :, lo:hi])
            send(grad_rows(part, other, kk), rs2.at[b, tt, kk, :, lo:hi], nxt + kk, 2 * other + k, t)
        for kk in range(2):
            arrive(rs1.at[b, tt, kk, 1, :, lo:hi], base + 2 * kk + 1)
            add_rows(part, c, kk, rs1[b, tt, kk, 1, :, lo:hi])
        return part, nxt

    outer = t == (ranks - 1) * (1 - k)
    joiner = t == 1 + (1 - k)
    inward = t + 2 * k - 1
    z_bases = {}

    def reduce_join(state):
        part, nxt = state
        b, tt, lo, hi = part
        base = new("r", 2)
        for kk in range(2):
            arrive(rs2.at[b, tt, kk, :, lo:hi], nxt + kk)
            add_rows(part, c, kk, rs2[b, tt, kk, :, lo:hi])
            send_if(outer, grad_rows(part, c, kk), rs3.at[b, tt, kk, :, lo:hi], base + kk, d,
                    lax.rem(inward + ranks, ranks))
        return part, base

    def reduce_z(state):
        part, base = state
        b, tt, lo, hi = part
        if (b, lo) not in z_bases:
            z_bases[(b, lo)] = new("r", 3)
        z_base = z_bases[(b, lo)]
        for kk in range(2):
            @pl.when(joiner)
            def _(kk=kk):
                arrive(rs3.at[b, tt, kk, :, lo:hi], base + kk)
                add_rows(part, c, kk, rs3[b, tt, kk, :, lo:hi])

            from_slot = lax.rem(t - k + ranks, ranks)
            target = zbuf.at[b, jnp.minimum(from_slot, 2), :, lo:hi]
            cp = remote(grad_rows(part, c, kk), target, new("s"), z_base + jnp.minimum(from_slot, 2),
                        2 * c + kk, 2 * k + tt)
            mine = jnp.logical_and(kk == k, t == 2 * k + tt)

            @pl.when(mine)
            def _(kk=kk):
                pltpu.make_async_copy(grad_rows(part, c, kk), target,
                                      rsem.at[z_base + jnp.minimum(from_slot, 2)]).start()

            away = jnp.logical_and(jnp.logical_not(mine), jnp.logical_not(outer))

            @pl.when(away)
            def _(cp=cp):
                cp.start()

            pending.append((jnp.logical_not(away), cp))

    def reduce_end(b):
        for (blk, lo), base in z_bases.items():
            if blk == b:
                hi = lo + (width if (b, width // 2) not in z_bases else width // 2)
                for q in range(3):
                    arrive(zbuf.at[b, q, :, lo:hi], base + q)
        total = zbuf[b, 0].astype(F32)
        for q in range(1, 3):
            total = total + zbuf[b, q].astype(F32)
        return total

    def grad_matmul(b, tt, right):
        def run(i, _):
            rows = rows_at(i * ROW_BLOCK, ROW_BLOCK)
            dW[b, tt, rows, :] = dot(tbuf[rows, :], right[tt]).astype(BF)
            return 0

        lax.fori_loop(0, width // ROW_BLOCK, run, 0)

    transpose_half(G2, here)
    wait_pieces(G2, g2b)
    transpose_half(G2, there)
    grad_matmul(C_BLK, 0, act)
    rc0 = reduce_one((C_BLK, 0, 0, width))
    grad_matmul(C_BLK, 1, act)
    rc1 = reduce_one((C_BLK, 1, 0, width))

    def back_up(i, _):
        rows = rows_at(i * ROW_BLOCK, ROW_BLOCK)
        for tt in range(2):
            gi = (dot(G2[rows, :], W[C_BLK, tt]) * gp[tt, rows, :].astype(F32)).astype(BF)
            gp[tt, rows, :] = gi
            row = 6 + 2 * k + tt
            vec[pl.ds(row, 1), :] = vec[pl.ds(row, 1), :] + jnp.sum(gi.astype(F32), axis=0, keepdims=True)
        return 0

    lax.fori_loop(0, length // ROW_BLOCK, back_up, 0)
    rh = exchange(lambda rows: dot(gp[0, rows, :], W[B_BLK, 0], 1, 1) + dot(gp[1, rows, :], W[B_BLK, 1], 1, 1), 0)
    transpose_into(H)

    def norm_one_back(rows, i):
        rh(i)
        grad = mix[rows, :] + own[rows, :] + rbuf[0, rows, :].astype(F32)
        normed = n1[rows, :]
        col_add(3, grad * normed)
        col_add(4, grad)
        hh = grad * row_of['g1']
        back = r1[rows, 0:1] * (hh - row_mean(hh) - normed * row_mean(hh * normed))
        col_add(5, back)
        mix[rows, :] = back
        return back.astype(BF)

    g1b = over_pieces(norm_one_back, G1)
    grad_matmul(B_BLK, 0, gp)
    sc0 = reduce_two(rc0)
    rb0 = reduce_one((B_BLK, 0, 0, width))
    grad_matmul(B_BLK, 1, gp)
    sc1 = reduce_two(rc1)
    rb1 = reduce_one((B_BLK, 1, 0, width))

    def back_context(start):
        def run(i, _):
            rows = rows_at(start + i * ROW_BLOCK, ROW_BLOCK)
            for tt in range(2):
                dctx[tt, rows, :] = dot(G1[rows, :], W[A_BLK, tt, :, 512:768]).astype(BF)
            return 0

        lax.fori_loop(0, half // ROW_BLOCK, run, 0)

    back_context(here)
    wait_pieces(G1, g1b)
    back_context(there)
    transpose_into(G1)

    def out_matmul(i, _):
        rows = rows_at(i * ROW_BLOCK, ROW_BLOCK)
        for tt in range(2):
            dW[A_BLK, tt, rows, 512:768] = dot(tbuf[rows, :], ctx[tt]).astype(BF)
        return 0

    lax.fori_loop(0, width // ROW_BLOCK, out_matmul, 0)
    transpose_into(X)

    grads = act

    def attend_back(tt, g, lo=0, hi=length // BACKWARD_BLOCK):
        base = 6 * tt
        heads = HALF_HEADS[0:2] if g == 0 else HALF_HEADS[2:3]
        lanes = slice(128, 256) if g == 0 else slice(0, 128)
        if lo == 0:
            dkv[...] = jnp.zeros_like(dkv)
        ki, vi = heads[0][1], heads[0][2]
        k_t = tiles[base + ki].astype(F32).T
        row = lax.broadcasted_iota(jnp.int32, k_t.shape, 0)
        k_masks = [jnp.where((row < HD) if hd[3] == 0 else (row >= HD), k_t, 0.0).astype(BF) for hd in heads]

        def back(i, _):
            rows = rows_at(i * BACKWARD_BLOCK, BACKWARD_BLOCK)
            dq_t = jnp.zeros((128, BACKWARD_BLOCK), F32)
            do = dctx[tt, rows, lanes]
            prod = do.astype(F32) * ctx[tt, rows, lanes].astype(F32)
            for h, (qi, _, _, qh, vh) in enumerate(heads):
                qt = tiles[base + qi, rows, :]
                qm = jnp.where(lane_mask(qt.shape, qh), qt, jnp.zeros_like(qt))
                qa = jnp.concatenate([qm, raug[3 * tt + 2 * g + h, rows, :]], axis=1)
                pt = jnp.exp(dot(jnp.concatenate([tiles[base + ki], kf[...]], axis=1), qa, 1, 1))
                vmask = lane_mask(do.shape, vh)
                dom = jnp.where(vmask, do, jnp.zeros_like(do))
                delta = jnp.sum(jnp.where(vmask, prod, 0.0), axis=1, keepdims=True)
                doa = jnp.concatenate([dom, pieces(-delta, do.shape).astype(BF)], axis=1)
                dst = (pt * dot(jnp.concatenate([tiles[base + vi], kf[...]], axis=1), doa, 1, 1)).astype(BF)
                dkv[1] += dot(pt.astype(BF), dom)
                dkv[0] += dot(dst, qm)
                dq_t = dq_t + dot(k_masks[h], dst)
            dq = (dq_t.T * 0.125).astype(BF)
            if g == 0:
                grads[tt, rows, 0:128] = dq
            else:
                grads[tt, rows, 384:512] = dq
            return 0

        lax.fori_loop(lo, hi, back, 0)
        if hi < length // BACKWARD_BLOCK:
            return
        if g == 0:
            grads[tt, :, 128:256] = dkv[0].astype(BF)
            grads[tt, :, 256:384] = dkv[1].astype(BF)
        else:
            grads[tt, :, 384:512] = grads[tt, :, 384:512] + pltpu.roll(dkv[0], 64, 1).astype(BF)
            grads[tt, :, 512:640] = pltpu.roll(dkv[1], 64, 1).astype(BF)

    mid = width // 2

    def qkv_matmul(tt, part):
        low = lax.broadcasted_iota(jnp.int32, (ROW_BLOCK, 128), 1) < HD

        def run(i, _):
            rows = rows_at(i * ROW_BLOCK, ROW_BLOCK)
            if part == 0:
                dW[A_BLK, tt, rows, 0:384] = dot(tbuf[rows, :], grads[tt, :, 0:384]).astype(BF)
            else:
                g = dot(tbuf[rows, :], grads[tt, :, 384:640]).astype(BF)
                dW[A_BLK, tt, rows, 384:512] = g[:, 0:128]
                kept = dW[A_BLK, tt, rows, 512:640]
                dW[A_BLK, tt, rows, 512:640] = jnp.where(low, g[:, 128:256], kept)
            return 0

        lax.fori_loop(0, width // ROW_BLOCK, run, 0)
        row = 10 + 2 * k + tt
        lanes = slice(0, 384) if part == 0 else slice(384, 640)
        vec[pl.ds(row, 1), lanes] = jnp.sum(grads[tt, :, lanes].astype(F32), axis=0, keepdims=True)
        return reduce_one((A_BLK, tt, part * mid, part * mid + mid))

    blocks = length // BACKWARD_BLOCK
    attend_back(0, 0)
    ra00 = qkv_matmul(0, 0)
    jc0 = reduce_join(sc0)
    jc1 = reduce_join(sc1)
    reduce_z(jc0)
    sb0 = reduce_two(rb0)
    attend_back(0, 1)
    ra01 = qkv_matmul(0, 1)
    sb1 = reduce_two(rb1)
    reduce_z(jc1)
    attend_back(1, 0, 0, blocks // 2)
    jb0 = reduce_join(sb0)
    sa00 = reduce_two(ra00)
    attend_back(1, 0, blocks // 2, blocks)
    ra10 = qkv_matmul(1, 0)
    sa01 = reduce_two(ra01)
    jb1 = reduce_join(sb1)
    reduce_z(jb0)
    attend_back(1, 1)
    ra11 = qkv_matmul(1, 1)
    ja00 = reduce_join(sa00)
    reduce_z(jb1)

    v_base = new("r", 8)
    send(vec, vrecv.at[0], v_base, 2 * c + 1 - k, t)
    ja01 = reduce_join(sa01)
    sa10 = reduce_two(ra10)
    my_rows = pl.ds(pl.multiple_of(8 * k, 8), 8)
    arrive(vrecv.at[0], v_base)
    chip_total = vrecv.at[1]
    chip_total[...] = vec[...] + vrecv[0]
    vgather[pl.ds(t, 1)] = chip_total[my_rows, :][None]
    for j in range(1, ranks):
        send(chip_total.at[my_rows, :], vgather.at[t], v_base + 1 + t, d, lax.rem(t + j, ranks))
    reduce_z(ja00)
    rx = exchange(lambda rows: dot(grads[0, rows, 0:640], W[A_BLK, 0, :, 0:640], 1, 1)
                  + dot(grads[1, rows, 0:640], W[A_BLK, 1, :, 0:640], 1, 1), 1)
    for s in range(2):
        for h in range(2):
            arrive(out.at[s, pl.ds(h * piece, piece), :], out_base + 2 * s + h)
    for entry in out_entries:
        pending[:] = [e for e in pending if e is not entry]
        settle(entry)
    reduce_z(ja01)
    ja10 = reduce_join(sa10)
    dx_base, dx_sends = new("r", 4), new("s", ranks)

    def finish(i, _):
        rx(i)
        rows = rows_at(i * piece, piece)
        obuf[rows, :] = (mix[rows, :] + own[rows, :] + rbuf[1, rows, :].astype(F32)).astype(BF)
        give_back(i, dxr, dx_base, dx_sends)
        return 0

    lax.fori_loop(0, ranks, finish, 0)
    pending.extend(given(dxr, dx_base, dx_sends))
    sa11 = reduce_two(ra11)
    ja11 = reduce_join(sa11)
    gc_out[...] = reduce_end(C_BLK)
    gb_out[...] = reduce_end(B_BLK)

    for j in range(1, ranks):
        src = lax.rem(t + j, ranks)
        arrive(vgather.at[src], v_base + 1 + src)
    total = vgather[0]
    for j in range(1, ranks):
        total = total + vgather[j]
    vgather[4] = total
    send(vgather.at[4], vgather.at[5], v_base + 5, 2 * cx + k, t)
    reduce_z(ja10)
    arrive(vgather.at[5], v_base + 5)
    total = total + vgather[5]
    vgather[6] = total
    send(vgather.at[6], vgather.at[7], v_base + 6, 2 * cy + k, t)
    reduce_z(ja11)
    arrive(vgather.at[7], v_base + 6)
    final = vrecv.at[2]
    final[my_rows, :] = total + vgather[7]
    send(final.at[my_rows, :], final.at[my_rows, :], v_base + 7, 2 * c + 1 - k, t)
    for s in range(2):
        for h in range(2):
            arrive(dxr.at[s, pl.ds(h * piece, piece), :], dx_base + 2 * s + h)
    ga_out[...] = reduce_end(A_BLK)
    arrive(final.at[pl.ds(pl.multiple_of(8 * (1 - k), 8), 8), :], v_base + 7)
    vec_out[...] = final[...]
    for entry in pending:
        settle(entry)


def fused_layer(tokens, cotangent, parents, segment_ids, w_qkv, w_out, w_up, w_down, vectors):
    local, quarter, width = tokens.shape
    length = segment_ids.shape[1]
    half = length // 2
    shard = w_qkv.shape[1]
    vm = pl.BlockSpec(memory_space=pltpu.VMEM)
    anywhere = pl.BlockSpec(memory_space=pl.ANY)
    rows = list(vectors)
    sems = 224
    return pl.pallas_call(
        layer_kernel,
        name="layer",
        out_shape=(
            jax.ShapeDtypeStruct(tokens.shape, BF),
            jax.ShapeDtypeStruct(tokens.shape, BF),
            jax.ShapeDtypeStruct((shard, width), F32),
            jax.ShapeDtypeStruct((shard, width), F32),
            jax.ShapeDtypeStruct((shard, width), F32),
            jax.ShapeDtypeStruct((16, width), F32),
        ),
        in_specs=[anywhere, anywhere, vm, vm, vm, vm, anywhere, anywhere] + [vm] * len(rows),
        out_specs=(anywhere, anywhere, vm, vm, vm, vm),
        scratch_shapes=[
            pltpu.VMEM((3, 2, width, width), BF),
            pltpu.VMEM((length, width), BF),
            pltpu.VMEM((12, length, 128), BF),
            pltpu.VMEM((2, length, 256), BF),
            pltpu.VMEM((6, length, 128), BF),
            pltpu.VMEM((length, 128), BF),
            pltpu.VMEM((length, 128), BF),
            pltpu.VMEM((half, width), F32),
            pltpu.VMEM((half, 128), F32),
            pltpu.VMEM((length, width), BF),
            pltpu.VMEM((2, length, width), BF),
            pltpu.VMEM((2, length, width), BF),
            pltpu.VMEM((half, width), F32),
            pltpu.VMEM((length, width), BF),
            pltpu.VMEM((length, width), BF),
            pltpu.VMEM((2, length, 256), BF),
            pltpu.VMEM((half, width), F32),
            pltpu.VMEM((2, half, width), BF),
            pltpu.VMEM((2, half, width), BF),
            pltpu.VMEM((half, width), BF),
            pltpu.VMEM((3, 2, width, width), BF),
            pltpu.VMEM((3, 2, 2, 2, shard, width), BF),
            pltpu.VMEM((3, 2, 2, shard, width), BF),
            pltpu.VMEM((3, 2, 2, shard, width), BF),
            pltpu.VMEM((3, 3, shard, width), BF),
            pltpu.VMEM((width, length), BF),
            pltpu.VMEM((2, length, 128), F32),
            pltpu.VMEM((shard, width), BF),
            pltpu.VMEM((2,) + segment_ids.shape, jnp.int32),
            pltpu.VMEM((2,) + parents.shape, jnp.int32),
            pltpu.VMEM((16, width), F32),
            pltpu.VMEM((3, 16, width), F32),
            pltpu.VMEM((8, 8, width), F32),
            pltpu.SemaphoreType.DMA((sems,)),
            pltpu.SemaphoreType.DMA((sems,)),
        ],
        compiler_params=pltpu.CompilerParams(collective_id=0, has_side_effects=True, vmem_limit_bytes=63 << 20),
        cost_estimate=pl.CostEstimate(flops=60 * 10**9, bytes_accessed=30 * 10**6, transcendentals=16 * 10**6),
    )(tokens, cotangent, parents, segment_ids, w_qkv, w_out, w_up, w_down, *rows)


def finish_kernel(out, dx_in, ga_in, gb_in, gc_in, vec_in, o_out, o_dx, o_qkv, o_bq, o_bv, o_wout, o_bout, o_g1, o_s1, o_up, o_bup,
                  o_down, o_bdown, o_g2, o_s2, dx, ga, vec, sem):
    copies = [pltpu.make_async_copy(src, dst, sem.at[i]) for i, (src, dst) in enumerate(
        ((dx_in, dx), (ga_in, ga), (vec_in, vec), (out, o_out), (gb_in, o_up), (gc_in, o_down)))]
    for copy in copies:
        copy.start()
    for copy in copies[:3]:
        copy.wait()
    o_dx[...] = dx[...].astype(F32)
    a = ga[...]
    for i, (pair, lo) in enumerate(((0, 384), (128, 448), (256, 512))):
        o_qkv[i] = jnp.concatenate([a[:, pair : pair + 128], a[:, lo : lo + HD]], axis=1)
    o_wout[...] = jnp.concatenate([a[:, 640:768], a[:, 576:640]], axis=1).T
    for ref, row in ((o_g2, 0), (o_s2, 1), (o_bdown, 2), (o_g1, 3), (o_s1, 4), (o_bout, 5)):
        ref[...] = vec[row, :]
    width = vec.shape[1]
    for i in range(4):
        o_bup[i * width : (i + 1) * width] = vec[6 + i, :]
    for ref, pair, lo in ((o_bq, 0, 384), (o_bv, 256, 512)):
        row = [vec[10 + i : 11 + i, :] for i in range(4)]
        parts = [p for r in row for p in (r[:, pair : pair + 128], r[:, lo : lo + HD])]
        ref[...] = jnp.concatenate(parts, axis=1)[0]
    for copy in copies[3:]:
        copy.wait()


def plane_body(tokens, parents, segment_ids, w_qkv, b_q, b_v, w_out, b_out, gain_one, shift_one,
               w_up, b_up, w_down, b_down, gain_two, shift_two, cotangent):
    raw = fused_layer(
        tokens, cotangent, parents, segment_ids, w_qkv.transpose(1, 0, 2), w_out, w_up, w_down.T,
        (b_q, b_v, b_out, gain_one, shift_one, b_up, b_down, gain_two, shift_two))
    vm = pl.BlockSpec(memory_space=pltpu.VMEM)
    anywhere = pl.BlockSpec(memory_space=pl.ANY)
    shard, kinds, part = w_qkv.shape
    vector = jax.ShapeDtypeStruct(b_q.shape, F32)
    outs = pl.pallas_call(
        finish_kernel,
        name="finish",
        out_shape=(
            jax.ShapeDtypeStruct(tokens.shape, BF),
            jax.ShapeDtypeStruct(tokens.shape, F32),
            jax.ShapeDtypeStruct((kinds, shard, part), F32),
            vector, vector,
            jax.ShapeDtypeStruct(w_out.shape, F32),
            vector, vector, vector,
            jax.ShapeDtypeStruct(w_up.shape, F32),
            jax.ShapeDtypeStruct(b_up.shape, F32),
            jax.ShapeDtypeStruct(w_down.shape[::-1], F32),
            vector, vector, vector,
        ),
        in_specs=[anywhere] * 6,
        out_specs=(vm,) * 15,
        scratch_shapes=[pltpu.VMEM(tokens.shape, BF), pltpu.VMEM((shard, 4 * part), F32), pltpu.VMEM((16, 4 * part), F32),
                        pltpu.SemaphoreType.DMA((6,))],
        compiler_params=pltpu.CompilerParams(vmem_limit_bytes=63 << 20),
    )(*raw)
    return (outs[0], outs[1], outs[2].transpose(1, 0, 2), *outs[3:11], outs[11].T, *outs[12:])


def solution(mesh):
    dp, ranks = mesh.shape["dp"], mesh.shape["tensor"]
    return jax.shard_map(
        plane_body if (dp, ranks) == (8, 4) else functools.partial(body, dp, ranks),
        mesh=mesh,
        in_specs=(P("dp", "tensor", None), P("dp", None), P("dp", None), P("dp", None, "tensor"), P(), P(),
                  P("tensor", "dp"), P(), P(), P(), P("dp", "tensor"), P(), P("tensor", "dp"), P(), P(), P(),
                  P("dp", "tensor", None)),
        out_specs=(P("dp", "tensor", None), P("dp", "tensor", None), P("dp", None, "tensor"), P(), P(),
                   P("tensor", "dp"), P(), P(), P(), P("dp", "tensor"), P(), P("tensor", "dp"), P(), P(), P()),
        check_vma=False,
    )
```
